32 devices in a mesh: dp: 16 (over z, y, core), tensor: 2 (over x).
Axes of the slice: x: 2, y: 2, z: 4, core: 2. Of those that a mesh axis runs over, the one named last changes fastest.
Arguments:
- tokens: bfloat16 [81920, 1024], P(('dp', 'tensor')), may hold values from -6 to 6
- kept: int32 [256], P('dp'), may hold values from 180 to 256
- cotangent: bfloat16 [81920, 1024], P(('dp', 'tensor')), may hold values from -6 to 6
- w_qkv: bfloat16 [3, 1024, 1024], P(None, 'dp', 'tensor'), may hold values from -0.1875 to 0.1875
- w_out: bfloat16 [1024, 1024], P('tensor', 'dp'), may hold values from -0.75 to 0.75
- w_up: bfloat16 [1024, 4096], P('dp', 'tensor'), may hold values from -0.1875 to 0.1875
- w_down: bfloat16 [4096, 1024], P('tensor', 'dp'), may hold values from -0.09375 to 0.09375
- qv_bias: bfloat16 [2, 1024], P(None, ('tensor', 'dp')), may hold values from -3 to 3
- up_bias: bfloat16 [4096], P(('tensor', 'dp')), may hold values from -3 to 3
- ln_gain: float32 [2, 1024], P(None, ('dp', 'tensor')), may hold values from 0.5 to 1.5
- shift: float32 [4, 1024], P(None, ('dp', 'tensor')), may hold values from -3 to 3
Outputs:
- layer_out: bfloat16 [81920, 1024], P(('dp', 'tensor'))
- grad_tokens: float32 [81920, 1024], P(('dp', 'tensor'))
- grad_qkv: float32 [3, 1024, 1024], P(None, 'dp', 'tensor')
- grad_out: float32 [1024, 1024], P('tensor', 'dp')
- grad_up: float32 [1024, 4096], P('dp', 'tensor')
- grad_down: float32 [4096, 1024], P('tensor', 'dp')
- grad_qv_bias: float32 [2, 1024], P(None, ('tensor', 'dp'))
- grad_up_bias: float32 [4096], P(('tensor', 'dp'))
- grad_gain: float32 [2, 1024], P(None, ('dp', 'tensor'))
- grad_shift: float32 [4, 1024], P(None, ('dp', 'tensor'))
The draws below stay inside these ranges and needn't reach their ends.
Inputs may be any that keep to these rules, and one draw needn't show every extreme that they name: kept patches of each image; an image's first 64 tokens and its first kept patch tokens are valid, the rest of its 320 tokens are padding.
All inputs are finite; a program needn't handle non-finite values.
Results may differ from the reference program's by a relative error of at most 0.02.
Values may be sent and summed in bfloat16 or wider, within the bound.
No kernel may reach another device: no remote copies, remote signals or barrier semaphores. Data moves between devices by JAX's collectives and lax.ppermute only.
A program may use at most 320 MiB of HBM per device.

```python
import jax
import jax.numpy as jnp
from jax import lax

D = 1024
HEADS = 16
HEAD_DIM = 64
FF = 4096
BUFFER = 64
PATCHES = 256
SEQ = 320
IMAGES = 256
TOKENS = 81920


def place_ends(drawn, rng, low, high):
    extent = drawn.shape
    place = [jax.random.randint(jax.random.fold_in(rng, axis), (), 0, extent[axis]) for axis in range(len(extent))]
    drawn = drawn.at[tuple(place)].set(low)
    longest = extent.index(max(extent))
    place[longest] = (place[longest] + 1) % extent[longest]
    return drawn.at[tuple(place)].set(high)


def strengthened(entries, key, source, target, shards_of, factor):
    owner, partner = [(jnp.arange(entries.shape[axis_at]) // (entries.shape[axis_at] // shards_of)).reshape([-1 if axis == axis_at else 1 for axis in range(entries.ndim)]) for axis_at in (source, target)]
    chosen = jax.random.permutation(key, shards_of)[partner]
    strong = (owner == chosen) | (owner == (partner + shards_of // 2) % shards_of)
    return jnp.where(strong, factor * entries, entries)


def block_levels(key, dims, shards, smallest, high):
    factor_of = 1.0
    for dim, blocks in shards:
        steps = jax.random.uniform(jax.random.fold_in(jax.random.fold_in(key, 6), dim), (blocks,), jnp.float32, smallest / len(shards), high / len(shards))
        factor_of = factor_of * jnp.repeat(jnp.exp(steps), dims[dim] // blocks).reshape((-1,) + (1,) * (len(dims) - 1 - dim))
    return factor_of


def normal_values(own_key, extent, width, reach, pieces=(), kind=jnp.bfloat16):
    level = block_levels(own_key, extent, pieces, -0.22, 0.18) if pieces else 1.0
    values = jax.random.normal(own_key, extent, jnp.float32) * width * level
    return jnp.minimum(jnp.maximum(values, -reach), reach).astype(kind)


def heavy_noise(rng, dims, scale, most, shards, heavy, held_as=jnp.bfloat16):
    values = scale * jax.random.normal(rng, dims, jnp.float32)
    if shards:
        values = values * block_levels(rng, dims, shards, -0.22, 0.18)
    return jnp.clip(strengthened(values, jax.random.fold_in(rng, 3), *heavy), -most, most).astype(held_as)


def setup_inputs(seed: int = 0) -> dict:
    key_of = jax.random.split(jax.random.key(seed), 12)
    return {
        "tokens": heavy_noise(key_of[0], (TOKENS, D), 1.0, 6.0, ((0, 32),), (0, 1, 32, 2.75)),
        "kept": place_ends(jax.random.randint(key_of[1], (IMAGES,), (7 * PATCHES + 9) // 10, PATCHES + 1), jax.random.fold_in(key_of[1], 1), (7 * PATCHES + 9) // 10, PATCHES).astype(jnp.int32),
        "cotangent": heavy_noise(key_of[2], (TOKENS, D), 1.0, 6.0, ((0, 32),), (0, 1, 32, 2.75)),
        "w_qkv": normal_values(key_of[3], (3, D, D), D ** -0.5, 0.1875, ((1, 16), (2, 2))),
        "w_out": normal_values(key_of[4], (D, D), (D // 16) ** -0.5, 0.75, ((0, 2), (1, 16))),
        "w_up": normal_values(key_of[5], (D, FF), D ** -0.5, 0.1875, ((0, 16), (1, 2))),
        "w_down": normal_values(key_of[6], (FF, D), FF ** -0.5, 0.09375, ((0, 2), (1, 16))),
        "qv_bias": normal_values(key_of[7], (2, D), 0.5, 3.0, ((1, 32),)),
        "up_bias": normal_values(key_of[8], (FF,), 0.5, 3.0, ((0, 32),)),
        "ln_gain": jnp.clip(1.0 + 0.1 * jax.random.normal(key_of[9], (2, D), jnp.float32), 0.5, 1.5),
        "shift": normal_values(key_of[10], (4, D), 0.5, 3.0, ((1, 32),), jnp.float32),
    }


@jax.custom_vjp
def low(v):
    return lax.optimization_barrier(v.astype(jnp.bfloat16)).astype(jnp.float32)

@jax.custom_vjp
def low_back(v):
    return v

def low_keep(v):
    return (low(v), None)

def low_pass(kept, grad):
    return (grad,)

def back_keep(v):
    return (v, None)

def back_low(kept, grad):
    return (low(grad),)
low.defvjp(low_keep, low_pass)
low_back.defvjp(back_keep, back_low)

def layer_norm(values, gain, bias):
    centred = values - lax.optimization_barrier(jnp.mean(values, axis=-1, keepdims=True))
    variance = lax.optimization_barrier(jnp.mean(centred * centred, axis=-1, keepdims=True))
    return centred * lax.rsqrt(variance + 1e-06) * gain + bias

def forward(x, w_qkv, w_out, w_up, w_down, qv_bias, up_bias, ln_gain, shift, valid):
    top = lax.Precision.HIGHEST
    count = x.shape[0] // SEQ
    h1 = low(layer_norm(x, ln_gain[0], shift[0]))
    query = low(low_back(jnp.dot(h1, w_qkv[0], precision=top) + qv_bias[0]))
    key = low(low_back(jnp.dot(h1, w_qkv[1], precision=top)))
    value = low(low_back(jnp.dot(h1, w_qkv[2], precision=top) + qv_bias[1]))
    shape = (count, SEQ, HEADS, HEAD_DIM)
    scores = jnp.einsum('bqhe,bkhe->bhqk', query.reshape(shape), key.reshape(shape), precision=top) * HEAD_DIM ** (-0.5)
    keymask = valid.reshape(count, 1, 1, SEQ) > 0.5
    scores = low_back(jnp.where(keymask, scores, -1000000000.0))
    probs = low(jax.nn.softmax(scores, axis=-1))
    attn = jnp.einsum('bhqk,bkhe->bqhe', probs, value.reshape(shape), precision=top).reshape(count * SEQ, D)
    attn = low(low_back(attn))
    mixed = x + low_back(jnp.dot(attn, w_out, precision=top)) + shift[2]
    h2 = low(layer_norm(mixed, ln_gain[1], shift[1]))
    pre = low_back(jnp.dot(h2, w_up, precision=top) + up_bias)
    act = low(jax.nn.gelu(pre, approximate=True))
    result = mixed + low_back(jnp.dot(act, w_down, precision=top)) + shift[3]
    return result * valid[:, None]

def reference(tokens, kept, cotangent, w_qkv, w_out, w_up, w_down, qv_bias, up_bias, ln_gain, shift):
    params = tuple((p.astype(jnp.float32) for p in (w_qkv, w_out, w_up, w_down, qv_bias, up_bias, ln_gain, shift)))
    block = 8
    blocks = IMAGES // block
    positions = jnp.arange(SEQ, dtype=jnp.int32)
    valid_all = (positions[None, :] < BUFFER + kept[:, None]).astype(jnp.float32).reshape(blocks, block * SEQ)
    x_all = tokens.astype(jnp.float32).reshape(blocks, block * SEQ, D)
    dy_all = cotangent.astype(jnp.float32).reshape(blocks, block * SEQ, D)

    def one(total, item):
        x, dy, valid = item

        def local(xx, a, b, c, d, e, f, g, h):
            return forward(xx, a, b, c, d, e, f, g, h, valid)
        result, pull = jax.vjp(local, x, *params)
        grads = pull(dy)
        total = tuple((s + t for s, t in zip(total, grads[1:])))
        return (total, (result.astype(jnp.bfloat16), grads[0]))
    zeros = tuple((jnp.zeros_like(p) for p in params))
    total, (results, grads_x) = lax.scan(one, zeros, (x_all, dy_all, valid_all))
    return (results.reshape(TOKENS, D), grads_x.reshape(TOKENS, D), total[0], total[1], total[2], total[3], total[4], total[5], total[6], total[7])
```

```python
import functools

import jax
import jax.numpy as jnp
from jax import lax
from jax.experimental import pallas as pl
from jax.experimental.pallas import tpu as pltpu
from jax.sharding import PartitionSpec as P

HEAD_DIM = 64
BUFFER = 64
SEQ = 320
KEYS = 384
LANES = 128
EPSILON = 1e-06
SCALE = HEAD_DIM ** (-0.5)
LOG2E = 1.4426950408889634
NEGATIVE = -1000000000.0 / SCALE
VMEM = 56 << 20

f32 = jnp.float32
bf16 = jnp.bfloat16


def dot(left, right):
    return lax.dot_general(left, right, (((1,), (0,)), ((), ())), preferred_element_type=f32)


def dot_flip(left, right):
    return lax.dot_general(left, right, (((1,), (1,)), ((), ())), preferred_element_type=f32)


def split_heads(values):
    low = lax.broadcasted_iota(jnp.int32, (1, LANES), 1) < HEAD_DIM
    zero = jnp.zeros_like(values)
    return jnp.where(low, values, zero), jnp.where(low, zero, values)


def pad_keys(values):
    return jnp.concatenate([values, jnp.zeros((KEYS - SEQ, values.shape[1]), values.dtype)], 0)


def attend_kernel(kept_ref, q_ref, k_ref, v_ref, o_ref, e_ref, r_ref, *, pairs):
    valid = BUFFER + kept_ref[pl.program_id(1)]
    alive = lax.broadcasted_iota(jnp.int32, (1, KEYS), 1) < valid
    ones = split_heads(jnp.ones((KEYS, LANES), bf16))
    for pair in range(pairs):
        cols = slice(LANES * pair, LANES * (pair + 1))
        keys = pad_keys(k_ref[0, :, cols])
        values = split_heads(pad_keys(v_ref[0, :, cols]))
        expos = []
        for head, query in enumerate(split_heads(q_ref[0, :, cols])):
            scores = jnp.where(alive, dot_flip(query, keys), NEGATIVE)
            highest = jnp.max(scores, axis=-1, keepdims=True)
            expo = jnp.exp2((scores - highest) * (SCALE * LOG2E)).astype(bf16)
            e_ref[0, 0, pair, head] = expo
            expos.append(expo)
        right = jnp.concatenate(
            [jnp.concatenate([value, one], 1) for value, one in zip(values, ones)], 0
        )
        both = dot(jnp.concatenate(expos, 1), right)
        inverse = 1.0 / both[:, LANES:]
        o_ref[0, :, cols] = (both[:, :LANES] * inverse).astype(bf16)
        r_ref[0, :, cols] = inverse


def attend(qkv, kept):
    shards, rows, width = qkv.shape
    cols = width // 3
    pairs = cols // LANES
    images = rows // SEQ
    part = lambda which: pl.BlockSpec((1, SEQ, cols), lambda t, i, k: (t, i, which))
    probs = pl.BlockSpec((1, 1, pairs, 2, SEQ, KEYS), lambda t, i, k: (t, i, 0, 0, 0, 0))
    return pl.pallas_call(
        functools.partial(attend_kernel, pairs=pairs),
        grid_spec=pltpu.PrefetchScalarGridSpec(
            num_scalar_prefetch=1,
            grid=(shards, images),
            in_specs=[part(0), part(1), part(2)],
            out_specs=[part(0), probs, part(0)],
        ),
        out_shape=[
            jax.ShapeDtypeStruct((shards, rows, cols), bf16),
            jax.ShapeDtypeStruct((shards, images, pairs, 2, SEQ, KEYS), bf16),
            jax.ShapeDtypeStruct((shards, rows, cols), f32),
        ],
        name="attend",
        compiler_params=pltpu.CompilerParams(
            dimension_semantics=("arbitrary", "arbitrary"), vmem_limit_bytes=VMEM
        ),
    )(kept, qkv, qkv, qkv)


def attend_back_kernel(q_ref, k_ref, v_ref, g_ref, o_ref, e_ref, r_ref, out_ref, bias_ref, *, pairs):
    width = pairs * LANES

    @pl.when(pl.program_id(1) == 0)
    def _():
        bias_ref[...] = jnp.zeros_like(bias_ref)

    for pair in range(pairs):
        cols = slice(LANES * pair, LANES * (pair + 1))
        query = q_ref[0, :, cols]
        values = pad_keys(v_ref[0, :, cols])
        grad = (g_ref[0, :, cols].astype(f32) * r_ref[0, :, cols]).astype(bf16)
        product = split_heads(grad.astype(f32) * o_ref[0, :, cols].astype(f32))
        grads = []
        for head, grad_head in enumerate(split_heads(grad)):
            inner = jnp.sum(product[head], axis=-1, keepdims=True)
            expo = e_ref[0, 0, pair, head].astype(f32)
            grads.append((expo * (dot_flip(grad_head, values) - inner)).astype(bf16))
        keys = jnp.concatenate(split_heads(pad_keys(k_ref[0, :, cols])), 0)
        grad_query = (dot(jnp.concatenate(grads, 1), keys) * SCALE).astype(bf16)
        query_flip, grad_flip = query.T, grad.T
        halves = [slice(HEAD_DIM * head, HEAD_DIM * (head + 1)) for head in range(2)]
        grad_key = jnp.concatenate([dot(query_flip[half], grads[h]) for h, half in enumerate(halves)], 0)
        grad_value = jnp.concatenate(
            [dot(grad_flip[half], e_ref[0, 0, pair, h]) for h, half in enumerate(halves)], 0
        )
        grad_key = (grad_key.T[:SEQ] * SCALE).astype(bf16)
        grad_value = grad_value.T[:SEQ].astype(bf16)
        for which, value in enumerate((grad_query, grad_key, grad_value)):
            start = which * width + LANES * pair
            out_ref[0, :, start : start + LANES] = value
        bias_ref[0, 0:1, cols] += jnp.sum(grad_query.astype(f32), axis=0, keepdims=True)
        bias_ref[0, 1:2, cols] += jnp.sum(grad_value.astype(f32), axis=0, keepdims=True)


def attend_back(qkv, grad, attn, expo, inverse):
    shards, rows, width = qkv.shape
    cols = width // 3
    pairs = cols // LANES
    images = rows // SEQ
    part = lambda which: pl.BlockSpec((1, SEQ, cols), lambda t, i: (t, i, which))
    probs = pl.BlockSpec((1, 1, pairs, 2, SEQ, KEYS), lambda t, i: (t, i, 0, 0, 0, 0))
    return pl.pallas_call(
        functools.partial(attend_back_kernel, pairs=pairs),
        grid=(shards, images),
        in_specs=[part(0), part(1), part(2), part(0), part(0), probs, part(0)],
        out_specs=[
            pl.BlockSpec((1, SEQ, width), lambda t, i: (t, i, 0)),
            pl.BlockSpec((1, 2, cols), lambda t, i: (t, 0, 0)),
        ],
        out_shape=[
            jax.ShapeDtypeStruct((shards, rows, width), bf16),
            jax.ShapeDtypeStruct((shards, 2, cols), f32),
        ],
        name="attend_back",
        compiler_params=pltpu.CompilerParams(
            dimension_semantics=("arbitrary", "arbitrary"), vmem_limit_bytes=VMEM
        ),
    )(qkv, qkv, qkv, grad, attn, expo, inverse)


def norm_parts(values):
    centred = values - jnp.mean(values, axis=-1, keepdims=True)
    inverse = lax.rsqrt(jnp.mean(centred * centred, axis=-1, keepdims=True) + EPSILON)
    return centred * inverse, inverse


def norm_back(grad_normed, normed, inverse):
    first = jnp.mean(grad_normed, axis=-1, keepdims=True)
    second = jnp.mean(grad_normed * normed, axis=-1, keepdims=True)
    return inverse * (grad_normed - first - normed * second)


def gelu_tanh(values):
    return jax.nn.gelu(values, approximate=True)


def columns(left, right):
    return jnp.einsum("rd,tdc->trc", left, right, preferred_element_type=f32)


def contract(left, right):
    return jnp.einsum("trc,tdc->rd", left, right, preferred_element_type=f32)


def weight_grad(left, right):
    return jnp.einsum("rd,trc->tdc", left, right, preferred_element_type=f32).astype(bf16)


def gather(part):
    full = lax.all_gather(part, ("tensor", "dp"), axis=0, tiled=True)
    return full.reshape(lax.axis_size("tensor"), -1, part.shape[1])


def scatter(full):
    flat = full.reshape(-1, full.shape[2])
    return lax.psum_scatter(flat, ("tensor", "dp"), scatter_dimension=0, tiled=True)


def body(tokens, kept, cotangent, w_qkv, w_out, w_up, w_down, qv_bias, up_bias, ln_gain, shift):
    rows, width = tokens.shape
    dp, shards = lax.axis_size("dp"), lax.axis_size("tensor")
    images = rows // SEQ
    part = w_qkv.shape[1]
    cols = w_qkv.shape[2]

    small = jnp.concatenate(
        [ln_gain, shift, qv_bias.astype(f32), up_bias.astype(f32).reshape(-1, ln_gain.shape[1])], 0
    )
    small = lax.all_gather(small, ("dp", "tensor"), axis=0, tiled=False)
    small = small.reshape((dp, shards) + small.shape[1:])
    straight = small[:, :, :6].transpose(2, 0, 1, 3).reshape(6, width)
    gain, shifts = straight[:2], straight[2:]
    bias_qv = small[:, :, 6:8].transpose(1, 2, 0, 3).reshape(shards, 2, cols)
    bias_up = small[:, :, 8:].transpose(1, 0, 2, 3).reshape(shards, -1)

    full_qkv = gather(w_qkv.transpose(1, 0, 2).reshape(part, 3 * cols))
    full_out = gather(w_out.T)
    full_up = gather(w_up)
    full_down = gather(w_down.T)

    first_image = lax.axis_index("tensor") * images
    kept_own = lax.dynamic_slice_in_dim(kept, first_image, images, 0)
    positions = jnp.arange(SEQ, dtype=jnp.int32)
    keep = (positions[None, :] < BUFFER + kept_own[:, None]).astype(f32).reshape(rows, 1)

    x_values = tokens.astype(f32)
    normed1, inverse1 = norm_parts(x_values)
    h1 = (normed1 * gain[0] + shifts[0]).astype(bf16)
    bias_rows = jnp.concatenate([bias_qv[:, 0], jnp.zeros_like(bias_qv[:, 0]), bias_qv[:, 1]], 1)
    qkv = (columns(h1, full_qkv) + bias_rows[:, None, :]).astype(bf16)
    attn, expo, inverse_sum = attend(qkv, kept_own)
    mixed = x_values + contract(attn, full_out) + shifts[2]
    normed2, inverse2 = norm_parts(mixed)
    h2 = (normed2 * gain[1] + shifts[1]).astype(bf16)
    pre = columns(h2, full_up) + bias_up[:, None, :]
    activated, gelu_pull = jax.vjp(gelu_tanh, pre)
    slope = gelu_pull(jnp.ones_like(pre))[0].astype(bf16)
    activated = activated.astype(bf16)

    grad = cotangent.astype(f32) * keep
    grad_m = grad.astype(bf16)
    grad_down = weight_grad(grad_m, activated)
    sent_down = scatter(grad_down)
    grad_pre = (columns(grad_m, full_down) * slope.astype(f32)).astype(bf16)
    grad_bias_up = jnp.sum(grad_pre, axis=1, dtype=f32)
    grad_up = weight_grad(h2, grad_pre)
    sent_up = scatter(grad_up)
    grad_h2 = contract(grad_pre, full_up)
    grad_mixed = grad + norm_back(grad_h2 * gain[1], normed2, inverse2)
    grad_o = grad_mixed.astype(bf16)
    grad_out = weight_grad(grad_o, attn)
    sent_out = scatter(grad_out)
    grad_attn = columns(grad_o, full_out).astype(bf16)
    grad_heads, grad_bias_qv = attend_back(qkv, grad_attn, attn, expo, inverse_sum)
    grad_qkv = weight_grad(h1, grad_heads)
    sent_qkv = scatter(grad_qkv)
    grad_h1 = contract(grad_heads, full_qkv)
    grad_tokens = grad_mixed + norm_back(grad_h1 * gain[0], normed1, inverse1)

    result = (mixed + contract(activated, full_down) + shifts[3]) * keep
    layer_out = result.astype(bf16)

    grad_rows = jnp.stack(
        [
            jnp.sum(grad_h1 * normed1, axis=0),
            jnp.sum(grad_h2 * normed2, axis=0),
            jnp.sum(grad_h1, axis=0),
            jnp.sum(grad_h2, axis=0),
            jnp.sum(grad_mixed, axis=0),
            jnp.sum(grad, axis=0),
        ]
    )
    own = ln_gain.shape[1]
    packed = jnp.concatenate(
        [
            grad_rows.reshape(6, dp, shards, own).transpose(1, 2, 0, 3),
            grad_bias_qv.reshape(shards, 2, dp, own).transpose(2, 0, 1, 3),
            grad_bias_up.reshape(shards, dp, -1, own).transpose(1, 0, 2, 3),
        ],
        2,
    )
    packed = packed.reshape((dp * shards,) + packed.shape[2:])
    sent_small = lax.psum_scatter(packed, ("dp", "tensor"), scatter_dimension=0, tiled=False)

    return (
        layer_out,
        grad_tokens,
        sent_qkv.astype(f32).reshape(part, 3, cols).transpose(1, 0, 2),
        sent_out.astype(f32).T,
        sent_up.astype(f32),
        sent_down.astype(f32).T,
        sent_small[6:8],
        sent_small[8:].reshape(-1),
        sent_small[:2],
        sent_small[2:6],
    )


def solution(mesh):
    both = P(("dp", "tensor"), None)
    matrices = (
        P(None, "dp", "tensor"),
        P("tensor", "dp"),
        P("dp", "tensor"),
        P("tensor", "dp"),
        P(None, ("tensor", "dp")),
        P(("tensor", "dp")),
        P(None, ("dp", "tensor")),
        P(None, ("dp", "tensor")),
    )
    return jax.shard_map(
        body,
        mesh=mesh,
        in_specs=(both, P("dp"), both) + matrices,
        out_specs=(both, both) + matrices,
        check_vma=False,
    )
```

```python
import functools

import jax
import jax.numpy as jnp
from jax import lax
from jax.experimental import pallas as pl
from jax.experimental.pallas import tpu as pltpu
from jax.sharding import PartitionSpec as P

HEAD_DIM = 64
BUFFER = 64
SEQ = 320
KEYS = 384
LANES = 128
EPSILON = 1e-06
SCALE = HEAD_DIM ** (-0.5)
LOG2E = 1.4426950408889634
NEGATIVE = -1000000000.0 / SCALE
VMEM = 56 << 20

f32 = jnp.float32
bf16 = jnp.bfloat16


def dot(left, right):
    return lax.dot_general(left, right, (((1,), (0,)), ((), ())), preferred_element_type=f32)


def dot_flip(left, right):
    return lax.dot_general(left, right, (((1,), (1,)), ((), ())), preferred_element_type=f32)


def split_heads(values):
    low = lax.broadcasted_iota(jnp.int32, (1, LANES), 1) < HEAD_DIM
    zero = jnp.zeros_like(values)
    return jnp.where(low, values, zero), jnp.where(low, zero, values)


def pad_keys(values):
    return jnp.concatenate([values, jnp.zeros((KEYS - SEQ, values.shape[1]), values.dtype)], 0)


def attend_kernel(kept_ref, q_ref, k_ref, v_ref, o_ref, e_ref, r_ref, *, pairs):
    valid = BUFFER + kept_ref[pl.program_id(1)]
    alive = lax.broadcasted_iota(jnp.int32, (1, KEYS), 1) < valid
    ones = split_heads(jnp.ones((KEYS, LANES), bf16))
    for pair in range(pairs):
        cols = slice(LANES * pair, LANES * (pair + 1))
        keys = pad_keys(k_ref[0, :, cols])
        values = split_heads(pad_keys(v_ref[0, :, cols]))
        expos = []
        for head, query in enumerate(split_heads(q_ref[0, :, cols])):
            scores = jnp.where(alive, dot_flip(query, keys), NEGATIVE)
            highest = jnp.max(scores, axis=-1, keepdims=True)
            expo = jnp.exp2((scores - highest) * (SCALE * LOG2E)).astype(bf16)
            e_ref[0, 0, pair, head] = expo
            expos.append(expo)
        right = jnp.concatenate(
            [jnp.concatenate([value, one], 1) for value, one in zip(values, ones)], 0
        )
        both = dot(jnp.concatenate(expos, 1), right)
        inverse = 1.0 / both[:, LANES:]
        o_ref[0, :, cols] = (both[:, :LANES] * inverse).astype(bf16)
        r_ref[0, :, cols] = inverse


def attend(qkv, kept):
    shards, rows, width = qkv.shape
    cols = width // 3
    pairs = cols // LANES
    images = rows // SEQ
    part = lambda which: pl.BlockSpec((1, SEQ, cols), lambda t, i, k: (t, i, which))
    probs = pl.BlockSpec((1, 1, pairs, 2, SEQ, KEYS), lambda t, i, k: (t, i, 0, 0, 0, 0))
    return pl.pallas_call(
        functools.partial(attend_kernel, pairs=pairs),
        grid_spec=pltpu.PrefetchScalarGridSpec(
            num_scalar_prefetch=1,
            grid=(shards, images),
            in_specs=[part(0), part(1), part(2)],
            out_specs=[part(0), probs, part(0)],
        ),
        out_shape=[
            jax.ShapeDtypeStruct((shards, rows, cols), bf16),
            jax.ShapeDtypeStruct((shards, images, pairs, 2, SEQ, KEYS), bf16),
            jax.ShapeDtypeStruct((shards, rows, cols), f32),
        ],
        name="attend",
        cost_estimate=cost(rows * cols * shards * SEQ * 16, qkv, qkv),
        compiler_params=pltpu.CompilerParams(
            dimension_semantics=("arbitrary", "arbitrary"), vmem_limit_bytes=VMEM
        ),
    )(kept, qkv, qkv, qkv)


def attend_back_kernel(q_ref, k_ref, v_ref, g_ref, o_ref, e_ref, r_ref, out_ref, bias_ref, *, pairs):
    width = pairs * LANES

    @pl.when(pl.program_id(1) == 0)
    def _():
        bias_ref[...] = jnp.zeros_like(bias_ref)

    for pair in range(pairs):
        cols = slice(LANES * pair, LANES * (pair + 1))
        query = q_ref[0, :, cols]
        values = pad_keys(v_ref[0, :, cols])
        grad = (g_ref[0, :, cols].astype(f32) * r_ref[0, :, cols]).astype(bf16)
        product = split_heads(grad.astype(f32) * o_ref[0, :, cols].astype(f32))
        grads = []
        for head, grad_head in enumerate(split_heads(grad)):
            inner = jnp.sum(product[head], axis=-1, keepdims=True)
            expo = e_ref[0, 0, pair, head].astype(f32)
            grads.append((expo * (dot_flip(grad_head, values) - inner)).astype(bf16))
        keys = jnp.concatenate(split_heads(pad_keys(k_ref[0, :, cols])), 0)
        grad_query = (dot(jnp.concatenate(grads, 1), keys) * SCALE).astype(bf16)
        query_flip, grad_flip = query.T, grad.T
        halves = [slice(HEAD_DIM * head, HEAD_DIM * (head + 1)) for head in range(2)]
        grad_key = jnp.concatenate([dot(query_flip[half], grads[h]) for h, half in enumerate(halves)], 0)
        grad_value = jnp.concatenate(
            [dot(grad_flip[half], e_ref[0, 0, pair, h]) for h, half in enumerate(halves)], 0
        )
        grad_key = (grad_key.T[:SEQ] * SCALE).astype(bf16)
        grad_value = grad_value.T[:SEQ].astype(bf16)
        for which, value in enumerate((grad_query, grad_key, grad_value)):
            start = which * width + LANES * pair
            out_ref[0, :, start : start + LANES] = value
        bias_ref[0, 0:1, cols] += jnp.sum(grad_query.astype(f32), axis=0, keepdims=True)
        bias_ref[0, 1:2, cols] += jnp.sum(grad_value.astype(f32), axis=0, keepdims=True)


def attend_back(qkv, grad, attn, expo, inverse):
    shards, rows, width = qkv.shape
    cols = width // 3
    pairs = cols // LANES
    images = rows // SEQ
    part = lambda which: pl.BlockSpec((1, SEQ, cols), lambda t, i: (t, i, which))
    probs = pl.BlockSpec((1, 1, pairs, 2, SEQ, KEYS), lambda t, i: (t, i, 0, 0, 0, 0))
    return pl.pallas_call(
        functools.partial(attend_back_kernel, pairs=pairs),
        grid=(shards, images),
        in_specs=[part(0), part(1), part(2), part(0), part(0), probs, part(0)],
        out_specs=[
            pl.BlockSpec((1, SEQ, width), lambda t, i: (t, i, 0)),
            pl.BlockSpec((1, 2, cols), lambda t, i: (t, 0, 0)),
        ],
        out_shape=[
            jax.ShapeDtypeStruct((shards, rows, width), bf16),
            jax.ShapeDtypeStruct((shards, 2, cols), f32),
        ],
        name="attend_back",
        cost_estimate=cost(rows * cols * shards * SEQ * 24, qkv, qkv, expo),
        compiler_params=pltpu.CompilerParams(
            dimension_semantics=("arbitrary", "arbitrary"), vmem_limit_bytes=VMEM
        ),
    )(qkv, qkv, qkv, grad, attn, expo, inverse)


def norm_parts(values):
    centred = values - jnp.mean(values, axis=-1, keepdims=True)
    inverse = lax.rsqrt(jnp.mean(centred * centred, axis=-1, keepdims=True) + EPSILON)
    return centred * inverse, inverse


def norm_back(grad_normed, normed, inverse):
    first = jnp.mean(grad_normed, axis=-1, keepdims=True)
    second = jnp.mean(grad_normed * normed, axis=-1, keepdims=True)
    return inverse * (grad_normed - first - normed * second)


def block_rows(rows):
    return next(size for size in (512, 320, rows) if rows % size == 0)


def cost(flops, *arrays):
    return pl.CostEstimate(
        flops=flops, transcendentals=0, bytes_accessed=sum(a.size * a.dtype.itemsize for a in arrays)
    )


def call(kernel, name, grid, in_specs, outs, prefetch=0, aliases=None, estimate=None):
    return pl.pallas_call(
        kernel,
        grid_spec=pltpu.PrefetchScalarGridSpec(
            num_scalar_prefetch=prefetch,
            grid=grid,
            in_specs=in_specs,
            out_specs=[pl.BlockSpec(block, index) for block, index, _, _ in outs],
        ),
        out_shape=[jax.ShapeDtypeStruct(shape, kind) for _, _, shape, kind in outs],
        name=name,
        input_output_aliases=aliases or {},
        cost_estimate=estimate,
        compiler_params=pltpu.CompilerParams(
            dimension_semantics=("arbitrary",) * len(grid), vmem_limit_bytes=VMEM
        ),
    )


def fixed(block, *index):
    return pl.BlockSpec(block, lambda *_: index, pipeline_mode=pl.Buffered(1))


GAIN1, GAIN2, SHIFT1, SHIFT2, SHIFT3, SHIFT4 = range(6)


def row(ref, index):
    return ref[index : index + 1, :]


def norm_in_kernel(x_ref, vec_ref, h_ref):
    normed, _ = norm_parts(x_ref[...].astype(f32))
    h_ref[...] = (normed * row(vec_ref, GAIN1) + row(vec_ref, SHIFT1)).astype(bf16)


def norm_in(tokens, vectors):
    rows, width = tokens.shape
    step = pl.BlockSpec((SEQ, width), lambda i: (i, 0))
    return call(
        norm_in_kernel,
        "norm_in",
        (rows // SEQ,),
        [step, fixed(vectors.shape, 0, 0)],
        [((SEQ, width), lambda i: (i, 0), (rows, width), bf16)],
        estimate=cost(16 * rows * width, tokens, tokens),
    )(tokens, vectors)[0]


def project_kernel(h_ref, w_ref, bias_ref, out_ref):
    for shard in range(out_ref.shape[0]):
        out_ref[shard] = (dot(h_ref[...], w_ref[shard]) + bias_ref[shard]).astype(bf16)


def project(h1, weights, bias):
    rows, width = h1.shape
    shards, _, cols = bias.shape
    size = block_rows(rows)
    return call(
        project_kernel,
        "project",
        (rows // size,),
        [
            pl.BlockSpec((size, width), lambda i: (i, 0)),
            fixed((shards, width, cols), 0, 0, 0),
            fixed(bias.shape, 0, 0, 0),
        ],
        [((shards, size, cols), lambda i: (0, i, 0), (shards, rows, cols), bf16)],
        estimate=cost(2 * rows * width * cols * shards, h1, weights),
    )(h1, weights, bias)[0]


def mix_kernel(attn_ref, w_ref, x_ref, vec_ref, mixed_ref, h_ref):
    total = dot_flip(attn_ref[0], w_ref[0])
    for shard in range(1, attn_ref.shape[0]):
        total += dot_flip(attn_ref[shard], w_ref[shard])
    mixed = x_ref[...].astype(f32) + total + row(vec_ref, SHIFT3)
    normed, _ = norm_parts(mixed)
    mixed_ref[...] = mixed
    h_ref[...] = (normed * row(vec_ref, GAIN2) + row(vec_ref, SHIFT2)).astype(bf16)


def mix(attn, weights, tokens, vectors):
    shards, rows, cols = attn.shape
    width = tokens.shape[1]
    size = block_rows(rows)
    step = lambda i: (i, 0)
    return call(
        mix_kernel,
        "mix",
        (rows // size,),
        [
            pl.BlockSpec((shards, size, cols), lambda i: (0, i, 0)),
            fixed((shards, width, cols), 0, 0, 3),
            pl.BlockSpec((size, width), step),
            fixed(vectors.shape, 0, 0),
        ],
        [
            ((size, width), step, (rows, width), f32),
            ((size, width), step, (rows, width), bf16),
        ],
        estimate=cost(2 * rows * width * cols * shards, attn, tokens),
    )(attn, weights, tokens, vectors)


GELU_IN = 0.7978845608
GELU_CUBE = 0.044715


def gelu_parts(pre):
    square = pre * pre
    tanh = jnp.tanh(pre * (GELU_IN + (GELU_IN * GELU_CUBE) * square))
    half = 0.5 * tanh + 0.5
    slope = half + (0.5 * pre * (1.0 - tanh * tanh)) * (GELU_IN + (3.0 * GELU_IN * GELU_CUBE) * square)
    return pre * half, slope


CHUNK = 512


def expand_kernel(h_ref, w_ref, bias_ref, act_ref, slope_ref):
    cols = act_ref.shape[2]
    chunk = min(CHUNK, cols)
    for start in range(0, cols, chunk):
        part = slice(start, start + chunk)
        act, slope = gelu_parts(dot(h_ref[...], w_ref[0, :, part]) + bias_ref[0, :, part])
        act_ref[0, :, part] = act.astype(bf16)
        slope_ref[0, :, part] = slope.astype(bf16)


def expand(h2, weights, bias):
    rows, width = h2.shape
    shards, _, cols = weights.shape
    size = block_rows(rows)
    out = ((1, size, cols), lambda t, i: (t, i, 0), (shards, rows, cols), bf16)
    return call(
        expand_kernel,
        "expand",
        (shards, rows // size),
        [
            pl.BlockSpec((size, width), lambda t, i: (i, 0)),
            pl.BlockSpec((1, width, cols), lambda t, i: (t, 0, 0)),
            pl.BlockSpec((1, 1, cols), lambda t, i: (t, 0, 0)),
        ],
        [out, out],
        estimate=cost(3 * rows * width * cols * shards, h2, weights),
    )(h2, weights, bias)


def expand_back_kernel(g_ref, w_ref, slope_ref, out_ref, bias_ref):
    @pl.when(pl.program_id(1) == 0)
    def _():
        bias_ref[...] = jnp.zeros_like(bias_ref)

    cols = out_ref.shape[2]
    chunk = min(CHUNK, cols)
    for start in range(0, cols, chunk):
        part = slice(start, start + chunk)
        grad = (dot(g_ref[...], w_ref[0, :, part]) * slope_ref[0, :, part].astype(f32)).astype(bf16)
        out_ref[0, :, part] = grad
        bias_ref[0, :, part] += jnp.sum(grad.astype(f32), axis=0, keepdims=True)


def expand_back(grad, weights, slope):
    rows, width = grad.shape
    shards, _, cols = weights.shape
    size = block_rows(rows)
    step = lambda t, i: (t, i, 0)
    return call(
        expand_back_kernel,
        "expand_back",
        (shards, rows // size),
        [
            pl.BlockSpec((size, width), lambda t, i: (i, 0)),
            pl.BlockSpec((1, width, cols), lambda t, i: (t, 0, 0)),
            pl.BlockSpec((1, size, cols), step),
        ],
        [
            ((1, size, cols), step, (shards, rows, cols), bf16),
            ((1, 1, cols), lambda t, i: (t, 0, 0), (shards, 1, cols), f32),
        ],
        estimate=cost(2 * rows * width * cols * shards, slope, slope),
    )(grad, weights, slope)


def dot_rows(left, right):
    return lax.dot_general(left, right, (((0,), (0,)), ((), ())), preferred_element_type=f32)


def weight_grad_kernel(left_ref, right_ref, out_ref, *, chunk, used):
    which = pl.program_id(1)
    start = pl.multiple_of(which * chunk, chunk)
    out_ref[0, :, pl.ds(start, chunk)] = dot_rows(left_ref[...], right_ref[0]).astype(bf16)
    if out_ref.shape[2] > used:

        @pl.when(which == 0)
        def _():
            spare = out_ref.shape[2] - used
            out_ref[0, :, used:] = jnp.zeros((out_ref.shape[1], spare), bf16)


def weight_grad(left, right, spare=0):
    rows, width = left.shape
    shards, _, cols = right.shape
    chunk = min(512, cols)
    return call(
        functools.partial(weight_grad_kernel, chunk=chunk, used=cols),
        "weight_grad",
        (shards, cols // chunk),
        [
            fixed((rows, width), 0, 0),
            pl.BlockSpec((1, rows, chunk), lambda t, n: (t, 0, n)),
        ],
        [
            (
                (1, width, cols + spare),
                lambda t, n: (t, 0, 0),
                (shards, width, cols + spare),
                bf16,
            )
        ],
        estimate=cost(2 * rows * width * cols * shards, left, right),
    )(left, right)[0]


def weight_grad_slots_kernel(slot_ref, left_ref, right_ref, out_ref, *, owners, per_chain):
    which, shard = pl.program_id(0), pl.program_id(1)
    grad = dot_rows(left_ref[...], right_ref[0]).astype(bf16)
    part = out_ref.shape[1]
    base = which // per_chain * out_ref.shape[0] + shard * owners
    for owner in range(owners):
        out_ref[slot_ref[base + owner]] = grad[owner * part : (owner + 1) * part]


def weight_grad_slots(left, right, slots, chains):
    rows, width = left.shape
    shards, _, cols = right.shape
    count = slots.shape[0] // chains
    owners = count // shards
    part = width // owners
    share = cols // chains
    chunk = share if share <= 1024 else 512
    return call(
        functools.partial(weight_grad_slots_kernel, owners=owners, per_chain=share // chunk),
        "weight_grad_slots",
        (cols // chunk, shards),
        [
            fixed((rows, width), 0, 0),
            pl.BlockSpec((1, rows, chunk), lambda n, t, s: (t, 0, n)),
        ],
        [((count, part, chunk), lambda n, t, s: (0, 0, n), (count, part, cols), bf16)],
        prefetch=1,
        estimate=cost(2 * rows * width * cols * shards, left, right),
    )(slots, left, right)[0]


def middle_back_kernel(
    g_ref, up_ref, mixed_ref, gm_ref, vec_ref, out_w_ref, gmixed_ref, go_ref, gattn_ref, sums_ref
):
    @pl.when(pl.program_id(0) == 0)
    def _():
        sums_ref[...] = jnp.zeros_like(sums_ref)

    grad_h = dot_flip(g_ref[0], up_ref[0])
    for shard in range(1, g_ref.shape[0]):
        grad_h += dot_flip(g_ref[shard], up_ref[shard])
    normed, inverse = norm_parts(mixed_ref[...])
    grad = gm_ref[...].astype(f32)
    grad_mixed = grad + norm_back(grad_h * row(vec_ref, GAIN2), normed, inverse)
    gmixed_ref[...] = grad_mixed
    rounded = grad_mixed.astype(bf16)
    go_ref[...] = rounded
    for index, value in enumerate((grad_h * normed, grad_h, grad_mixed, grad)):
        sums_ref[index : index + 1, :] += jnp.sum(value, axis=0, keepdims=True)
    for shard in range(gattn_ref.shape[0]):
        gattn_ref[shard] = dot(rounded, out_w_ref[shard]).astype(bf16)


def middle_back(grad_pre, up, mixed, grad_m, vectors, weights):
    shards, rows, cols = grad_pre.shape
    width = mixed.shape[1]
    heads = weights.shape[2] // 4
    step = lambda i: (i, 0)
    wide = pl.BlockSpec((SEQ, width), step)
    return call(
        middle_back_kernel,
        "middle_back",
        (rows // SEQ,),
        [
            pl.BlockSpec((shards, SEQ, cols), lambda i: (0, i, 0)),
            fixed(up.shape, 0, 0, 0),
            wide,
            wide,
            fixed(vectors.shape, 0, 0),
            fixed((shards, width, heads), 0, 0, 3),
        ],
        [
            ((SEQ, width), step, (rows, width), f32),
            ((SEQ, width), step, (rows, width), bf16),
            ((shards, SEQ, heads), lambda i: (0, i, 0), (shards, rows, heads), bf16),
            ((8, width), lambda i: (0, 0), (8, width), f32),
        ],
        estimate=cost(2 * rows * width * (cols + heads) * shards, grad_pre, up, mixed),
    )(grad_pre, up, mixed, grad_m, vectors, weights)


def input_back_kernel(g_ref, w_ref, x_ref, gmixed_ref, vec_ref, before_ref, *refs):
    out_ref, sums_ref = refs[-2:]

    @pl.when(pl.program_id(0) == 0)
    def _():
        sums_ref[...] = before_ref[...]

    grad_h = dot_flip(g_ref[0], w_ref[0])
    for shard in range(1, g_ref.shape[0]):
        grad_h += dot_flip(g_ref[shard], w_ref[shard])
    normed, inverse = norm_parts(x_ref[...].astype(f32))
    out_ref[...] = gmixed_ref[...] + norm_back(grad_h * row(vec_ref, GAIN1), normed, inverse)
    for index, value in enumerate((grad_h * normed, grad_h)):
        sums_ref[index : index + 1, :] += jnp.sum(value, axis=0, keepdims=True)


def input_back(first, count, grad_heads, weights, tokens, grad_mixed, vectors, sums, *out):
    shards, rows, cols = grad_heads.shape
    width = tokens.shape[1]
    step = lambda i: (first + i, 0)
    wide = pl.BlockSpec((SEQ, width), step)
    return call(
        input_back_kernel,
        "input_back",
        (count,),
        [
            pl.BlockSpec((shards, SEQ, cols), lambda i: (0, first + i, 0)),
            fixed((shards, width, cols), 0, 0, 0),
            wide,
            wide,
            fixed(vectors.shape, 0, 0),
            fixed(sums.shape, 0, 0),
        ]
        + [pl.BlockSpec(memory_space=pl.ANY)] * len(out),
        [
            ((SEQ, width), step, (rows, width), f32),
            ((8, width), lambda i: (0, 0), (8, width), f32),
        ],
        aliases={6: 0} if out else None,
        estimate=cost(2 * count * SEQ * width * cols * shards, weights),
    )(grad_heads, weights, tokens, grad_mixed, vectors, sums, *out)


def shrink_kernel(kept_ref, act_ref, w_ref, mixed_ref, vec_ref, *refs, first):
    out_ref = refs[-1]
    total = dot_flip(act_ref[0], w_ref[0])
    for shard in range(1, act_ref.shape[0]):
        total += dot_flip(act_ref[shard], w_ref[shard])
    valid = BUFFER + kept_ref[first + pl.program_id(0)]
    alive = lax.broadcasted_iota(jnp.int32, (SEQ, 1), 0) < valid
    result = mixed_ref[...] + total + row(vec_ref, SHIFT4)
    out_ref[...] = jnp.where(alive, result, 0.0).astype(bf16)


def shrink(first, count, kept, act, weights, mixed, vectors, *out):
    shards, rows, cols = act.shape
    width = mixed.shape[1]
    step = lambda i, k: (first + i, 0)
    return call(
        functools.partial(shrink_kernel, first=first),
        "shrink",
        (count,),
        [
            pl.BlockSpec((shards, SEQ, cols), lambda i, k: (0, first + i, 0)),
            fixed(weights.shape, 0, 0, 0),
            pl.BlockSpec((SEQ, width), step),
            fixed(vectors.shape, 0, 0),
        ]
        + [pl.BlockSpec(memory_space=pl.ANY)] * len(out),
        [((SEQ, width), step, (rows, width), bf16)],
        prefetch=1,
        aliases={5: 0} if out else None,
        estimate=cost(2 * count * SEQ * width * cols * shards, weights),
    )(kept, act, weights, mixed, vectors, *out)[0]


def swap(values, axis, bit):
    places = range(lax.axis_size(axis))
    return lax.ppermute(values, axis, [(place, place ^ bit) for place in places])


def bits_of(axis):
    return [1 << power for power in range(lax.axis_size(axis).bit_length() - 1)]


def flip_gather(part):
    values = part[None]
    for axis in ("tensor", "dp"):
        for bit in bits_of(axis):
            values = jnp.concatenate([values, swap(values, axis, bit)], 0)
    here = lax.axis_index("dp") * lax.axis_size("tensor") + lax.axis_index("tensor")
    places = jnp.arange(values.shape[0], dtype=jnp.int32) ^ here.astype(jnp.int32)
    values = jnp.take(values, places, axis=0)
    return values.reshape((lax.axis_size("dp"), lax.axis_size("tensor")) + part.shape)


def owner_tables(order):
    dp, shards = lax.axis_size("dp"), lax.axis_size("tensor")
    here = {axis: lax.axis_index(axis).astype(jnp.int32) for axis in ("dp", "tensor")}
    index = jnp.arange(dp * shards, dtype=jnp.int32)
    apart = {"tensor": (index // dp) ^ here["tensor"], "dp": (index % dp) ^ here["dp"]}
    slot = jnp.zeros_like(index)
    place = dict(here)
    for depth, (axis, bit) in enumerate(order):
        weight = 1 << (len(order) - 1 - depth)
        slot += jnp.where((apart[axis] & bit) != 0, weight, 0)
        place[axis] = place[axis] ^ jnp.where((index & weight) != 0, bit, 0)
    return slot, place["tensor"] * dp + place["dp"]


class Chain:
    def __init__(self, values, order):
        self.values, self.order = values, list(order)

    def send(self):
        axis, bit = self.order.pop(0)
        half = self.values.shape[0] // 2
        self.near = self.values[:half]
        self.far = swap(self.values[half:], axis, bit)

    def settle(self):
        self.values = self.near + self.far

    def finish(self):
        self.settle()
        while self.order:
            self.send()
            self.settle()
        return self.values[0]


def meet(values, *chains):
    values, far = lax.optimization_barrier((values, [chain.far for chain in chains]))
    for chain, arrived in zip(chains, far):
        chain.far = arrived
        chain.settle()
        if chain.order:
            chain.send()
    return values


def gather(part):
    full = lax.all_gather(part, ("tensor", "dp"), axis=0, tiled=True)
    return full.reshape(lax.axis_size("tensor"), -1, part.shape[1])


def scatter(full):
    flat = full.reshape(-1, full.shape[2])
    return lax.psum_scatter(flat, ("tensor", "dp"), scatter_dimension=0, tiled=True)


def body(tokens, kept, cotangent, w_qkv, w_out, w_up, w_down, qv_bias, up_bias, ln_gain, shift):
    rows, width = tokens.shape
    dp, shards = lax.axis_size("dp"), lax.axis_size("tensor")
    images = rows // SEQ
    part = w_qkv.shape[1]
    cols = w_qkv.shape[2]
    own = ln_gain.shape[1]
    barrier = lax.optimization_barrier

    full_heads = gather(jnp.concatenate([w_qkv.transpose(1, 0, 2).reshape(part, 3 * cols), w_out.T], 1))
    full_up = gather(w_up)
    full_down = gather(w_down.T)

    small = jnp.concatenate(
        [ln_gain, shift, qv_bias.astype(f32), up_bias.astype(f32).reshape(-1, own)], 0
    )
    small = flip_gather(small)
    vectors = small[:, :, :6].transpose(2, 0, 1, 3).reshape(6, width)
    vectors = jnp.concatenate([vectors, jnp.zeros((2, width), f32)], 0)
    bias_qv = small[:, :, 6:8].transpose(1, 2, 0, 3).reshape(shards, 2, cols)
    bias_up = small[:, :, 8:].transpose(1, 0, 2, 3).reshape(shards, 1, -1)
    bias_heads = jnp.concatenate([bias_qv[:, :1], jnp.zeros_like(bias_qv[:, :1]), bias_qv[:, 1:]], 2)

    first_image = lax.axis_index("tensor") * images
    kept_own = lax.dynamic_slice_in_dim(kept, first_image, images, 0)
    positions = jnp.arange(SEQ, dtype=jnp.int32)
    alive = (positions[None, :] < BUFFER + kept_own[:, None]).reshape(rows, 1)
    grad_m = jnp.where(alive, cotangent, jnp.zeros_like(cotangent))

    core, along_x = [("dp", 1)], [("tensor", bit) for bit in bits_of("tensor")[::-1]]
    low, high = [("dp", 2)], [("dp", bit) for bit in bits_of("dp")[::-1] if bit > 2]
    order_x, order_low = core + along_x + low + high, core + low + along_x + high
    slots_x, owners_x = owner_tables(order_x)
    slots_both = jnp.concatenate([slots_x, owner_tables(order_low)[0]])

    h1 = norm_in(tokens, vectors)
    qkv = project(h1, full_heads, bias_heads)
    attn, expo, inverse_sum = attend(qkv, kept_own)
    mixed, h2 = mix(attn, full_heads, tokens, vectors)
    act, slope = expand(h2, full_up, bias_up)

    spare = act.shape[2] // 8
    grad_down = weight_grad(grad_m, act, spare)
    grad_m, grad_down = barrier((grad_m, grad_down))
    sent_down = scatter(grad_down)[:, : act.shape[2]]
    grad_pre, grad_bias_up = expand_back(grad_m, full_down, slope)
    grad_up = weight_grad(h2, grad_pre, spare)
    grad_pre, grad_up = barrier((grad_pre, grad_up))
    sent_up = scatter(grad_up)[:, : act.shape[2]]
    grad_mixed, grad_o, grad_attn, sums2 = middle_back(
        grad_pre, full_up, mixed, grad_m, vectors, full_heads
    )

    grad_out = weight_grad_slots(grad_o, attn, slots_x, 1)
    grad_attn, grad_out = barrier((grad_attn, grad_out))
    chain_out = Chain(grad_out, order_x)
    chain_out.send()
    grad_heads, grad_bias_qv = attend_back(qkv, grad_attn, attn, expo, inverse_sum)
    grad_heads = meet(grad_heads, chain_out)
    chains = 2 if (3 * cols // 2) % LANES == 0 else 1
    grad_qkv = weight_grad_slots(h1, grad_heads, slots_both if chains == 2 else slots_x, chains)
    grad_qkv = meet(grad_qkv, chain_out)
    grad_heads, grad_qkv = barrier((grad_heads, grad_qkv))
    share = 3 * cols // chains
    chains_qkv = [
        Chain(grad_qkv[..., share * at : share * (at + 1)], order)
        for at, order in enumerate((order_x, order_low)[:chains])
    ]
    for chain in chains_qkv:
        chain.send()

    first = images // 2
    blank = jnp.zeros((8, width), f32)
    grad_tokens, sums1 = input_back(
        0, first, grad_heads, full_heads, tokens, grad_mixed, vectors, blank
    )
    sums1 = meet(sums1, chain_out, *chains_qkv)
    grad_tokens, sums1 = input_back(
        first, images - first, grad_heads, full_heads, tokens, grad_mixed, vectors, sums1, grad_tokens
    )
    sums1, act = meet((sums1, act), chain_out, *chains_qkv)

    sums = jnp.stack([sums1[0], sums2[0], sums1[1], sums2[1], sums2[2], sums2[3]])
    packed = jnp.concatenate(
        [
            sums.reshape(6, dp, shards, own).transpose(2, 1, 0, 3),
            grad_bias_qv.reshape(shards, 2, dp, own).transpose(0, 2, 1, 3),
            grad_bias_up.reshape(shards, dp, -1, own),
        ],
        2,
    )
    packed = jnp.take(packed.reshape((dp * shards,) + packed.shape[2:]), owners_x, axis=0)
    packed, act = barrier((packed, act))
    chain_small = Chain(packed, order_x)
    chain_small.send()
    layer_out = shrink(0, first, kept_own, act, full_down, mixed, vectors)
    layer_out = meet(layer_out, chain_small, *chains_qkv)
    layer_out = shrink(first, images - first, kept_own, act, full_down, mixed, vectors, layer_out)
    layer_out = meet(layer_out, chain_small, *chains_qkv)
    sent_qkv = jnp.concatenate([chain.finish() for chain in chains_qkv], 1)
    sent_out = chain_out.finish()
    sent_small = chain_small.finish()

    return (
        layer_out,
        grad_tokens,
        sent_qkv.astype(f32).reshape(part, 3, cols).transpose(1, 0, 2),
        sent_out.astype(f32).T,
        sent_up.astype(f32),
        sent_down.astype(f32).T,
        sent_small[6:8],
        sent_small[8:].reshape(-1),
        sent_small[:2],
        sent_small[2:6],
    )


def solution(mesh):
    both = P(("dp", "tensor"), None)
    matrices = (
        P(None, "dp", "tensor"),
        P("tensor", "dp"),
        P("dp", "tensor"),
        P("tensor", "dp"),
        P(None, ("tensor", "dp")),
        P(("tensor", "dp")),
        P(None, ("dp", "tensor")),
        P(None, ("dp", "tensor")),
    )
    return jax.shard_map(
        body,
        mesh=mesh,
        in_specs=(both, P("dp"), both) + matrices,
        out_specs=(both, both) + matrices,
        check_vma=False,
    )
```

```python
import functools

import jax
import jax.numpy as jnp
from jax import lax
from jax.experimental import pallas as pl
from jax.experimental.pallas import tpu as pltpu
from jax.sharding import PartitionSpec as P

HEAD_DIM = 64
BUFFER = 64
SEQ = 320
KEYS = 384
LANES = 128
EPSILON = 1e-06
SCALE = HEAD_DIM ** (-0.5)
LOG2E = 1.4426950408889634
NEGATIVE = -1000000000.0 / SCALE
VMEM = 56 << 20

f32 = jnp.float32
bf16 = jnp.bfloat16


def dot(left, right):
    return lax.dot_general(left, right, (((1,), (0,)), ((), ())), preferred_element_type=f32)


def dot_flip(left, right):
    return lax.dot_general(left, right, (((1,), (1,)), ((), ())), preferred_element_type=f32)


def split_heads(values):
    low = lax.broadcasted_iota(jnp.int32, (1, LANES), 1) < HEAD_DIM
    zero = jnp.zeros_like(values)
    return jnp.where(low, values, zero), jnp.where(low, zero, values)


def pad_keys(values):
    return jnp.concatenate([values, jnp.zeros((KEYS - SEQ, values.shape[1]), values.dtype)], 0)


def attend_kernel(kept_ref, q_ref, k_ref, v_ref, o_ref, e_ref, r_ref, *, pairs):
    valid = BUFFER + kept_ref[pl.program_id(1)]
    alive = lax.broadcasted_iota(jnp.int32, (1, KEYS), 1) < valid
    ones = split_heads(jnp.ones((KEYS, LANES), bf16))
    for pair in range(pairs):
        cols = slice(LANES * pair, LANES * (pair + 1))
        keys = pad_keys(k_ref[0, :, cols])
        values = split_heads(pad_keys(v_ref[0, :, cols]))
        expos = []
        for head, query in enumerate(split_heads(q_ref[0, :, cols])):
            scores = jnp.where(alive, dot_flip(query, keys), NEGATIVE)
            highest = jnp.max(scores, axis=-1, keepdims=True)
            expo = jnp.exp2((scores - highest) * (SCALE * LOG2E)).astype(bf16)
            e_ref[0, 0, pair, head] = expo
            expos.append(expo)
        right = jnp.concatenate(
            [jnp.concatenate([value, one], 1) for value, one in zip(values, ones)], 0
        )
        both = dot(jnp.concatenate(expos, 1), right)
        inverse = 1.0 / both[:, LANES:]
        o_ref[0, :, cols] = (both[:, :LANES] * inverse).astype(bf16)
        r_ref[0, :, cols] = inverse


def attend(qkv, kept):
    shards, rows, width = qkv.shape
    cols = width // 3
    pairs = cols // LANES
    images = rows // SEQ
    part = lambda which: pl.BlockSpec((1, SEQ, cols), lambda t, i, k: (t, i, which))
    probs = pl.BlockSpec((1, 1, pairs, 2, SEQ, KEYS), lambda t, i, k: (t, i, 0, 0, 0, 0))
    return pl.pallas_call(
        functools.partial(attend_kernel, pairs=pairs),
        grid_spec=pltpu.PrefetchScalarGridSpec(
            num_scalar_prefetch=1,
            grid=(shards, images),
            in_specs=[part(0), part(1), part(2)],
            out_specs=[part(0), probs, part(0)],
        ),
        out_shape=[
            jax.ShapeDtypeStruct((shards, rows, cols), bf16),
            jax.ShapeDtypeStruct((shards, images, pairs, 2, SEQ, KEYS), bf16),
            jax.ShapeDtypeStruct((shards, rows, cols), f32),
        ],
        name="attend",
        cost_estimate=cost(rows * cols * shards * SEQ * 16, qkv, qkv),
        compiler_params=pltpu.CompilerParams(
            dimension_semantics=("arbitrary", "arbitrary"), vmem_limit_bytes=VMEM
        ),
    )(kept, qkv, qkv, qkv)


def attend_back_kernel(q_ref, k_ref, v_ref, g_ref, o_ref, e_ref, r_ref, out_ref, bias_ref, *, pairs):
    width = pairs * LANES

    @pl.when(pl.program_id(1) == 0)
    def _():
        bias_ref[...] = jnp.zeros_like(bias_ref)

    for pair in range(pairs):
        cols = slice(LANES * pair, LANES * (pair + 1))
        query = q_ref[0, :, cols]
        values = pad_keys(v_ref[0, :, cols])
        grad = (g_ref[0, :, cols].astype(f32) * r_ref[0, :, cols]).astype(bf16)
        product = split_heads(grad.astype(f32) * o_ref[0, :, cols].astype(f32))
        grads = []
        for head, grad_head in enumerate(split_heads(grad)):
            inner = jnp.sum(product[head], axis=-1, keepdims=True)
            expo = e_ref[0, 0, pair, head].astype(f32)
            grads.append((expo * (dot_flip(grad_head, values) - inner)).astype(bf16))
        keys = jnp.concatenate(split_heads(pad_keys(k_ref[0, :, cols])), 0)
        grad_query = (dot(jnp.concatenate(grads, 1), keys) * SCALE).astype(bf16)
        query_flip, grad_flip = query.T, grad.T
        halves = [slice(HEAD_DIM * head, HEAD_DIM * (head + 1)) for head in range(2)]
        grad_key = jnp.concatenate([dot(query_flip[half], grads[h]) for h, half in enumerate(halves)], 0)
        grad_value = jnp.concatenate(
            [dot(grad_flip[half], e_ref[0, 0, pair, h]) for h, half in enumerate(halves)], 0
        )
        grad_key = (grad_key.T[:SEQ] * SCALE).astype(bf16)
        grad_value = grad_value.T[:SEQ].astype(bf16)
        for which, value in enumerate((grad_query, grad_key, grad_value)):
            start = which * width + LANES * pair
            out_ref[0, :, start : start + LANES] = value
        bias_ref[0, 0:1, cols] += jnp.sum(grad_query.astype(f32), axis=0, keepdims=True)
        bias_ref[0, 1:2, cols] += jnp.sum(grad_value.astype(f32), axis=0, keepdims=True)


def attend_back(qkv, grad, attn, expo, inverse):
    shards, rows, width = qkv.shape
    cols = width // 3
    pairs = cols // LANES
    images = rows // SEQ
    part = lambda which: pl.BlockSpec((1, SEQ, cols), lambda t, i: (t, i, which))
    probs = pl.BlockSpec((1, 1, pairs, 2, SEQ, KEYS), lambda t, i: (t, i, 0, 0, 0, 0))
    return pl.pallas_call(
        functools.partial(attend_back_kernel, pairs=pairs),
        grid=(shards, images),
        in_specs=[part(0), part(1), part(2), part(0), part(0), probs, part(0)],
        out_specs=[
            pl.BlockSpec((1, SEQ, width), lambda t, i: (t, i, 0)),
            pl.BlockSpec((1, 2, cols), lambda t, i: (t, 0, 0)),
        ],
        out_shape=[
            jax.ShapeDtypeStruct((shards, rows, width), bf16),
            jax.ShapeDtypeStruct((shards, 2, cols), f32),
        ],
        name="attend_back",
        cost_estimate=cost(rows * cols * shards * SEQ * 24, qkv, qkv, expo),
        compiler_params=pltpu.CompilerParams(
            dimension_semantics=("arbitrary", "arbitrary"), vmem_limit_bytes=VMEM
        ),
    )(qkv, qkv, qkv, grad, attn, expo, inverse)


def norm_parts(values):
    centred = values - jnp.mean(values, axis=-1, keepdims=True)
    inverse = lax.rsqrt(jnp.mean(centred * centred, axis=-1, keepdims=True) + EPSILON)
    return centred * inverse, inverse


def norm_back(grad_normed, normed, inverse):
    first = jnp.mean(grad_normed, axis=-1, keepdims=True)
    second = jnp.mean(grad_normed * normed, axis=-1, keepdims=True)
    return inverse * (grad_normed - first - normed * second)


def block_rows(rows):
    return next(size for size in (512, 320, rows) if rows % size == 0)


def cost(flops, *arrays):
    return pl.CostEstimate(
        flops=flops, transcendentals=0, bytes_accessed=sum(a.size * a.dtype.itemsize for a in arrays)
    )


def call(kernel, name, grid, in_specs, outs, prefetch=0, aliases=None, estimate=None):
    return pl.pallas_call(
        kernel,
        grid_spec=pltpu.PrefetchScalarGridSpec(
            num_scalar_prefetch=prefetch,
            grid=grid,
            in_specs=in_specs,
            out_specs=[pl.BlockSpec(block, index) for block, index, _, _ in outs],
        ),
        out_shape=[jax.ShapeDtypeStruct(shape, kind) for _, _, shape, kind in outs],
        name=name,
        input_output_aliases=aliases or {},
        cost_estimate=estimate,
        compiler_params=pltpu.CompilerParams(
            dimension_semantics=("arbitrary",) * len(grid), vmem_limit_bytes=VMEM
        ),
    )


def fixed(block, *index):
    return pl.BlockSpec(block, lambda *_: index, pipeline_mode=pl.Buffered(1))


GAIN1, GAIN2, SHIFT1, SHIFT2, SHIFT3, SHIFT4 = range(6)


def row(ref, index):
    return ref[index : index + 1, :]


def norm_in_kernel(x_ref, vec_ref, h_ref):
    normed, _ = norm_parts(x_ref[...].astype(f32))
    h_ref[...] = (normed * row(vec_ref, GAIN1) + row(vec_ref, SHIFT1)).astype(bf16)


def norm_in(tokens, vectors):
    rows, width = tokens.shape
    step = pl.BlockSpec((SEQ, width), lambda i: (i, 0))
    return call(
        norm_in_kernel,
        "norm_in",
        (rows // SEQ,),
        [step, fixed(vectors.shape, 0, 0)],
        [((SEQ, width), lambda i: (i, 0), (rows, width), bf16)],
        estimate=cost(16 * rows * width, tokens, tokens),
    )(tokens, vectors)[0]


def project_kernel(h_ref, w_ref, bias_ref, out_ref):
    for shard in range(out_ref.shape[0]):
        out_ref[shard] = (dot(h_ref[...], w_ref[shard]) + bias_ref[shard]).astype(bf16)


def project(h1, weights, bias):
    rows, width = h1.shape
    shards, _, cols = bias.shape
    size = block_rows(rows)
    return call(
        project_kernel,
        "project",
        (rows // size,),
        [
            pl.BlockSpec((size, width), lambda i: (i, 0)),
            fixed((shards, width, cols), 0, 0, 0),
            fixed(bias.shape, 0, 0, 0),
        ],
        [((shards, size, cols), lambda i: (0, i, 0), (shards, rows, cols), bf16)],
        estimate=cost(2 * rows * width * cols * shards, h1, weights),
    )(h1, weights, bias)[0]


def mix_kernel(attn_ref, w_ref, x_ref, vec_ref, mixed_ref, h_ref):
    total = dot_flip(attn_ref[0], w_ref[0])
    for shard in range(1, attn_ref.shape[0]):
        total += dot_flip(attn_ref[shard], w_ref[shard])
    mixed = x_ref[...].astype(f32) + total + row(vec_ref, SHIFT3)
    normed, _ = norm_parts(mixed)
    mixed_ref[...] = mixed
    h_ref[...] = (normed * row(vec_ref, GAIN2) + row(vec_ref, SHIFT2)).astype(bf16)


def mix(attn, weights, tokens, vectors):
    shards, rows, cols = attn.shape
    width = tokens.shape[1]
    size = block_rows(rows)
    step = lambda i: (i, 0)
    return call(
        mix_kernel,
        "mix",
        (rows // size,),
        [
            pl.BlockSpec((shards, size, cols), lambda i: (0, i, 0)),
            fixed((shards, width, cols), 0, 0, 3),
            pl.BlockSpec((size, width), step),
            fixed(vectors.shape, 0, 0),
        ],
        [
            ((size, width), step, (rows, width), f32),
            ((size, width), step, (rows, width), bf16),
        ],
        estimate=cost(2 * rows * width * cols * shards, attn, tokens),
    )(attn, weights, tokens, vectors)


GELU_IN = 0.7978845608
GELU_CUBE = 0.044715


def gelu_parts(pre):
    cube = (GELU_IN * GELU_CUBE) * (pre * pre)
    half = 0.5 * jnp.tanh(pre * (GELU_IN + cube)) + 0.5
    act = pre * half
    return act, half + (act - act * half) * (2.0 * GELU_IN + 6.0 * cube)


CHUNK = 512


def expand_kernel(h_ref, w_ref, bias_ref, act_ref, slope_ref):
    cols = act_ref.shape[2]
    chunk = min(CHUNK, cols)
    for start in range(0, cols, chunk):
        part = slice(start, start + chunk)
        act, slope = gelu_parts(dot(h_ref[...], w_ref[0, :, part]) + bias_ref[0, :, part])
        act_ref[0, :, part] = act.astype(bf16)
        slope_ref[0, :, part] = slope.astype(bf16)


def expand(h2, weights, bias):
    rows, width = h2.shape
    shards, _, cols = weights.shape
    size = block_rows(rows)
    out = ((1, size, cols), lambda t, i: (t, i, 0), (shards, rows, cols), bf16)
    return call(
        expand_kernel,
        "expand",
        (shards, rows // size),
        [
            pl.BlockSpec((size, width), lambda t, i: (i, 0)),
            pl.BlockSpec((1, width, cols), lambda t, i: (t, 0, 0)),
            pl.BlockSpec((1, 1, cols), lambda t, i: (t, 0, 0)),
        ],
        [out, out],
        estimate=cost(3 * rows * width * cols * shards, h2, weights),
    )(h2, weights, bias)


def expand_back_kernel(g_ref, w_ref, slope_ref, out_ref, bias_ref):
    @pl.when(pl.program_id(1) == 0)
    def _():
        bias_ref[...] = jnp.zeros_like(bias_ref)

    cols = out_ref.shape[2]
    chunk = min(CHUNK, cols)
    for start in range(0, cols, chunk):
        part = slice(start, start + chunk)
        grad = (dot(g_ref[...], w_ref[0, :, part]) * slope_ref[0, :, part].astype(f32)).astype(bf16)
        out_ref[0, :, part] = grad
        bias_ref[0, :, part] += jnp.sum(grad.astype(f32), axis=0, keepdims=True)


def expand_back(grad, weights, slope):
    rows, width = grad.shape
    shards, _, cols = weights.shape
    size = block_rows(rows)
    step = lambda t, i: (t, i, 0)
    return call(
        expand_back_kernel,
        "expand_back",
        (shards, rows // size),
        [
            pl.BlockSpec((size, width), lambda t, i: (i, 0)),
            pl.BlockSpec((1, width, cols), lambda t, i: (t, 0, 0)),
            pl.BlockSpec((1, size, cols), step),
        ],
        [
            ((1, size, cols), step, (shards, rows, cols), bf16),
            ((1, 1, cols), lambda t, i: (t, 0, 0), (shards, 1, cols), f32),
        ],
        estimate=cost(2 * rows * width * cols * shards, slope, slope),
    )(grad, weights, slope)


def dot_rows(left, right):
    return lax.dot_general(left, right, (((0,), (0,)), ((), ())), preferred_element_type=f32)


def weight_grad_kernel(left_ref, right_ref, out_ref, *, chunk, fill):
    which = pl.program_id(1)
    start = pl.multiple_of(which * chunk, chunk)
    out_ref[0, :, pl.ds(start, chunk)] = dot_rows(left_ref[...], right_ref[0]).astype(bf16)
    if fill:

        @pl.when(which == 0)
        def _():
            spare = jnp.zeros((out_ref.shape[1], fill), bf16)
            out_ref[0, :, out_ref.shape[2] - fill :] = spare


def weight_grad(left, right, used, spare, fill):
    rows, width = left.shape
    shards = right.shape[0]
    chunk = min(512, used)
    block = (1, width, used + spare)
    return call(
        functools.partial(weight_grad_kernel, chunk=chunk, fill=spare if fill else 0),
        "weight_grad",
        (shards, used // chunk),
        [
            fixed((rows, width), 0, 0),
            pl.BlockSpec((1, rows, chunk), lambda t, n: (t, 0, n)),
        ],
        [(block, lambda t, n: (t, 0, 0), (shards,) + block[1:], bf16)],
        estimate=cost(2 * rows * width * used * shards, left, right),
    )(left, right)[0]


def weight_grad_into_kernel(left_ref, right_ref, _, out_ref):
    out_ref[0] = dot_rows(left_ref[...], right_ref[0]).astype(bf16)


def weight_grad_into(left, right, out):
    rows, width = left.shape
    shards, _, cols = right.shape
    place = out.shape[2] // cols - 1
    return call(
        weight_grad_into_kernel,
        "weight_grad_into",
        (shards,),
        [
            fixed((rows, width), 0, 0),
            pl.BlockSpec((1, rows, cols), lambda t: (t, 0, 0)),
            pl.BlockSpec(memory_space=pl.ANY),
        ],
        [((1, width, cols), lambda t: (t, 0, place), out.shape, bf16)],
        aliases={2: 0},
        estimate=cost(2 * rows * width * cols * shards, left, right),
    )(left, right, out)[0]


def weight_grad_split_kernel(slot_ref, left_ref, right_ref, *out_refs, per_chain):
    which, shard = pl.program_id(0), pl.program_id(1)
    grad = dot_rows(left_ref[...], right_ref[0]).astype(bf16)
    pairs = grad.shape[0] // (2 * out_refs[0].shape[1])
    second = slot_ref[slot_ref.shape[0] - 1] == 1
    for chain in range(len(out_refs) // 2):

        @pl.when(which // per_chain == chain)
        def _():
            near_ref, far_ref = out_refs[2 * chain : 2 * chain + 2]
            part = near_ref.shape[1]
            base = chain * near_ref.shape[0] + shard * pairs
            for pair in range(pairs):
                slot = slot_ref[base + pair]
                low = grad[2 * pair * part : (2 * pair + 1) * part]
                high = grad[(2 * pair + 1) * part : (2 * pair + 2) * part]
                near_ref[slot] = jnp.where(second, high, low)
                far_ref[slot] = jnp.where(second, low, high)


def weight_grad_split(left, right, first, share, tables, second):
    rows, width = left.shape
    shards, _, _ = right.shape
    chains = len(tables)
    half = tables[0].shape[0]
    part = width // (2 * half // shards)
    chunk = share if share <= 1024 else 512
    per_chain = share // chunk
    out = lambda chain: (
        (half, part, chunk),
        lambda n, t, s: (0, 0, jnp.clip(n - chain * per_chain, 0, per_chain - 1)),
        (half, part, share),
        bf16,
    )
    parts = call(
        functools.partial(weight_grad_split_kernel, per_chain=per_chain),
        "weight_grad_split",
        (chains * per_chain, shards),
        [
            fixed((rows, width), 0, 0),
            pl.BlockSpec((1, rows, chunk), lambda n, t, s: (t, 0, first // chunk + n)),
        ],
        [out(chain) for chain in range(chains) for _ in range(2)],
        prefetch=1,
        estimate=cost(2 * rows * width * share * chains * shards, left, right),
    )(jnp.concatenate(list(tables) + [second[None]]), left, right)
    return [(parts[2 * chain], parts[2 * chain + 1]) for chain in range(chains)]


def middle_back_kernel(
    g_ref, up_ref, mixed_ref, gm_ref, vec_ref, out_w_ref, gmixed_ref, go_ref, gattn_ref, sums_ref
):
    @pl.when(pl.program_id(0) == 0)
    def _():
        sums_ref[...] = jnp.zeros_like(sums_ref)

    grad_h = dot_flip(g_ref[0], up_ref[0])
    for shard in range(1, g_ref.shape[0]):
        grad_h += dot_flip(g_ref[shard], up_ref[shard])
    normed, inverse = norm_parts(mixed_ref[...])
    grad = gm_ref[...].astype(f32)
    grad_mixed = grad + norm_back(grad_h * row(vec_ref, GAIN2), normed, inverse)
    gmixed_ref[...] = grad_mixed
    rounded = grad_mixed.astype(bf16)
    go_ref[...] = rounded
    for index, value in ((1, grad_h * normed), (3, grad_h), (4, grad_mixed), (5, grad)):
        sums_ref[index : index + 1, :] += jnp.sum(value, axis=0, keepdims=True)
    for shard in range(gattn_ref.shape[0]):
        gattn_ref[shard] = dot(rounded, out_w_ref[shard]).astype(bf16)


def middle_back(grad_pre, up, mixed, grad_m, vectors, weights):
    shards, rows, cols = grad_pre.shape
    width = mixed.shape[1]
    heads = weights.shape[2] // 4
    step = lambda i: (i, 0)
    wide = pl.BlockSpec((SEQ, width), step)
    return call(
        middle_back_kernel,
        "middle_back",
        (rows // SEQ,),
        [
            pl.BlockSpec((shards, SEQ, cols), lambda i: (0, i, 0)),
            fixed(up.shape, 0, 0, 0),
            wide,
            wide,
            fixed(vectors.shape, 0, 0),
            fixed((shards, width, heads), 0, 0, 3),
        ],
        [
            ((SEQ, width), step, (rows, width), f32),
            ((SEQ, width), step, (rows, width), bf16),
            ((shards, SEQ, heads), lambda i: (0, i, 0), (shards, rows, heads), bf16),
            ((8, width), lambda i: (0, 0), (8, width), f32),
        ],
        estimate=cost(2 * rows * width * (cols + heads) * shards, grad_pre, up, mixed),
    )(grad_pre, up, mixed, grad_m, vectors, weights)


def input_back_kernel(g_ref, w_ref, x_ref, gmixed_ref, vec_ref, before_ref, *refs):
    out_ref, sums_ref = refs[-2:]

    @pl.when(pl.program_id(0) == 0)
    def _():
        sums_ref[...] = before_ref[...]

    grad_h = dot_flip(g_ref[0], w_ref[0])
    for shard in range(1, g_ref.shape[0]):
        grad_h += dot_flip(g_ref[shard], w_ref[shard])
    normed, inverse = norm_parts(x_ref[...].astype(f32))
    out_ref[...] = gmixed_ref[...] + norm_back(grad_h * row(vec_ref, GAIN1), normed, inverse)
    for index, value in ((0, grad_h * normed), (2, grad_h)):
        sums_ref[index : index + 1, :] += jnp.sum(value, axis=0, keepdims=True)


def input_back(first, count, grad_heads, weights, tokens, grad_mixed, vectors, sums, *out):
    shards, rows, cols = grad_heads.shape
    width = tokens.shape[1]
    step = lambda i: (first + i, 0)
    wide = pl.BlockSpec((SEQ, width), step)
    return call(
        input_back_kernel,
        "input_back",
        (count,),
        [
            pl.BlockSpec((shards, SEQ, cols), lambda i: (0, first + i, 0)),
            fixed((shards, width, cols), 0, 0, 0),
            wide,
            wide,
            fixed(vectors.shape, 0, 0),
            fixed(sums.shape, 0, 0),
        ]
        + [pl.BlockSpec(memory_space=pl.ANY)] * len(out),
        [
            ((SEQ, width), step, (rows, width), f32),
            (sums.shape, lambda i: (0, 0), sums.shape, f32),
        ],
        aliases={6: 0} if out else None,
        estimate=cost(2 * count * SEQ * width * cols * shards, weights),
    )(grad_heads, weights, tokens, grad_mixed, vectors, sums, *out)


def shrink_kernel(kept_ref, act_ref, w_ref, mixed_ref, vec_ref, *refs, first):
    out_ref = refs[-1]
    total = dot_flip(act_ref[0], w_ref[0])
    for shard in range(1, act_ref.shape[0]):
        total += dot_flip(act_ref[shard], w_ref[shard])
    valid = BUFFER + kept_ref[first + pl.program_id(0)]
    alive = lax.broadcasted_iota(jnp.int32, (SEQ, 1), 0) < valid
    result = mixed_ref[...] + total + row(vec_ref, SHIFT4)
    out_ref[...] = jnp.where(alive, result, 0.0).astype(bf16)


def shrink(first, count, kept, act, weights, mixed, vectors, *out):
    shards, rows, cols = act.shape
    width = mixed.shape[1]
    step = lambda i, k: (first + i, 0)
    return call(
        functools.partial(shrink_kernel, first=first),
        "shrink",
        (count,),
        [
            pl.BlockSpec((shards, SEQ, cols), lambda i, k: (0, first + i, 0)),
            fixed(weights.shape, 0, 0, 0),
            pl.BlockSpec((SEQ, width), step),
            fixed(vectors.shape, 0, 0),
        ]
        + [pl.BlockSpec(memory_space=pl.ANY)] * len(out),
        [((SEQ, width), step, (rows, width), bf16)],
        prefetch=1,
        aliases={5: 0} if out else None,
        estimate=cost(2 * count * SEQ * width * cols * shards, weights),
    )(kept, act, weights, mixed, vectors, *out)[0]


def swap(values, axis, bit):
    places = range(lax.axis_size(axis))
    return lax.ppermute(values, axis, [(place, place ^ bit) for place in places])


def bits_of(axis):
    return [1 << power for power in range(lax.axis_size(axis).bit_length() - 1)]


def flip_gather(part):
    values = part[None]
    for axis in ("tensor", "dp"):
        for bit in bits_of(axis):
            values = jnp.concatenate([values, swap(values, axis, bit)], 0)
    here = lax.axis_index("dp") * lax.axis_size("tensor") + lax.axis_index("tensor")
    places = jnp.arange(values.shape[0], dtype=jnp.int32) ^ here.astype(jnp.int32)
    values = jnp.take(values, places, axis=0)
    return values.reshape((lax.axis_size("dp"), lax.axis_size("tensor")) + part.shape)


def slot_table(order):
    dp, shards = lax.axis_size("dp"), lax.axis_size("tensor")
    index = jnp.arange(shards * dp // 2, dtype=jnp.int32)
    apart = {
        "tensor": (index // (dp // 2)) ^ lax.axis_index("tensor").astype(jnp.int32),
        "dp": (2 * (index % (dp // 2))) ^ lax.axis_index("dp").astype(jnp.int32),
    }
    slot = jnp.zeros_like(index)
    for depth, (axis, bit) in enumerate(order[1:]):
        slot += jnp.where((apart[axis] & bit) != 0, 1 << (len(order) - 2 - depth), 0)
    return slot


class Chain:
    def __init__(self, near, far, order):
        self.near, self.order = near, list(order)
        self.far = swap(far, *self.order.pop(0))

    def send(self):
        half = self.values.shape[0] // 2
        self.near = self.values[:half]
        self.far = swap(self.values[half:], *self.order.pop(0))

    def settle(self):
        self.values = self.near + self.far

    def finish(self):
        self.settle()
        while self.order:
            self.send()
            self.settle()
        return self.values[0]


class Sum(Chain):
    def __init__(self, values, order):
        self.values, self.order = values, list(order)
        self.send()

    def send(self):
        self.near = self.values
        self.far = swap(self.values, *self.order.pop(0))

    def finish(self):
        super().finish()
        return self.values


def meet(values, *chains):
    values, far = lax.optimization_barrier((values, [chain.far for chain in chains]))
    for chain, arrived in zip(chains, far):
        chain.far = arrived
        chain.settle()
        if chain.order:
            chain.send()
    return values


def gather(part):
    full = lax.all_gather(part, ("tensor", "dp"), axis=0, tiled=True)
    return full.reshape(lax.axis_size("tensor"), -1, part.shape[1])


def scatter(full):
    flat = full.reshape(-1, full.shape[2])
    return lax.psum_scatter(flat, ("tensor", "dp"), scatter_dimension=0, tiled=True)


def body(tokens, kept, cotangent, w_qkv, w_out, w_up, w_down, qv_bias, up_bias, ln_gain, shift):
    rows, width = tokens.shape
    dp, shards = lax.axis_size("dp"), lax.axis_size("tensor")
    images = rows // SEQ
    part = w_qkv.shape[1]
    cols = w_qkv.shape[2]
    own = ln_gain.shape[1]
    barrier = lax.optimization_barrier

    full_heads = gather(jnp.concatenate([w_qkv.transpose(1, 0, 2).reshape(part, 3 * cols), w_out.T], 1))
    full_up = gather(w_up)
    full_down = gather(w_down.T)

    small = jnp.concatenate(
        [ln_gain, shift, qv_bias.astype(f32), up_bias.astype(f32).reshape(-1, own)], 0
    )
    small = flip_gather(small)
    vectors = small[:, :, :6].transpose(2, 0, 1, 3).reshape(6, width)
    vectors = jnp.concatenate([vectors, jnp.zeros((2, width), f32)], 0)
    bias_qv = small[:, :, 6:8].transpose(1, 2, 0, 3).reshape(shards, 2, cols)
    bias_up = small[:, :, 8:].transpose(1, 0, 2, 3).reshape(shards, 1, -1)
    bias_heads = jnp.concatenate([bias_qv[:, :1], jnp.zeros_like(bias_qv[:, :1]), bias_qv[:, 1:]], 2)

    first_image = lax.axis_index("tensor") * images
    kept_own = lax.dynamic_slice_in_dim(kept, first_image, images, 0)
    positions = jnp.arange(SEQ, dtype=jnp.int32)
    alive = (positions[None, :] < BUFFER + kept_own[:, None]).reshape(rows, 1)
    grad_m = jnp.where(alive, cotangent, jnp.zeros_like(cotangent))

    core, along_x = [("dp", 1)], [("tensor", bit) for bit in bits_of("tensor")[::-1]]
    low, high = [("dp", 2)], [("dp", bit) for bit in bits_of("dp")[::-1] if bit > 2]
    order_x, order_low = core + along_x + low + high, core + low + along_x + high
    tables = [slot_table(order_x), slot_table(order_low)]
    second = lax.axis_index("dp").astype(jnp.int32) & 1

    h1 = norm_in(tokens, vectors)
    qkv = project(h1, full_heads, bias_heads)
    attn, expo, inverse_sum = attend(qkv, kept_own)
    mixed, h2 = mix(attn, full_heads, tokens, vectors)
    act, slope = expand(h2, full_up, bias_up)

    hidden = act.shape[2]
    grad_down = weight_grad(grad_m, act, hidden, hidden // 8, True)
    grad_m, grad_down = barrier((grad_m, grad_down))
    sent_down = scatter(grad_down)[:, :hidden]
    grad_pre, grad_bias_up = expand_back(grad_m, full_down, slope)

    share = hidden // 2
    ((near, far),) = weight_grad_split(h2, grad_pre, share, share, tables[:1], second)
    grad_pre, near, far = barrier((grad_pre, near, far))
    chain_up = Chain(near, far, order_x)
    grad_first = weight_grad(h2, grad_pre, share, cols, False)
    grad_pre, grad_first = barrier((grad_pre, grad_first))
    grad_pre = meet(grad_pre, chain_up)
    grad_mixed, grad_o, grad_attn, sums2 = middle_back(
        grad_pre, full_up, mixed, grad_m, vectors, full_heads
    )
    grad_o = meet(grad_o, chain_up)
    grad_first = weight_grad_into(grad_o, attn, grad_first)
    grad_attn, grad_first = barrier((grad_attn, grad_first))
    grad_heads, grad_bias_qv = attend_back(qkv, grad_attn, attn, expo, inverse_sum)
    grad_heads = meet(grad_heads, chain_up)
    grad_heads, sent_down, grad_first = barrier((grad_heads, sent_down, grad_first))
    sent_first = scatter(grad_first)

    chains = 2 if (3 * cols // 2) % LANES == 0 else 1
    halves = weight_grad_split(h1, grad_heads, 0, 3 * cols // chains, tables[:chains], second)
    grad_heads, halves = barrier((grad_heads, halves))
    chains_qkv = [Chain(*half, order) for half, order in zip(halves, (order_x, order_low))]
    sums = jnp.concatenate(
        [
            sums2[:6],
            grad_bias_qv.transpose(1, 0, 2).reshape(2, width),
            grad_bias_up.reshape(-1, width),
        ],
        0,
    )
    grad_heads = meet(grad_heads, chain_up)
    first = images // 2
    grad_tokens, sums = input_back(
        0, first, grad_heads, full_heads, tokens, grad_mixed, vectors, sums
    )
    sums = meet(sums, *chains_qkv)
    grad_tokens, sums = input_back(
        first, images - first, grad_heads, full_heads, tokens, grad_mixed, vectors, sums, grad_tokens
    )
    chain_small = Sum(sums, order_x)
    act = meet(barrier((act, sums))[0], *chains_qkv)
    layer_out = shrink(0, first, kept_own, act, full_down, mixed, vectors)
    layer_out = meet(layer_out, chain_small, *chains_qkv)
    layer_out = shrink(first, images - first, kept_own, act, full_down, mixed, vectors, layer_out)
    layer_out = meet(layer_out, chain_small, *chains_qkv)
    sent_up = jnp.concatenate([sent_first[:, :share], chain_up.finish()], 1)
    sent_qkv = jnp.concatenate([chain.finish() for chain in chains_qkv], 1)
    small = chain_small.finish()
    at_dp, at_tensor = lax.axis_index("dp"), lax.axis_index("tensor")
    row_place, shard_place = at_dp * shards + at_tensor, at_tensor * dp + at_dp
    rows_own = lax.dynamic_slice(small, (0, row_place * own), (6, own))
    heads_own = lax.dynamic_slice(small, (6, shard_place * own), (2, own))
    count = up_bias.shape[0]
    start = shard_place * count
    up_own = lax.dynamic_slice(small, (8 + start // width, start % width), (1, count))

    return (
        layer_out,
        grad_tokens,
        sent_qkv.astype(f32).reshape(part, 3, cols).transpose(1, 0, 2),
        sent_first[:, share:].astype(f32).T,
        sent_up.astype(f32),
        sent_down.astype(f32).T,
        heads_own,
        up_own.reshape(-1),
        rows_own[:2],
        rows_own[2:],
    )


def solution(mesh):
    both = P(("dp", "tensor"), None)
    matrices = (
        P(None, "dp", "tensor"),
        P("tensor", "dp"),
        P("dp", "tensor"),
        P("tensor", "dp"),
        P(None, ("tensor", "dp")),
        P(("tensor", "dp")),
        P(None, ("dp", "tensor")),
        P(None, ("dp", "tensor")),
    )
    return jax.shard_map(
        body,
        mesh=mesh,
        in_specs=(both, P("dp"), both) + matrices,
        out_specs=(both, both) + matrices,
        check_vma=False,
    )
```

```python
import functools

import jax
import jax.numpy as jnp
from jax import lax
from jax.experimental import pallas as pl
from jax.experimental.pallas import tpu as pltpu
from jax.sharding import PartitionSpec as P

HEAD_DIM = 64
BUFFER = 64
SEQ = 320
KEYS = 384
LANES = 128
EPSILON = 1e-06
SCALE = HEAD_DIM ** (-0.5)
LOG2E = 1.4426950408889634
NEGATIVE = -1000000000.0 / SCALE
VMEM = 56 << 20

f32 = jnp.float32
bf16 = jnp.bfloat16


def dot(left, right):
    return lax.dot_general(left, right, (((1,), (0,)), ((), ())), preferred_element_type=f32)


def dot_flip(left, right):
    return lax.dot_general(left, right, (((1,), (1,)), ((), ())), preferred_element_type=f32)


def split_heads(values):
    low = lax.broadcasted_iota(jnp.int32, (1, LANES), 1) < HEAD_DIM
    zero = jnp.zeros_like(values)
    return jnp.where(low, values, zero), jnp.where(low, zero, values)


def pad_keys(values):
    return jnp.concatenate([values, jnp.zeros((KEYS - SEQ, values.shape[1]), values.dtype)], 0)


def attend_kernel(kept_ref, q_ref, k_ref, v_ref, o_ref, e_ref, r_ref, *, pairs):
    valid = BUFFER + kept_ref[pl.program_id(1)]
    alive = lax.broadcasted_iota(jnp.int32, (1, KEYS), 1) < valid
    ones = split_heads(jnp.ones((KEYS, LANES), bf16))
    for pair in range(pairs):
        cols = slice(LANES * pair, LANES * (pair + 1))
        keys = pad_keys(k_ref[0, :, cols])
        values = split_heads(pad_keys(v_ref[0, :, cols]))
        expos = []
        for head, query in enumerate(split_heads(q_ref[0, :, cols])):
            scores = jnp.where(alive, dot_flip(query, keys), NEGATIVE)
            highest = jnp.max(scores, axis=-1, keepdims=True)
            expo = jnp.exp2((scores - highest) * (SCALE * LOG2E)).astype(bf16)
            e_ref[0, 0, pair, head] = expo
            expos.append(expo)
        right = jnp.concatenate(
            [jnp.concatenate([value, one], 1) for value, one in zip(values, ones)], 0
        )
        both = dot(jnp.concatenate(expos, 1), right)
        inverse = 1.0 / both[:, LANES:]
        o_ref[0, :, cols] = (both[:, :LANES] * inverse).astype(bf16)
        r_ref[0, :, cols] = inverse


def attend(qkv, kept):
    shards, rows, width = qkv.shape
    cols = width // 3
    pairs = cols // LANES
    images = rows // SEQ
    part = lambda which: pl.BlockSpec((1, SEQ, cols), lambda t, i, k: (t, i, which))
    probs = pl.BlockSpec((1, 1, pairs, 2, SEQ, KEYS), lambda t, i, k: (t, i, 0, 0, 0, 0))
    return pl.pallas_call(
        functools.partial(attend_kernel, pairs=pairs),
        grid_spec=pltpu.PrefetchScalarGridSpec(
            num_scalar_prefetch=1,
            grid=(shards, images),
            in_specs=[part(0), part(1), part(2)],
            out_specs=[part(0), probs, part(0)],
        ),
        out_shape=[
            jax.ShapeDtypeStruct((shards, rows, cols), bf16),
            jax.ShapeDtypeStruct((shards, images, pairs, 2, SEQ, KEYS), bf16),
            jax.ShapeDtypeStruct((shards, rows, cols), f32),
        ],
        name="attend",
        cost_estimate=cost(rows * cols * shards * SEQ * 16, qkv, qkv),
        compiler_params=pltpu.CompilerParams(
            dimension_semantics=("arbitrary", "arbitrary"), vmem_limit_bytes=VMEM
        ),
    )(kept, qkv, qkv, qkv)


def attend_back_kernel(q_ref, k_ref, v_ref, g_ref, o_ref, e_ref, r_ref, out_ref, bias_ref, *, pairs):
    width = pairs * LANES

    @pl.when(pl.program_id(1) == 0)
    def _():
        bias_ref[...] = jnp.zeros_like(bias_ref)

    for pair in range(pairs):
        cols = slice(LANES * pair, LANES * (pair + 1))
        query = q_ref[0, :, cols]
        values = pad_keys(v_ref[0, :, cols])
        grad = (g_ref[0, :, cols].astype(f32) * r_ref[0, :, cols]).astype(bf16)
        product = split_heads(grad.astype(f32) * o_ref[0, :, cols].astype(f32))
        grads = []
        for head, grad_head in enumerate(split_heads(grad)):
            inner = jnp.sum(product[head], axis=-1, keepdims=True)
            expo = e_ref[0, 0, pair, head].astype(f32)
            grads.append((expo * (dot_flip(grad_head, values) - inner)).astype(bf16))
        keys = jnp.concatenate(split_heads(pad_keys(k_ref[0, :, cols])), 0)
        grad_query = (dot(jnp.concatenate(grads, 1), keys) * SCALE).astype(bf16)
        query_flip, grad_flip = query.T, grad.T
        halves = [slice(HEAD_DIM * head, HEAD_DIM * (head + 1)) for head in range(2)]
        grad_key = jnp.concatenate([dot(query_flip[half], grads[h]) for h, half in enumerate(halves)], 0)
        grad_value = jnp.concatenate(
            [dot(grad_flip[half], e_ref[0, 0, pair, h]) for h, half in enumerate(halves)], 0
        )
        grad_key = (grad_key.T[:SEQ] * SCALE).astype(bf16)
        grad_value = grad_value.T[:SEQ].astype(bf16)
        for which, value in enumerate((grad_query, grad_key, grad_value)):
            start = which * width + LANES * pair
            out_ref[0, :, start : start + LANES] = value
        bias_ref[0, 0:1, cols] += jnp.sum(grad_query.astype(f32), axis=0, keepdims=True)
        bias_ref[0, 1:2, cols] += jnp.sum(grad_key.astype(f32), axis=0, keepdims=True)
        bias_ref[0, 2:3, cols] += jnp.sum(grad_value.astype(f32), axis=0, keepdims=True)


def attend_back(qkv, grad, attn, expo, inverse):
    shards, rows, width = qkv.shape
    cols = width // 3
    pairs = cols // LANES
    images = rows // SEQ
    part = lambda which: pl.BlockSpec((1, SEQ, cols), lambda t, i: (t, i, which))
    probs = pl.BlockSpec((1, 1, pairs, 2, SEQ, KEYS), lambda t, i: (t, i, 0, 0, 0, 0))
    return pl.pallas_call(
        functools.partial(attend_back_kernel, pairs=pairs),
        grid=(shards, images),
        in_specs=[part(0), part(1), part(2), part(0), part(0), probs, part(0)],
        out_specs=[
            pl.BlockSpec((1, SEQ, width), lambda t, i: (t, i, 0)),
            pl.BlockSpec((1, 3, cols), lambda t, i: (t, 0, 0)),
        ],
        out_shape=[
            jax.ShapeDtypeStruct((shards, rows, width), bf16),
            jax.ShapeDtypeStruct((shards, 3, cols), f32),
        ],
        name="attend_back",
        cost_estimate=cost(rows * cols * shards * SEQ * 24, qkv, qkv, expo),
        compiler_params=pltpu.CompilerParams(
            dimension_semantics=("arbitrary", "arbitrary"), vmem_limit_bytes=VMEM
        ),
    )(qkv, qkv, qkv, grad, attn, expo, inverse)


def norm_parts(values):
    centred = values - jnp.mean(values, axis=-1, keepdims=True)
    inverse = lax.rsqrt(jnp.mean(centred * centred, axis=-1, keepdims=True) + EPSILON)
    return centred * inverse, inverse


def norm_back(grad_normed, normed, inverse):
    first = jnp.mean(grad_normed, axis=-1, keepdims=True)
    second = jnp.mean(grad_normed * normed, axis=-1, keepdims=True)
    return inverse * (grad_normed - first - normed * second)


def block_rows(rows):
    return next(size for size in (512, 320, rows) if rows % size == 0)


def cost(flops, *arrays):
    return pl.CostEstimate(
        flops=flops, transcendentals=0, bytes_accessed=sum(a.size * a.dtype.itemsize for a in arrays)
    )


def call(kernel, name, grid, in_specs, outs, prefetch=0, aliases=None, estimate=None):
    return pl.pallas_call(
        kernel,
        grid_spec=pltpu.PrefetchScalarGridSpec(
            num_scalar_prefetch=prefetch,
            grid=grid,
            in_specs=in_specs,
            out_specs=[pl.BlockSpec(block, index) for block, index, _, _ in outs],
        ),
        out_shape=[jax.ShapeDtypeStruct(shape, kind) for _, _, shape, kind in outs],
        name=name,
        input_output_aliases=aliases or {},
        cost_estimate=estimate,
        compiler_params=pltpu.CompilerParams(
            dimension_semantics=("arbitrary",) * len(grid), vmem_limit_bytes=VMEM
        ),
    )


def fixed(block, *index):
    return pl.BlockSpec(block, lambda *_: index, pipeline_mode=pl.Buffered(1))


GAIN1, GAIN2, SHIFT1, SHIFT2, SHIFT3, SHIFT4 = range(6)


def row(ref, index):
    return ref[index : index + 1, :]


def norm_in_kernel(x_ref, vec_ref, h_ref):
    normed, _ = norm_parts(x_ref[...].astype(f32))
    h_ref[...] = (normed * row(vec_ref, GAIN1) + row(vec_ref, SHIFT1)).astype(bf16)


def norm_in(tokens, vectors):
    rows, width = tokens.shape
    step = pl.BlockSpec((SEQ, width), lambda i: (i, 0))
    return call(
        norm_in_kernel,
        "norm_in",
        (rows // SEQ,),
        [step, fixed(vectors.shape, 0, 0)],
        [((SEQ, width), lambda i: (i, 0), (rows, width), bf16)],
        estimate=cost(16 * rows * width, tokens, tokens),
    )(tokens, vectors)[0]


def project_kernel(h_ref, w_ref, bias_ref, out_ref):
    for shard in range(out_ref.shape[0]):
        out_ref[shard] = (dot(h_ref[...], w_ref[shard]) + bias_ref[shard]).astype(bf16)


def project(h1, weights, bias):
    rows, width = h1.shape
    shards, _, cols = bias.shape
    size = block_rows(rows)
    return call(
        project_kernel,
        "project",
        (rows // size,),
        [
            pl.BlockSpec((size, width), lambda i: (i, 0)),
            fixed((shards, width, cols), 0, 0, 0),
            fixed(bias.shape, 0, 0, 0),
        ],
        [((shards, size, cols), lambda i: (0, i, 0), (shards, rows, cols), bf16)],
        estimate=cost(2 * rows * width * cols * shards, h1, weights),
    )(h1, weights, bias)[0]


def mix_kernel(attn_ref, w_ref, x_ref, vec_ref, mixed_ref, h_ref):
    total = dot_flip(attn_ref[0], w_ref[0])
    for shard in range(1, attn_ref.shape[0]):
        total += dot_flip(attn_ref[shard], w_ref[shard])
    mixed = x_ref[...].astype(f32) + total + row(vec_ref, SHIFT3)
    normed, _ = norm_parts(mixed)
    mixed_ref[...] = mixed
    h_ref[...] = (normed * row(vec_ref, GAIN2) + row(vec_ref, SHIFT2)).astype(bf16)


def mix(attn, weights, tokens, vectors):
    shards, rows, cols = attn.shape
    width = tokens.shape[1]
    size = block_rows(rows)
    step = lambda i: (i, 0)
    return call(
        mix_kernel,
        "mix",
        (rows // size,),
        [
            pl.BlockSpec((shards, size, cols), lambda i: (0, i, 0)),
            fixed(weights.shape, 0, 0, 0),
            pl.BlockSpec((size, width), step),
            fixed(vectors.shape, 0, 0),
        ],
        [
            ((size, width), step, (rows, width), f32),
            ((size, width), step, (rows, width), bf16),
        ],
        estimate=cost(2 * rows * width * cols * shards, attn, tokens),
    )(attn, weights, tokens, vectors)


GELU_IN = 0.7978845608
GELU_CUBE = 0.044715


def gelu_parts(pre):
    cube = (GELU_IN * GELU_CUBE) * (pre * pre)
    half = 0.5 * jnp.tanh(pre * (GELU_IN + cube)) + 0.5
    act = pre * half
    return act, half + (act - act * half) * (2.0 * GELU_IN + 6.0 * cube)


CHUNK = 512


def expand_kernel(h_ref, w_ref, bias_ref, act_ref, slope_ref):
    cols = act_ref.shape[2]
    chunk = min(CHUNK, cols)
    for start in range(0, cols, chunk):
        part = slice(start, start + chunk)
        act, slope = gelu_parts(dot(h_ref[...], w_ref[0, :, part]) + bias_ref[0, :, part])
        act_ref[0, :, part] = act.astype(bf16)
        slope_ref[0, :, part] = slope.astype(bf16)


def expand(h2, weights, bias):
    rows, width = h2.shape
    shards, _, cols = weights.shape
    size = block_rows(rows)
    out = ((1, size, cols), lambda t, i: (t, i, 0), (shards, rows, cols), bf16)
    return call(
        expand_kernel,
        "expand",
        (shards, rows // size),
        [
            pl.BlockSpec((size, width), lambda t, i: (i, 0)),
            pl.BlockSpec((1, width, cols), lambda t, i: (t, 0, 0)),
            pl.BlockSpec((1, 1, cols), lambda t, i: (t, 0, 0)),
        ],
        [out, out],
        estimate=cost(3 * rows * width * cols * shards, h2, weights),
    )(h2, weights, bias)


def expand_back_kernel(g_ref, w_ref, slope_ref, out_ref, bias_ref):
    @pl.when(pl.program_id(1) == 0)
    def _():
        bias_ref[...] = jnp.zeros_like(bias_ref)

    cols = out_ref.shape[2]
    chunk = min(CHUNK, cols)
    for start in range(0, cols, chunk):
        part = slice(start, start + chunk)
        grad = (dot(g_ref[...], w_ref[0, :, part]) * slope_ref[0, :, part].astype(f32)).astype(bf16)
        out_ref[0, :, part] = grad
        bias_ref[0, :, part] += jnp.sum(grad.astype(f32), axis=0, keepdims=True)


def expand_back(grad, weights, slope):
    rows, width = grad.shape
    shards, _, cols = weights.shape
    size = block_rows(rows)
    step = lambda t, i: (t, i, 0)
    return call(
        expand_back_kernel,
        "expand_back",
        (shards, rows // size),
        [
            pl.BlockSpec((size, width), lambda t, i: (i, 0)),
            pl.BlockSpec((1, width, cols), lambda t, i: (t, 0, 0)),
            pl.BlockSpec((1, size, cols), step),
        ],
        [
            ((1, size, cols), step, (shards, rows, cols), bf16),
            ((1, 1, cols), lambda t, i: (t, 0, 0), (shards, 1, cols), f32),
        ],
        estimate=cost(2 * rows * width * cols * shards, slope, slope),
    )(grad, weights, slope)


def dot_rows(left, right):
    return lax.dot_general(left, right, (((0,), (0,)), ((), ())), preferred_element_type=f32)


def weight_grad_kernel(left_ref, right_ref, out_ref, *, chunk, fill):
    which = pl.program_id(1)
    start = pl.multiple_of(which * chunk, chunk)
    out_ref[0, :, pl.ds(start, chunk)] = dot_rows(left_ref[...], right_ref[0]).astype(bf16)
    if fill:

        @pl.when(which == 0)
        def _():
            spare = jnp.zeros((out_ref.shape[1], fill), bf16)
            out_ref[0, :, out_ref.shape[2] - fill :] = spare


def weight_grad(left, right, spare):
    rows, width = left.shape
    shards, _, used = right.shape
    chunk = min(512, used)
    block = (1, width, used + spare)
    return call(
        functools.partial(weight_grad_kernel, chunk=chunk, fill=spare),
        "weight_grad",
        (shards, used // chunk),
        [
            fixed((rows, width), 0, 0),
            pl.BlockSpec((1, rows, chunk), lambda t, n: (t, 0, n)),
        ],
        [(block, lambda t, n: (t, 0, 0), (shards,) + block[1:], bf16)],
        estimate=cost(2 * rows * width * used * shards, left, right),
    )(left, right)[0]


def weight_grad_split_kernel(slot_ref, left_ref, right_ref, *refs, per_chain, chains):
    which, shard = pl.program_id(0), pl.program_id(1)
    grad = dot_rows(left_ref[...], right_ref[0])
    if len(refs) > 2 * chains:
        w_ref, total_ref, product_ref, sum_ref = refs[0], refs[1], refs[-2], refs[-1]

        @pl.when((which == 0) & (shard == 0))
        def _():
            product_ref[...] = jnp.zeros_like(product_ref)
            sum_ref[...] = jnp.zeros_like(sum_ref)

        for start in range(0, grad.shape[1], LANES):
            part = slice(start, start + LANES)
            weights = w_ref[0, :, part].astype(f32)
            product_ref[...] += weights * grad[:, part]
            sum_ref[...] += weights * total_ref[0, :, part]
        refs = refs[2:-2]
    grad = grad.astype(bf16)
    pairs = grad.shape[0] // (2 * refs[0].shape[1])
    second = slot_ref[slot_ref.shape[0] - 1] == 1
    for chain in range(chains):

        @pl.when(which // per_chain == chain)
        def _():
            near_ref, far_ref = refs[2 * chain : 2 * chain + 2]
            part = near_ref.shape[1]
            base = chain * near_ref.shape[0] + shard * pairs
            for pair in range(pairs):
                slot = slot_ref[base + pair]
                low = grad[2 * pair * part : (2 * pair + 1) * part]
                high = grad[(2 * pair + 1) * part : (2 * pair + 2) * part]
                near_ref[slot] = jnp.where(second, high, low)
                far_ref[slot] = jnp.where(second, low, high)


def weight_grad_split(left, right, tables, second, weights=None, total=None):
    rows, width = left.shape
    shards, _, cols = right.shape
    chains = len(tables)
    share = cols // chains
    half = tables[0].shape[0]
    part = width // (2 * half // shards)
    chunk = share if share <= 1024 else 512
    per_chain = share // chunk
    out = lambda chain: (
        (half, part, chunk),
        lambda n, t, s: (0, 0, jnp.clip(n - chain * per_chain, 0, per_chain - 1)),
        (half, part, share),
        bf16,
    )
    outs = [out(chain) for chain in range(chains) for _ in range(2)]
    more_specs, more = [], []
    if weights is not None:
        more = [weights, total]
        more_specs = [
            pl.BlockSpec((1, width, chunk), lambda n, t, s: (t, 0, n)),
            pl.BlockSpec((1, 1, chunk), lambda n, t, s: (t, 0, n)),
        ]
        outs = outs + [((width, LANES), lambda n, t, s: (0, 0), (width, LANES), f32)] * 2
    parts = call(
        functools.partial(weight_grad_split_kernel, per_chain=per_chain, chains=chains),
        "weight_grad_split",
        (chains * per_chain, shards),
        [
            fixed((rows, width), 0, 0),
            pl.BlockSpec((1, rows, chunk), lambda n, t, s: (t, 0, n)),
        ]
        + more_specs,
        outs,
        prefetch=1,
        estimate=cost(2 * rows * width * cols * shards, left, right),
    )(jnp.concatenate(list(tables) + [second[None]]), left, right, *more)
    return [(parts[2 * chain], parts[2 * chain + 1]) for chain in range(chains)], parts[2 * chains :]


def middle_back_kernel(
    g_ref, up_ref, mixed_ref, gm_ref, vec_ref, out_w_ref, gmixed_ref, go_ref, gattn_ref, sums_ref
):
    @pl.when(pl.program_id(0) == 0)
    def _():
        sums_ref[...] = jnp.zeros_like(sums_ref)

    grad_h = dot_flip(g_ref[0], up_ref[0])
    for shard in range(1, g_ref.shape[0]):
        grad_h += dot_flip(g_ref[shard], up_ref[shard])
    normed, inverse = norm_parts(mixed_ref[...])
    grad = gm_ref[...].astype(f32)
    grad_mixed = grad + norm_back(grad_h * row(vec_ref, GAIN2), normed, inverse)
    gmixed_ref[...] = grad_mixed
    rounded = grad_mixed.astype(bf16)
    go_ref[...] = rounded
    for index, value in ((1, grad_h * normed), (3, grad_h), (4, grad_mixed), (5, grad)):
        sums_ref[index : index + 1, :] += jnp.sum(value, axis=0, keepdims=True)
    for shard in range(gattn_ref.shape[0]):
        gattn_ref[shard] = dot(rounded, out_w_ref[shard]).astype(bf16)


def middle_back(grad_pre, up, mixed, grad_m, vectors, weights):
    shards, rows, cols = grad_pre.shape
    width = mixed.shape[1]
    heads = weights.shape[2]
    step = lambda i: (i, 0)
    wide = pl.BlockSpec((SEQ, width), step)
    return call(
        middle_back_kernel,
        "middle_back",
        (rows // SEQ,),
        [
            pl.BlockSpec((shards, SEQ, cols), lambda i: (0, i, 0)),
            fixed(up.shape, 0, 0, 0),
            wide,
            wide,
            fixed(vectors.shape, 0, 0),
            fixed(weights.shape, 0, 0, 0),
        ],
        [
            ((SEQ, width), step, (rows, width), f32),
            ((SEQ, width), step, (rows, width), bf16),
            ((shards, SEQ, heads), lambda i: (0, i, 0), (shards, rows, heads), bf16),
            ((8, width), lambda i: (0, 0), (8, width), f32),
        ],
        estimate=cost(2 * rows * width * (cols + heads) * shards, grad_pre, up, mixed),
    )(grad_pre, up, mixed, grad_m, vectors, weights)


def input_back_kernel(g_ref, w_ref, x_ref, gmixed_ref, vec_ref, *refs):
    out_ref = refs[-1]
    grad_h = dot_flip(g_ref[0], w_ref[0])
    for shard in range(1, g_ref.shape[0]):
        grad_h += dot_flip(g_ref[shard], w_ref[shard])
    normed, inverse = norm_parts(x_ref[...].astype(f32))
    out_ref[...] = gmixed_ref[...] + norm_back(grad_h * row(vec_ref, GAIN1), normed, inverse)


def input_back(first, count, grad_heads, weights, tokens, grad_mixed, vectors, *out):
    shards, rows, cols = grad_heads.shape
    width = tokens.shape[1]
    step = lambda i: (first + i, 0)
    wide = pl.BlockSpec((SEQ, width), step)
    return call(
        input_back_kernel,
        "input_back",
        (count,),
        [
            pl.BlockSpec((shards, SEQ, cols), lambda i: (0, first + i, 0)),
            fixed(weights.shape, 0, 0, 0),
            wide,
            wide,
            fixed(vectors.shape, 0, 0),
        ]
        + [pl.BlockSpec(memory_space=pl.ANY)] * len(out),
        [((SEQ, width), step, (rows, width), f32)],
        aliases={5: 0} if out else None,
        estimate=cost(2 * count * SEQ * width * cols * shards, weights),
    )(grad_heads, weights, tokens, grad_mixed, vectors, *out)[0]


def shrink_kernel(kept_ref, act_ref, w_ref, mixed_ref, vec_ref, *refs, first):
    out_ref = refs[-1]
    total = dot_flip(act_ref[0], w_ref[0])
    for shard in range(1, act_ref.shape[0]):
        total += dot_flip(act_ref[shard], w_ref[shard])
    valid = BUFFER + kept_ref[first + pl.program_id(0)]
    alive = lax.broadcasted_iota(jnp.int32, (SEQ, 1), 0) < valid
    result = mixed_ref[...] + total + row(vec_ref, SHIFT4)
    out_ref[...] = jnp.where(alive, result, 0.0).astype(bf16)


def shrink(first, count, kept, act, weights, mixed, vectors, *out):
    shards, rows, cols = act.shape
    width = mixed.shape[1]
    step = lambda i, k: (first + i, 0)
    return call(
        functools.partial(shrink_kernel, first=first),
        "shrink",
        (count,),
        [
            pl.BlockSpec((shards, SEQ, cols), lambda i, k: (0, first + i, 0)),
            fixed(weights.shape, 0, 0, 0),
            pl.BlockSpec((SEQ, width), step),
            fixed(vectors.shape, 0, 0),
        ]
        + [pl.BlockSpec(memory_space=pl.ANY)] * len(out),
        [((SEQ, width), step, (rows, width), bf16)],
        prefetch=1,
        aliases={5: 0} if out else None,
        estimate=cost(2 * count * SEQ * width * cols * shards, weights),
    )(kept, act, weights, mixed, vectors, *out)[0]


def swap(values, axis, bit):
    places = range(lax.axis_size(axis))
    return lax.ppermute(values, axis, [(place, place ^ bit) for place in places])


def bits_of(axis):
    return [1 << power for power in range(lax.axis_size(axis).bit_length() - 1)]


def flip_gather(part, order):
    dp, shards = lax.axis_size("dp"), lax.axis_size("tensor")
    values = part[None]
    index = jnp.arange(shards * dp, dtype=jnp.int32)
    apart = {
        "tensor": (index // dp) ^ lax.axis_index("tensor").astype(jnp.int32),
        "dp": (index % dp) ^ lax.axis_index("dp").astype(jnp.int32),
    }
    place = jnp.zeros_like(index)
    for axis, bit in order:
        place += jnp.where((apart[axis] & bit) != 0, values.shape[0], 0)
        values = jnp.concatenate([values, swap(values, axis, bit)], 0)
    return jnp.take(values, place, axis=0)


def slot_table(order):
    dp, shards = lax.axis_size("dp"), lax.axis_size("tensor")
    index = jnp.arange(shards * dp // 2, dtype=jnp.int32)
    apart = {
        "tensor": (index // (dp // 2)) ^ lax.axis_index("tensor").astype(jnp.int32),
        "dp": (2 * (index % (dp // 2))) ^ lax.axis_index("dp").astype(jnp.int32),
    }
    slot = jnp.zeros_like(index)
    for depth, (axis, bit) in enumerate(order[1:]):
        slot += jnp.where((apart[axis] & bit) != 0, 1 << (len(order) - 2 - depth), 0)
    return slot


class Chain:
    def __init__(self, near, far, order):
        self.near, self.order = near, list(order)
        self.far = swap(far, *self.order.pop(0))

    def send(self):
        half = self.values.shape[0] // 2
        self.near = self.values[:half]
        self.far = swap(self.values[half:], *self.order.pop(0))

    def settle(self):
        self.values = self.near + self.far

    def finish(self):
        self.settle()
        while self.order:
            self.send()
            self.settle()
        return self.values[0]


class Sum(Chain):
    def __init__(self, values, order):
        self.values, self.order = values, list(order)
        self.send()

    def send(self):
        self.near = self.values
        self.far = swap(self.values, *self.order.pop(0))

    def finish(self):
        super().finish()
        return self.values


def meet(values, *chains):
    values, far = lax.optimization_barrier((values, [chain.far for chain in chains]))
    for chain, arrived in zip(chains, far):
        chain.far = arrived
        chain.settle()
        if chain.order:
            chain.send()
    return values


def gather(part):
    full = lax.all_gather(part, ("tensor", "dp"), axis=0, tiled=True)
    return full.reshape(lax.axis_size("tensor"), -1, part.shape[1])


def scatter(full):
    flat = full.reshape(-1, full.shape[2])
    return lax.psum_scatter(flat, ("tensor", "dp"), scatter_dimension=0, tiled=True)


def body(tokens, kept, cotangent, w_qkv, w_out, w_up, w_down, qv_bias, up_bias, ln_gain, shift):
    rows, width = tokens.shape
    dp, shards = lax.axis_size("dp"), lax.axis_size("tensor")
    images = rows // SEQ
    part = w_qkv.shape[1]
    cols = w_qkv.shape[2]
    own = ln_gain.shape[1]
    barrier = lax.optimization_barrier

    core, along_x = [("dp", 1)], [("tensor", bit) for bit in bits_of("tensor")[::-1]]
    low, high = [("dp", 2)], [("dp", bit) for bit in bits_of("dp")[::-1] if bit > 2]
    order_x, order_low = core + along_x + low + high, core + low + along_x + high

    full_qkv = gather(w_qkv.transpose(1, 0, 2).reshape(part, 3 * cols))
    full_up = gather(w_up)
    full_down = gather(w_down.T)

    small = jnp.concatenate(
        [ln_gain, shift, qv_bias.astype(f32), up_bias.astype(f32).reshape(-1, own)], 0
    )
    small = flip_gather(small, high + low + along_x + core)
    small = small.reshape((shards, dp) + small.shape[1:])
    vectors = small[:, :, :6].transpose(2, 1, 0, 3).reshape(6, width)
    vectors = jnp.concatenate([vectors, jnp.zeros((2, width), f32)], 0)
    bias_qv = small[:, :, 6:8].transpose(0, 2, 1, 3).reshape(shards, 2, cols)
    bias_up = small[:, :, 8:].reshape(shards, 1, -1)
    bias_heads = jnp.concatenate([bias_qv[:, :1], jnp.zeros_like(bias_qv[:, :1]), bias_qv[:, 1:]], 2)
    full_out = flip_gather(w_out.T, high + low + along_x + core).reshape(shards, width, cols)

    first_image = lax.axis_index("tensor") * images
    kept_own = lax.dynamic_slice_in_dim(kept, first_image, images, 0)
    positions = jnp.arange(SEQ, dtype=jnp.int32)
    alive = (positions[None, :] < BUFFER + kept_own[:, None]).reshape(rows, 1)
    grad_m = jnp.where(alive, cotangent, jnp.zeros_like(cotangent))

    tables = [slot_table(order_x), slot_table(order_low)]
    second = lax.axis_index("dp").astype(jnp.int32) & 1

    h1 = norm_in(tokens, vectors)
    qkv = project(h1, full_qkv, bias_heads)
    attn, expo, inverse_sum = attend(qkv, kept_own)
    mixed, h2 = mix(attn, full_out, tokens, vectors)
    act, slope = expand(h2, full_up, bias_up)

    hidden = act.shape[2]
    grad_down = weight_grad(grad_m, act, hidden // 8)
    grad_m, grad_down = barrier((grad_m, grad_down))
    sent_down = scatter(grad_down)[:, :hidden]
    grad_pre, grad_bias_up = expand_back(grad_m, full_down, slope)
    ((near, far),), _ = weight_grad_split(h2, grad_pre, tables[:1], second)
    grad_pre, near, far = barrier((grad_pre, near, far))
    chain_up = Chain(near, far, order_x)
    grad_mixed, grad_o, grad_attn, sums2 = middle_back(
        grad_pre, full_up, mixed, grad_m, vectors, full_out
    )
    grad_o = meet(grad_o, chain_up)
    grad_out = weight_grad(grad_o, attn, cols // 2)
    grad_attn, grad_out = barrier((grad_attn, grad_out))
    grad_heads, totals = attend_back(qkv, grad_attn, attn, expo, inverse_sum)
    grad_heads = meet(grad_heads, chain_up)
    grad_heads, sent_down, grad_out = barrier((grad_heads, sent_down, grad_out))
    sent_out = scatter(grad_out)[:, :cols]

    chains = 2 if (3 * cols // 2) % LANES == 0 else 1
    halves, (product, total) = weight_grad_split(
        h1, grad_heads, tables[:chains], second, full_qkv, totals.reshape(shards, 1, 3 * cols)
    )
    grad_heads, halves, product, total = barrier((grad_heads, halves, product, total))
    chains_qkv = [Chain(*half, order) for half, order in zip(halves, (order_x, order_low))]
    grad_heads = meet(grad_heads, chain_up)
    total = jnp.sum(total, axis=-1)
    product = (jnp.sum(product, axis=-1) - vectors[SHIFT1] * total) / vectors[GAIN1]
    sums = jnp.concatenate(
        [
            jnp.stack([product, sums2[1], total, sums2[3], sums2[4], sums2[5]]),
            totals[:, 0].reshape(1, width),
            totals[:, 2].reshape(1, width),
            grad_bias_up.reshape(-1, width),
        ],
        0,
    )
    chain_small = Sum(sums, order_x)
    first = images // 2
    grad_tokens = input_back(0, first, grad_heads, full_qkv, tokens, grad_mixed, vectors)
    grad_tokens = meet(grad_tokens, chain_small, *chains_qkv)
    grad_tokens = input_back(
        first, images - first, grad_heads, full_qkv, tokens, grad_mixed, vectors, grad_tokens
    )
    act, grad_tokens = meet((act, grad_tokens), chain_up, chain_small, *chains_qkv)
    layer_out = shrink(0, first, kept_own, act, full_down, mixed, vectors)
    layer_out = meet(layer_out, chain_up, chain_small, *chains_qkv)
    layer_out = shrink(first, images - first, kept_own, act, full_down, mixed, vectors, layer_out)
    layer_out = meet(layer_out, chain_small, *chains_qkv)
    sent_up = chain_up.finish()
    sent_qkv = jnp.concatenate([chain.finish() for chain in chains_qkv], 1)
    small = chain_small.finish()
    at_dp, at_tensor = lax.axis_index("dp"), lax.axis_index("tensor")
    row_place, shard_place = at_dp * shards + at_tensor, at_tensor * dp + at_dp
    rows_own = lax.dynamic_slice(small, (0, row_place * own), (6, own))
    heads_own = lax.dynamic_slice(small, (6, shard_place * own), (2, own))
    count = up_bias.shape[0]
    start = shard_place * count
    up_own = lax.dynamic_slice(small, (8 + start // width, start % width), (1, count))

    return (
        layer_out,
        grad_tokens,
        sent_qkv.astype(f32).reshape(part, 3, cols).transpose(1, 0, 2),
        sent_out.astype(f32).T,
        sent_up.astype(f32),
        sent_down.astype(f32).T,
        heads_own,
        up_own.reshape(-1),
        rows_own[:2],
        rows_own[2:],
    )


def solution(mesh):
    both = P(("dp", "tensor"), None)
    matrices = (
        P(None, "dp", "tensor"),
        P("tensor", "dp"),
        P("dp", "tensor"),
        P("tensor", "dp"),
        P(None, ("tensor", "dp")),
        P(("tensor", "dp")),
        P(None, ("dp", "tensor")),
        P(None, ("dp", "tensor")),
    )
    return jax.shard_map(
        body,
        mesh=mesh,
        in_specs=(both, P("dp"), both) + matrices,
        out_specs=(both, both) + matrices,
        check_vma=False,
    )
```

```python
import functools

import jax
import jax.numpy as jnp
from jax import lax
from jax.experimental import pallas as pl
from jax.experimental.pallas import tpu as pltpu
from jax.sharding import PartitionSpec as P

HEAD_DIM = 64
BUFFER = 64
SEQ = 320
KEYS = 384
LANES = 128
EPSILON = 1e-06
SCALE = HEAD_DIM ** (-0.5)
LOG2E = 1.4426950408889634
NEGATIVE = -1000000000.0 / SCALE
VMEM = 56 << 20


f32 = jnp.float32
bf16 = jnp.bfloat16


def dot(left, right):
    return lax.dot_general(left, right, (((1,), (0,)), ((), ())), preferred_element_type=f32)


def dot_flip(left, right):
    return lax.dot_general(left, right, (((1,), (1,)), ((), ())), preferred_element_type=f32)


def split_heads(values):
    low = lax.broadcasted_iota(jnp.int32, (1, LANES), 1) < HEAD_DIM
    zero = jnp.zeros_like(values)
    return jnp.where(low, values, zero), jnp.where(low, zero, values)


def pad_keys(values):
    return jnp.concatenate([values, jnp.zeros((KEYS - SEQ, values.shape[1]), values.dtype)], 0)


def attend_kernel(kept_ref, q_ref, k_ref, v_ref, o_ref, e_ref, r_ref, *, pairs):
    valid = BUFFER + kept_ref[pl.program_id(1)]
    alive = lax.broadcasted_iota(jnp.int32, (1, KEYS), 1) < valid
    ones = split_heads(jnp.ones((KEYS, LANES), bf16))
    for pair in range(pairs):
        cols = slice(LANES * pair, LANES * (pair + 1))
        keys = pad_keys(k_ref[0, :, cols])
        values = split_heads(pad_keys(v_ref[0, :, cols]))
        expos = []
        for head, query in enumerate(split_heads(q_ref[0, :, cols])):
            scores = jnp.where(alive, dot_flip(query, keys), NEGATIVE)
            highest = jnp.max(scores, axis=-1, keepdims=True)
            expo = jnp.exp2((scores - highest) * (SCALE * LOG2E)).astype(bf16)
            e_ref[0, 0, pair, head] = expo
            expos.append(expo)
        right = jnp.concatenate(
            [jnp.concatenate([value, one], 1) for value, one in zip(values, ones)], 0
        )
        both = dot(jnp.concatenate(expos, 1), right)
        inverse = 1.0 / both[:, LANES:]
        o_ref[0, :, cols] = (both[:, :LANES] * inverse).astype(bf16)
        r_ref[0, :, cols] = inverse


def attend(qkv, kept):
    shards, rows, width = qkv.shape
    cols = width // 3
    pairs = cols // LANES
    images = rows // SEQ
    part = lambda which: pl.BlockSpec((1, SEQ, cols), lambda t, i, k: (t, i, which))
    probs = pl.BlockSpec((1, 1, pairs, 2, SEQ, KEYS), lambda t, i, k: (t, i, 0, 0, 0, 0))
    return pl.pallas_call(
        functools.partial(attend_kernel, pairs=pairs),
        grid_spec=pltpu.PrefetchScalarGridSpec(
            num_scalar_prefetch=1,
            grid=(shards, images),
            in_specs=[part(0), part(1), part(2)],
            out_specs=[part(0), probs, part(0)],
        ),
        out_shape=[
            jax.ShapeDtypeStruct((shards, rows, cols), bf16),
            jax.ShapeDtypeStruct((shards, images, pairs, 2, SEQ, KEYS), bf16),
            jax.ShapeDtypeStruct((shards, rows, cols), f32),
        ],
        name="attend",
        cost_estimate=cost(rows * cols * shards * SEQ * 16, qkv, qkv),
        compiler_params=pltpu.CompilerParams(
            dimension_semantics=("arbitrary", "arbitrary"), vmem_limit_bytes=VMEM
        ),
    )(kept, qkv, qkv, qkv)


def attend_back_kernel(q_ref, k_ref, v_ref, g_ref, o_ref, e_ref, r_ref, out_ref, bias_ref, *, pairs):
    width = pairs * LANES

    @pl.when(pl.program_id(1) == 0)
    def _():
        bias_ref[...] = jnp.zeros_like(bias_ref)

    for pair in range(pairs):
        cols = slice(LANES * pair, LANES * (pair + 1))
        query = q_ref[0, :, cols]
        values = pad_keys(v_ref[0, :, cols])
        grad = (g_ref[0, :, cols].astype(f32) * r_ref[0, :, cols]).astype(bf16)
        product = split_heads(grad.astype(f32) * o_ref[0, :, cols].astype(f32))
        grads = []
        for head, grad_head in enumerate(split_heads(grad)):
            inner = jnp.sum(product[head], axis=-1, keepdims=True)
            expo = e_ref[0, 0, pair, head].astype(f32)
            grads.append((expo * (dot_flip(grad_head, values) - inner)).astype(bf16))
        keys = jnp.concatenate(split_heads(pad_keys(k_ref[0, :, cols])), 0)
        grad_query = (dot(jnp.concatenate(grads, 1), keys) * SCALE).astype(bf16)
        query_flip, grad_flip = query.T, grad.T
        halves = [slice(HEAD_DIM * head, HEAD_DIM * (head + 1)) for head in range(2)]
        grad_key = jnp.concatenate([dot(query_flip[half], grads[h]) for h, half in enumerate(halves)], 0)
        grad_value = jnp.concatenate(
            [dot(grad_flip[half], e_ref[0, 0, pair, h]) for h, half in enumerate(halves)], 0
        )
        grad_key = (grad_key.T[:SEQ] * SCALE).astype(bf16)
        grad_value = grad_value.T[:SEQ].astype(bf16)
        for which, value in enumerate((grad_query, grad_key, grad_value)):
            start = which * width + LANES * pair
            out_ref[0, :, start : start + LANES] = value
        bias_ref[0, 0:1, cols] += jnp.sum(grad_query.astype(f32), axis=0, keepdims=True)
        bias_ref[0, 1:2, cols] += jnp.sum(grad_value.astype(f32), axis=0, keepdims=True)


def attend_back(qkv, grad, attn, expo, inverse):
    shards, rows, width = qkv.shape
    cols = width // 3
    pairs = cols // LANES
    images = rows // SEQ
    part = lambda which: pl.BlockSpec((1, SEQ, cols), lambda t, i: (t, i, which))
    probs = pl.BlockSpec((1, 1, pairs, 2, SEQ, KEYS), lambda t, i: (t, i, 0, 0, 0, 0))
    return pl.pallas_call(
        functools.partial(attend_back_kernel, pairs=pairs),
        grid=(shards, images),
        in_specs=[part(0), part(1), part(2), part(0), part(0), probs, part(0)],
        out_specs=[
            pl.BlockSpec((1, SEQ, width), lambda t, i: (t, i, 0)),
            pl.BlockSpec((1, 2, cols), lambda t, i: (t, 0, 0)),
        ],
        out_shape=[
            jax.ShapeDtypeStruct((shards, rows, width), bf16),
            jax.ShapeDtypeStruct((shards, 2, cols), f32),
        ],
        name="attend_back",
        cost_estimate=cost(rows * cols * shards * SEQ * 24, qkv, qkv, expo),
        compiler_params=pltpu.CompilerParams(
            dimension_semantics=("arbitrary", "arbitrary"), vmem_limit_bytes=VMEM
        ),
    )(qkv, qkv, qkv, grad, attn, expo, inverse)


def norm_parts(values):
    centred = values - jnp.mean(values, axis=-1, keepdims=True)
    inverse = lax.rsqrt(jnp.mean(centred * centred, axis=-1, keepdims=True) + EPSILON)
    return centred * inverse, inverse


def norm_back(grad_normed, normed, inverse):
    first = jnp.mean(grad_normed, axis=-1, keepdims=True)
    second = jnp.mean(grad_normed * normed, axis=-1, keepdims=True)
    return inverse * (grad_normed - first - normed * second)


def block_rows(rows):
    return next(size for size in (512, 320, rows) if rows % size == 0)


def cost(flops, *arrays):
    return pl.CostEstimate(
        flops=flops, transcendentals=0, bytes_accessed=sum(a.size * a.dtype.itemsize for a in arrays)
    )


def call(kernel, name, grid, in_specs, outs, prefetch=0, aliases=None, estimate=None):
    return pl.pallas_call(
        kernel,
        grid_spec=pltpu.PrefetchScalarGridSpec(
            num_scalar_prefetch=prefetch,
            grid=grid,
            in_specs=in_specs,
            out_specs=[pl.BlockSpec(block, index) for block, index, _, _ in outs],
        ),
        out_shape=[jax.ShapeDtypeStruct(shape, kind) for _, _, shape, kind in outs],
        name=name,
        input_output_aliases=aliases or {},
        cost_estimate=estimate,
        compiler_params=pltpu.CompilerParams(
            dimension_semantics=("arbitrary",) * len(grid), vmem_limit_bytes=VMEM
        ),
    )


def fixed(block, *index):
    return pl.BlockSpec(block, lambda *_: index, pipeline_mode=pl.Buffered(1))


GAIN1, GAIN2, SHIFT1, SHIFT2, SHIFT3, SHIFT4 = range(6)


def row(ref, index):
    return ref[index : index + 1, :]


def norm_in_kernel(x_ref, vec_ref, h_ref):
    normed, _ = norm_parts(x_ref[...].astype(f32))
    h_ref[...] = (normed * row(vec_ref, GAIN1) + row(vec_ref, SHIFT1)).astype(bf16)


def norm_in(tokens, vectors):
    rows, width = tokens.shape
    step = pl.BlockSpec((SEQ, width), lambda i: (i, 0))
    return call(
        norm_in_kernel,
        "norm_in",
        (rows // SEQ,),
        [step, fixed(vectors.shape, 0, 0)],
        [((SEQ, width), lambda i: (i, 0), (rows, width), bf16)],
        estimate=cost(16 * rows * width, tokens, tokens),
    )(tokens, vectors)[0]


def project_kernel(h_ref, w_ref, bias_ref, out_ref):
    for shard in range(out_ref.shape[0]):
        out_ref[shard] = (dot(h_ref[...], w_ref[shard]) + bias_ref[shard]).astype(bf16)


def project(h1, weights, bias):
    rows, width = h1.shape
    shards, _, cols = bias.shape
    size = block_rows(rows)
    return call(
        project_kernel,
        "project",
        (rows // size,),
        [
            pl.BlockSpec((size, width), lambda i: (i, 0)),
            fixed((shards, width, cols), 0, 0, 0),
            fixed(bias.shape, 0, 0, 0),
        ],
        [((shards, size, cols), lambda i: (0, i, 0), (shards, rows, cols), bf16)],
        estimate=cost(2 * rows * width * cols * shards, h1, weights),
    )(h1, weights, bias)[0]


def mix_kernel(attn_ref, w_ref, x_ref, vec_ref, mixed_ref, h_ref):
    total = dot_flip(attn_ref[0], w_ref[0])
    for shard in range(1, attn_ref.shape[0]):
        total += dot_flip(attn_ref[shard], w_ref[shard])
    mixed = x_ref[...].astype(f32) + total + row(vec_ref, SHIFT3)
    normed, _ = norm_parts(mixed)
    mixed_ref[...] = mixed
    h_ref[...] = (normed * row(vec_ref, GAIN2) + row(vec_ref, SHIFT2)).astype(bf16)


def mix(attn, weights, tokens, vectors):
    shards, rows, cols = attn.shape
    width = tokens.shape[1]
    size = block_rows(rows)
    step = lambda i: (i, 0)
    return call(
        mix_kernel,
        "mix",
        (rows // size,),
        [
            pl.BlockSpec((shards, size, cols), lambda i: (0, i, 0)),
            fixed(weights.shape, 0, 0, 0),
            pl.BlockSpec((size, width), step),
            fixed(vectors.shape, 0, 0),
        ],
        [
            ((size, width), step, (rows, width), f32),
            ((size, width), step, (rows, width), bf16),
        ],
        estimate=cost(2 * rows * width * cols * shards, attn, tokens),
    )(attn, weights, tokens, vectors)


GELU_IN = 0.7978845608
GELU_CUBE = 0.044715


def gelu_parts(pre):
    cube = (GELU_IN * GELU_CUBE) * (pre * pre)
    half = 0.5 * jnp.tanh(pre * (GELU_IN + cube)) + 0.5
    act = pre * half
    return act, half + (act - act * half) * (2.0 * GELU_IN + 6.0 * cube)


CHUNK = 512


def expand_kernel(h_ref, w_ref, bias_ref, act_ref, slope_ref):
    cols = act_ref.shape[2]
    chunk = min(CHUNK, cols)
    for start in range(0, cols, chunk):
        part = slice(start, start + chunk)
        act, slope = gelu_parts(dot(h_ref[...], w_ref[0, :, part]) + bias_ref[0, :, part])
        act_ref[0, :, part] = act.astype(bf16)
        slope_ref[0, :, part] = slope.astype(bf16)


def expand(h2, weights, bias):
    rows, width = h2.shape
    shards, _, cols = weights.shape
    size = block_rows(rows)
    out = ((1, size, cols), lambda t, i: (t, i, 0), (shards, rows, cols), bf16)
    return call(
        expand_kernel,
        "expand",
        (shards, rows // size),
        [
            pl.BlockSpec((size, width), lambda t, i: (i, 0)),
            pl.BlockSpec((1, width, cols), lambda t, i: (t, 0, 0)),
            pl.BlockSpec((1, 1, cols), lambda t, i: (t, 0, 0)),
        ],
        [out, out],
        estimate=cost(3 * rows * width * cols * shards, h2, weights),
    )(h2, weights, bias)


def expand_back_kernel(g_ref, w_ref, slope_ref, out_ref, bias_ref):
    @pl.when(pl.program_id(1) == 0)
    def _():
        bias_ref[...] = jnp.zeros_like(bias_ref)

    cols = out_ref.shape[2]
    chunk = min(CHUNK, cols)
    for start in range(0, cols, chunk):
        part = slice(start, start + chunk)
        grad = (dot(g_ref[...], w_ref[0, :, part]) * slope_ref[0, :, part].astype(f32)).astype(bf16)
        out_ref[0, :, part] = grad
        bias_ref[0, :, part] += jnp.sum(grad.astype(f32), axis=0, keepdims=True)


def expand_back(grad, weights, slope):
    rows, width = grad.shape
    shards, _, cols = weights.shape
    size = block_rows(rows)
    step = lambda t, i: (t, i, 0)
    return call(
        expand_back_kernel,
        "expand_back",
        (shards, rows // size),
        [
            pl.BlockSpec((size, width), lambda t, i: (i, 0)),
            pl.BlockSpec((1, width, cols), lambda t, i: (t, 0, 0)),
            pl.BlockSpec((1, size, cols), step),
        ],
        [
            ((1, size, cols), step, (shards, rows, cols), bf16),
            ((1, 1, cols), lambda t, i: (t, 0, 0), (shards, 1, cols), f32),
        ],
        estimate=cost(2 * rows * width * cols * shards, slope, slope),
    )(grad, weights, slope)


def dot_rows(left, right):
    return lax.dot_general(left, right, (((0,), (0,)), ((), ())), preferred_element_type=f32)


def weight_grad_kernel(left_ref, right_ref, out_ref, *, chunk, fill):
    which = pl.program_id(1)
    start = pl.multiple_of(which * chunk, chunk)
    out_ref[0, :, pl.ds(start, chunk)] = dot_rows(left_ref[...], right_ref[0]).astype(bf16)
    if fill:

        @pl.when(which == 0)
        def _():
            spare = jnp.zeros((out_ref.shape[1], fill), bf16)
            out_ref[0, :, out_ref.shape[2] - fill :] = spare


def weight_grad(left, right, used, spare, fill):
    rows, width = left.shape
    shards = right.shape[0]
    chunk = min(512, used)
    block = (1, width, used + spare)
    return call(
        functools.partial(weight_grad_kernel, chunk=chunk, fill=spare if fill else 0),
        "weight_grad",
        (shards, used // chunk),
        [
            fixed((rows, width), 0, 0),
            pl.BlockSpec((1, rows, chunk), lambda t, n: (t, 0, n)),
        ],
        [(block, lambda t, n: (t, 0, 0), (shards,) + block[1:], bf16)],
        estimate=cost(2 * rows * width * used * shards, left, right),
    )(left, right)[0]


def weight_grad_into_kernel(left_ref, right_ref, _, out_ref):
    out_ref[0] = dot_rows(left_ref[...], right_ref[0]).astype(bf16)


def weight_grad_into(left, right, out):
    rows, width = left.shape
    shards, _, cols = right.shape
    place = out.shape[2] // cols - 1
    return call(
        weight_grad_into_kernel,
        "weight_grad_into",
        (shards,),
        [
            fixed((rows, width), 0, 0),
            pl.BlockSpec((1, rows, cols), lambda t: (t, 0, 0)),
            pl.BlockSpec(memory_space=pl.ANY),
        ],
        [((1, width, cols), lambda t: (t, 0, place), out.shape, bf16)],
        aliases={2: 0},
        estimate=cost(2 * rows * width * cols * shards, left, right),
    )(left, right, out)[0]


def weight_grad_slots_kernel(slot_ref, left_ref, right_ref, out_ref, *, owners):
    grad = dot_rows(left_ref[...], right_ref[0]).astype(bf16)
    part = out_ref.shape[1]
    for owner in range(owners):
        slot = slot_ref[pl.program_id(1) * owners + owner]
        out_ref[slot] = grad[owner * part : (owner + 1) * part]


def weight_grad_slots(left, right, which, shares, slots):
    rows, width = left.shape
    shards, _, cols = right.shape
    share = cols // shares
    count = slots.shape[0]
    owners = count // shards
    part = width // owners
    chunk = share if share <= 1024 else 512
    first = which * share // chunk
    return call(
        functools.partial(weight_grad_slots_kernel, owners=owners),
        "weight_grad_slots",
        (share // chunk, shards),
        [
            fixed((rows, width), 0, 0),
            pl.BlockSpec((1, rows, chunk), lambda n, t, s: (t, 0, first + n)),
        ],
        [((count, part, chunk), lambda n, t, s: (0, 0, n), (count, part, share), bf16)],
        prefetch=1,
        estimate=cost(2 * rows * width * share * shards, left, right),
    )(slots, left, right)[0]


def middle_back_kernel(
    g_ref, up_ref, mixed_ref, gm_ref, vec_ref, out_w_ref, gmixed_ref, go_ref, gattn_ref, sums_ref
):
    @pl.when(pl.program_id(0) == 0)
    def _():
        sums_ref[...] = jnp.zeros_like(sums_ref)

    grad_h = dot_flip(g_ref[0], up_ref[0])
    for shard in range(1, g_ref.shape[0]):
        grad_h += dot_flip(g_ref[shard], up_ref[shard])
    normed, inverse = norm_parts(mixed_ref[...])
    grad = gm_ref[...].astype(f32)
    grad_mixed = grad + norm_back(grad_h * row(vec_ref, GAIN2), normed, inverse)
    gmixed_ref[...] = grad_mixed
    rounded = grad_mixed.astype(bf16)
    go_ref[...] = rounded
    for index, value in ((1, grad_h * normed), (3, grad_h), (4, grad_mixed), (5, grad)):
        sums_ref[index : index + 1, :] += jnp.sum(value, axis=0, keepdims=True)
    for shard in range(gattn_ref.shape[0]):
        gattn_ref[shard] = dot(rounded, out_w_ref[shard]).astype(bf16)


def middle_back(grad_pre, up, mixed, grad_m, vectors, weights):
    shards, rows, cols = grad_pre.shape
    width = mixed.shape[1]
    heads = weights.shape[2]
    step = lambda i: (i, 0)
    wide = pl.BlockSpec((SEQ, width), step)
    return call(
        middle_back_kernel,
        "middle_back",
        (rows // SEQ,),
        [
            pl.BlockSpec((shards, SEQ, cols), lambda i: (0, i, 0)),
            fixed(up.shape, 0, 0, 0),
            wide,
            wide,
            fixed(vectors.shape, 0, 0),
            fixed(weights.shape, 0, 0, 0),
        ],
        [
            ((SEQ, width), step, (rows, width), f32),
            ((SEQ, width), step, (rows, width), bf16),
            ((shards, SEQ, heads), lambda i: (0, i, 0), (shards, rows, heads), bf16),
            ((8, width), lambda i: (0, 0), (8, width), f32),
        ],
        estimate=cost(2 * rows * width * (cols + heads) * shards, grad_pre, up, mixed),
    )(grad_pre, up, mixed, grad_m, vectors, weights)


def input_back_kernel(g_ref, w_ref, x_ref, gmixed_ref, vec_ref, before_ref, out_ref, sums_ref):
    @pl.when(pl.program_id(0) == 0)
    def _():
        sums_ref[...] = before_ref[...]

    grad_h = dot_flip(g_ref[0], w_ref[0])
    for shard in range(1, g_ref.shape[0]):
        grad_h += dot_flip(g_ref[shard], w_ref[shard])
    normed, inverse = norm_parts(x_ref[...].astype(f32))
    out_ref[...] = gmixed_ref[...] + norm_back(grad_h * row(vec_ref, GAIN1), normed, inverse)
    for index, value in ((0, grad_h * normed), (2, grad_h)):
        sums_ref[index : index + 1, :] += jnp.sum(value, axis=0, keepdims=True)


def input_back(grad_heads, weights, tokens, grad_mixed, vectors, sums):
    shards, rows, cols = grad_heads.shape
    width = tokens.shape[1]
    step = lambda i: (i, 0)
    wide = pl.BlockSpec((SEQ, width), step)
    return call(
        input_back_kernel,
        "input_back",
        (rows // SEQ,),
        [
            pl.BlockSpec((shards, SEQ, cols), lambda i: (0, i, 0)),
            fixed(weights.shape, 0, 0, 0),
            wide,
            wide,
            fixed(vectors.shape, 0, 0),
            fixed(sums.shape, 0, 0),
        ],
        [
            ((SEQ, width), step, (rows, width), f32),
            (sums.shape, lambda i: (0, 0), sums.shape, f32),
        ],
        estimate=cost(2 * rows * width * cols * shards, weights, tokens, grad_mixed),
    )(grad_heads, weights, tokens, grad_mixed, vectors, sums)


def shrink_kernel(kept_ref, act_ref, w_ref, mixed_ref, vec_ref, *refs, first):
    out_ref = refs[-1]
    total = dot_flip(act_ref[0], w_ref[0])
    for shard in range(1, act_ref.shape[0]):
        total += dot_flip(act_ref[shard], w_ref[shard])
    valid = BUFFER + kept_ref[first + pl.program_id(0)]
    alive = lax.broadcasted_iota(jnp.int32, (SEQ, 1), 0) < valid
    result = mixed_ref[...] + total + row(vec_ref, SHIFT4)
    out_ref[...] = jnp.where(alive, result, 0.0).astype(bf16)


def shrink(first, count, kept, act, weights, mixed, vectors, *out):
    shards, rows, cols = act.shape
    width = mixed.shape[1]
    step = lambda i, k: (first + i, 0)
    return call(
        functools.partial(shrink_kernel, first=first),
        "shrink",
        (count,),
        [
            pl.BlockSpec((shards, SEQ, cols), lambda i, k: (0, first + i, 0)),
            fixed(weights.shape, 0, 0, 0),
            pl.BlockSpec((SEQ, width), step),
            fixed(vectors.shape, 0, 0),
        ]
        + [pl.BlockSpec(memory_space=pl.ANY)] * len(out),
        [((SEQ, width), step, (rows, width), bf16)],
        prefetch=1,
        aliases={5: 0} if out else None,
        estimate=cost(2 * count * SEQ * width * cols * shards, weights),
    )(kept, act, weights, mixed, vectors, *out)[0]


def swap(values, axis, bit):
    places = range(lax.axis_size(axis))
    return lax.ppermute(values, axis, [(place, place ^ bit) for place in places])


def bits_of(axis):
    return [1 << power for power in range(lax.axis_size(axis).bit_length() - 1)]


def flip_gather(part, order):
    dp, shards = lax.axis_size("dp"), lax.axis_size("tensor")
    values = part[None]
    index = jnp.arange(shards * dp, dtype=jnp.int32)
    apart = {
        "tensor": (index // dp) ^ lax.axis_index("tensor").astype(jnp.int32),
        "dp": (index % dp) ^ lax.axis_index("dp").astype(jnp.int32),
    }
    place = jnp.zeros_like(index)
    for axis, bit in order:
        place += jnp.where((apart[axis] & bit) != 0, values.shape[0], 0)
        values = jnp.concatenate([values, swap(values, axis, bit)], 0)
    return jnp.take(values, place, axis=0)


def slot_table(order):
    dp, shards = lax.axis_size("dp"), lax.axis_size("tensor")
    index = jnp.arange(shards * dp, dtype=jnp.int32)
    apart = {
        "tensor": (index // dp) ^ lax.axis_index("tensor").astype(jnp.int32),
        "dp": (index % dp) ^ lax.axis_index("dp").astype(jnp.int32),
    }
    slot = jnp.zeros_like(index)
    for depth, (axis, bit) in enumerate(order):
        slot += jnp.where((apart[axis] & bit) != 0, 1 << (len(order) - 1 - depth), 0)
    return slot


class Chain:
    def __init__(self, values, order):
        self.values, self.order = values, list(order)
        self.send()

    def send(self):
        half = self.values.shape[0] // 2
        self.near = self.values[:half]
        self.far = swap(self.values[half:], *self.order.pop(0))

    def settle(self):
        self.values = self.near + self.far

    def finish(self):
        self.settle()
        while self.order:
            self.send()
            self.settle()
        return self.values


class Sum(Chain):
    def __init__(self, values, order):
        pairs = [order[at : at + 2] for at in range(1, len(order), 2)]
        super().__init__(values, [order[:1]] + pairs)

    def send(self):
        shards = lax.axis_size("tensor")
        places = range(lax.axis_size("dp") * shards)
        masks = [0]
        for axis, bit in self.order.pop(0):
            masks += [mask ^ (bit * shards if axis == "dp" else bit) for mask in masks]
        self.far = [
            lax.ppermute(self.values, ("dp", "tensor"), [(place, place ^ mask) for place in places])
            for mask in masks[1:]
        ]

    def settle(self):
        self.values = sum(self.far, self.values)


def meet(values, *chains):
    values, far = lax.optimization_barrier((values, [chain.far for chain in chains]))
    for chain, arrived in zip(chains, far):
        chain.far = arrived
        chain.settle()
        if chain.order:
            chain.send()
    return values


def gather(part):
    full = lax.all_gather(part, ("tensor", "dp"), axis=0, tiled=True)
    return full.reshape(lax.axis_size("tensor"), -1, part.shape[1])


def scatter(full):
    flat = full.reshape(-1, full.shape[2])
    return lax.psum_scatter(flat, ("tensor", "dp"), scatter_dimension=0, tiled=True)


def body(tokens, kept, cotangent, w_qkv, w_out, w_up, w_down, qv_bias, up_bias, ln_gain, shift):
    rows, width = tokens.shape
    dp, shards = lax.axis_size("dp"), lax.axis_size("tensor")
    images = rows // SEQ
    part = w_qkv.shape[1]
    cols = w_qkv.shape[2]
    own = ln_gain.shape[1]
    barrier = lax.optimization_barrier

    core, along_x = [("dp", 1)], [("tensor", bit) for bit in bits_of("tensor")[::-1]]
    low, high = [("dp", 2)], [("dp", bit) for bit in bits_of("dp")[::-1] if bit > 2]
    order_x, order_low = core + along_x + low + high, core + low + along_x + high

    full_qkv = gather(w_qkv.transpose(1, 0, 2).reshape(part, 3 * cols))
    full_up = gather(w_up)
    full_down = gather(w_down.T)

    small = jnp.concatenate(
        [ln_gain, shift, qv_bias.astype(f32), up_bias.astype(f32).reshape(-1, own)], 0
    )
    small = flip_gather(small, high + low + along_x + core)
    small = small.reshape((shards, dp) + small.shape[1:])
    vectors = small[:, :, :6].transpose(2, 1, 0, 3).reshape(6, width)
    vectors = jnp.concatenate([vectors, jnp.zeros((2, width), f32)], 0)
    bias_qv = small[:, :, 6:8].transpose(0, 2, 1, 3).reshape(shards, 2, cols)
    bias_up = small[:, :, 8:].reshape(shards, 1, -1)
    bias_heads = jnp.concatenate([bias_qv[:, :1], jnp.zeros_like(bias_qv[:, :1]), bias_qv[:, 1:]], 2)
    full_out = flip_gather(w_out.T, high + low + along_x + core).reshape(shards, width, cols)

    first_image = lax.axis_index("tensor") * images
    kept_own = lax.dynamic_slice_in_dim(kept, first_image, images, 0)
    positions = jnp.arange(SEQ, dtype=jnp.int32)
    alive = (positions[None, :] < BUFFER + kept_own[:, None]).reshape(rows, 1)
    grad_m = jnp.where(alive, cotangent, jnp.zeros_like(cotangent))

    tables = [slot_table(order_x), slot_table(order_low)]

    h1 = norm_in(tokens, vectors)
    qkv = project(h1, full_qkv, bias_heads)
    attn, expo, inverse_sum = attend(qkv, kept_own)
    mixed, h2 = mix(attn, full_out, tokens, vectors)
    act, slope = expand(h2, full_up, bias_up)

    hidden = act.shape[2]
    grad_down = weight_grad(grad_m, act, hidden, hidden // 8, True)
    grad_m, grad_down = barrier((grad_m, grad_down))
    sent_down = scatter(grad_down)[:, :hidden]
    grad_pre, grad_bias_up = expand_back(grad_m, full_down, slope)

    share = hidden // 2
    grad_second = weight_grad_slots(h2, grad_pre, 1, 2, tables[0])
    grad_pre, grad_second = barrier((grad_pre, grad_second))
    chain_up = Chain(grad_second, order_x)
    grad_first = weight_grad(h2, grad_pre, share, cols, False)
    grad_pre, grad_first = barrier((grad_pre, grad_first))
    grad_pre = meet(grad_pre, chain_up)
    grad_mixed, grad_o, grad_attn, sums2 = middle_back(
        grad_pre, full_up, mixed, grad_m, vectors, full_out
    )
    grad_o = meet(grad_o, chain_up)
    grad_first = weight_grad_into(grad_o, attn, grad_first)
    grad_attn, grad_first = barrier((grad_attn, grad_first))
    grad_heads, grad_bias_qv = attend_back(qkv, grad_attn, attn, expo, inverse_sum)
    grad_heads = meet(grad_heads, chain_up)
    grad_heads, sent_down, grad_first = barrier((grad_heads, sent_down, grad_first))
    sent_first = scatter(grad_first)

    chains_qkv = []
    shares = 2 if (3 * cols // 2) % LANES == 0 else 1
    for which, order in enumerate((order_x, order_low)[:shares]):
        grad_qkv = weight_grad_slots(h1, grad_heads, which, shares, tables[which])
        grad_heads, grad_qkv = barrier((grad_heads, grad_qkv))
        grad_qkv = meet(grad_qkv, *chains_qkv)
        chains_qkv.append(Chain(grad_qkv, order))
    sums = jnp.concatenate(
        [
            sums2[:6],
            grad_bias_qv.transpose(1, 0, 2).reshape(2, width),
            grad_bias_up.reshape(-1, width),
        ],
        0,
    )
    grad_heads = meet(grad_heads, chain_up, *chains_qkv[1:])
    grad_tokens, sums = input_back(grad_heads, full_qkv, tokens, grad_mixed, vectors, sums)
    sums, act = meet((sums, act), chain_up, *chains_qkv)
    chain_small = Sum(sums, order_x)
    first = images // 2
    layer_out = shrink(0, first, kept_own, act, full_down, mixed, vectors)
    layer_out = meet(layer_out, chain_small, *chains_qkv)
    layer_out = shrink(first, images - first, kept_own, act, full_down, mixed, vectors, layer_out)
    layer_out = meet(layer_out, chain_small, *chains_qkv)
    sent_up = jnp.concatenate([sent_first[:, :share], chain_up.finish()[0]], 1)
    sent_qkv = jnp.concatenate([chain.finish()[0] for chain in chains_qkv], 1)
    small = chain_small.finish()
    at_dp, at_tensor = lax.axis_index("dp"), lax.axis_index("tensor")
    row_place, shard_place = at_dp * shards + at_tensor, at_tensor * dp + at_dp
    rows_own = lax.dynamic_slice(small, (0, row_place * own), (6, own))
    heads_own = lax.dynamic_slice(small, (6, shard_place * own), (2, own))
    count = up_bias.shape[0]
    start = shard_place * count
    up_own = lax.dynamic_slice(small, (8 + start // width, start % width), (1, count))

    return (
        layer_out,
        grad_tokens,
        sent_qkv.astype(f32).reshape(part, 3, cols).transpose(1, 0, 2),
        sent_first[:, share:].astype(f32).T,
        sent_up.astype(f32),
        sent_down.astype(f32).T,
        heads_own,
        up_own.reshape(-1),
        rows_own[:2],
        rows_own[2:],
    )


def solution(mesh):
    both = P(("dp", "tensor"), None)
    matrices = (
        P(None, "dp", "tensor"),
        P("tensor", "dp"),
        P("dp", "tensor"),
        P("tensor", "dp"),
        P(None, ("tensor", "dp")),
        P(("tensor", "dp")),
        P(None, ("dp", "tensor")),
        P(None, ("dp", "tensor")),
    )
    return jax.shard_map(
        body,
        mesh=mesh,
        in_specs=(both, P("dp"), both) + matrices,
        out_specs=(both, both) + matrices,
        check_vma=False,
    )
```

```python
import functools

import jax
import jax.numpy as jnp
from jax import lax
from jax.experimental import pallas as pl
from jax.experimental.pallas import tpu as pltpu
from jax.sharding import PartitionSpec as P

HEAD_DIM = 64
BUFFER = 64
SEQ = 320
KEYS = 384
LANES = 128
EPSILON = 1e-06
SCALE = HEAD_DIM ** (-0.5)
LOG2E = 1.4426950408889634
NEGATIVE = -1000000000.0 / SCALE
VMEM = 56 << 20


f32 = jnp.float32
bf16 = jnp.bfloat16


def dot(left, right):
    return lax.dot_general(left, right, (((1,), (0,)), ((), ())), preferred_element_type=f32)


def dot_flip(left, right):
    return lax.dot_general(left, right, (((1,), (1,)), ((), ())), preferred_element_type=f32)


def split_heads(values):
    low = lax.broadcasted_iota(jnp.int32, (1, LANES), 1) < HEAD_DIM
    zero = jnp.zeros_like(values)
    return jnp.where(low, values, zero), jnp.where(low, zero, values)


def pad_keys(values):
    return jnp.concatenate([values, jnp.zeros((KEYS - SEQ, values.shape[1]), values.dtype)], 0)


def attend_kernel(kept_ref, q_ref, k_ref, v_ref, o_ref, e_ref, r_ref, *, pairs):
    valid = BUFFER + kept_ref[pl.program_id(1)]
    alive = lax.broadcasted_iota(jnp.int32, (1, KEYS), 1) < valid
    ones = split_heads(jnp.ones((KEYS, LANES), bf16))
    for pair in range(pairs):
        cols = slice(LANES * pair, LANES * (pair + 1))
        keys = pad_keys(k_ref[0, :, cols])
        values = split_heads(pad_keys(v_ref[0, :, cols]))
        expos = []
        for head, query in enumerate(split_heads(q_ref[0, :, cols])):
            scores = jnp.where(alive, dot_flip(query, keys), NEGATIVE)
            highest = jnp.max(scores, axis=-1, keepdims=True)
            expo = jnp.exp2((scores - highest) * (SCALE * LOG2E)).astype(bf16)
            e_ref[0, 0, pair, head] = expo
            expos.append(expo)
        right = jnp.concatenate(
            [jnp.concatenate([value, one], 1) for value, one in zip(values, ones)], 0
        )
        both = dot(jnp.concatenate(expos, 1), right)
        inverse = 1.0 / both[:, LANES:]
        o_ref[0, :, cols] = (both[:, :LANES] * inverse).astype(bf16)
        r_ref[0, :, cols] = inverse


def attend(qkv, kept):
    shards, rows, width = qkv.shape
    cols = width // 3
    pairs = cols // LANES
    images = rows // SEQ
    part = lambda which: pl.BlockSpec((1, SEQ, cols), lambda t, i, k: (t, i, which))
    probs = pl.BlockSpec((1, 1, pairs, 2, SEQ, KEYS), lambda t, i, k: (t, i, 0, 0, 0, 0))
    return pl.pallas_call(
        functools.partial(attend_kernel, pairs=pairs),
        grid_spec=pltpu.PrefetchScalarGridSpec(
            num_scalar_prefetch=1,
            grid=(shards, images),
            in_specs=[part(0), part(1), part(2)],
            out_specs=[part(0), probs, part(0)],
        ),
        out_shape=[
            jax.ShapeDtypeStruct((shards, rows, cols), bf16),
            jax.ShapeDtypeStruct((shards, images, pairs, 2, SEQ, KEYS), bf16),
            jax.ShapeDtypeStruct((shards, rows, cols), f32),
        ],
        name="attend",
        cost_estimate=cost(rows * cols * shards * SEQ * 16, qkv, qkv),
        compiler_params=pltpu.CompilerParams(
            dimension_semantics=("arbitrary", "arbitrary"), vmem_limit_bytes=VMEM
        ),
    )(kept, qkv, qkv, qkv)


def attend_back_kernel(q_ref, k_ref, v_ref, g_ref, o_ref, e_ref, r_ref, out_ref, bias_ref, *, pairs):
    width = pairs * LANES

    @pl.when(pl.program_id(1) == 0)
    def _():
        bias_ref[...] = jnp.zeros_like(bias_ref)

    for pair in range(pairs):
        cols = slice(LANES * pair, LANES * (pair + 1))
        query = q_ref[0, :, cols]
        values = pad_keys(v_ref[0, :, cols])
        grad = (g_ref[0, :, cols].astype(f32) * r_ref[0, :, cols]).astype(bf16)
        product = split_heads(grad.astype(f32) * o_ref[0, :, cols].astype(f32))
        grads = []
        for head, grad_head in enumerate(split_heads(grad)):
            inner = jnp.sum(product[head], axis=-1, keepdims=True)
            expo = e_ref[0, 0, pair, head].astype(f32)
            grads.append((expo * (dot_flip(grad_head, values) - inner)).astype(bf16))
        keys = jnp.concatenate(split_heads(pad_keys(k_ref[0, :, cols])), 0)
        grad_query = (dot(jnp.concatenate(grads, 1), keys) * SCALE).astype(bf16)
        query_flip, grad_flip = query.T, grad.T
        halves = [slice(HEAD_DIM * head, HEAD_DIM * (head + 1)) for head in range(2)]
        grad_key = jnp.concatenate([dot(query_flip[half], grads[h]) for h, half in enumerate(halves)], 0)
        grad_value = jnp.concatenate(
            [dot(grad_flip[half], e_ref[0, 0, pair, h]) for h, half in enumerate(halves)], 0
        )
        grad_key = (grad_key.T[:SEQ] * SCALE).astype(bf16)
        grad_value = grad_value.T[:SEQ].astype(bf16)
        for which, value in enumerate((grad_query, grad_key, grad_value)):
            start = which * width + LANES * pair
            out_ref[0, :, start : start + LANES] = value
        bias_ref[0, 0:1, cols] += jnp.sum(grad_query.astype(f32), axis=0, keepdims=True)
        bias_ref[0, 1:2, cols] += jnp.sum(grad_value.astype(f32), axis=0, keepdims=True)


def attend_back(qkv, grad, attn, expo, inverse):
    shards, rows, width = qkv.shape
    cols = width // 3
    pairs = cols // LANES
    images = rows // SEQ
    part = lambda which: pl.BlockSpec((1, SEQ, cols), lambda t, i: (t, i, which))
    probs = pl.BlockSpec((1, 1, pairs, 2, SEQ, KEYS), lambda t, i: (t, i, 0, 0, 0, 0))
    return pl.pallas_call(
        functools.partial(attend_back_kernel, pairs=pairs),
        grid=(shards, images),
        in_specs=[part(0), part(1), part(2), part(0), part(0), probs, part(0)],
        out_specs=[
            pl.BlockSpec((1, SEQ, width), lambda t, i: (t, i, 0)),
            pl.BlockSpec((1, 2, cols), lambda t, i: (t, 0, 0)),
        ],
        out_shape=[
            jax.ShapeDtypeStruct((shards, rows, width), bf16),
            jax.ShapeDtypeStruct((shards, 2, cols), f32),
        ],
        name="attend_back",
        cost_estimate=cost(rows * cols * shards * SEQ * 24, qkv, qkv, expo),
        compiler_params=pltpu.CompilerParams(
            dimension_semantics=("arbitrary", "arbitrary"), vmem_limit_bytes=VMEM
        ),
    )(qkv, qkv, qkv, grad, attn, expo, inverse)


def norm_parts(values):
    centred = values - jnp.mean(values, axis=-1, keepdims=True)
    inverse = lax.rsqrt(jnp.mean(centred * centred, axis=-1, keepdims=True) + EPSILON)
    return centred * inverse, inverse


def norm_back(grad_normed, normed, inverse):
    first = jnp.mean(grad_normed, axis=-1, keepdims=True)
    second = jnp.mean(grad_normed * normed, axis=-1, keepdims=True)
    return inverse * (grad_normed - first - normed * second)


def block_rows(rows):
    return next(size for size in (512, 320, rows) if rows % size == 0)


def cost(flops, *arrays):
    return pl.CostEstimate(
        flops=flops, transcendentals=0, bytes_accessed=sum(a.size * a.dtype.itemsize for a in arrays)
    )


def call(kernel, name, grid, in_specs, outs, prefetch=0, aliases=None, estimate=None):
    return pl.pallas_call(
        kernel,
        grid_spec=pltpu.PrefetchScalarGridSpec(
            num_scalar_prefetch=prefetch,
            grid=grid,
            in_specs=in_specs,
            out_specs=[pl.BlockSpec(block, index) for block, index, _, _ in outs],
        ),
        out_shape=[jax.ShapeDtypeStruct(shape, kind) for _, _, shape, kind in outs],
        name=name,
        input_output_aliases=aliases or {},
        cost_estimate=estimate,
        compiler_params=pltpu.CompilerParams(
            dimension_semantics=("arbitrary",) * len(grid), vmem_limit_bytes=VMEM
        ),
    )


def fixed(block, *index):
    return pl.BlockSpec(block, lambda *_: index, pipeline_mode=pl.Buffered(1))


GAIN1, GAIN2, SHIFT1, SHIFT2, SHIFT3, SHIFT4 = range(6)


def row(ref, index):
    return ref[index : index + 1, :]


def norm_in_kernel(x_ref, vec_ref, h_ref):
    normed, _ = norm_parts(x_ref[...].astype(f32))
    h_ref[...] = (normed * row(vec_ref, GAIN1) + row(vec_ref, SHIFT1)).astype(bf16)


def norm_in(tokens, vectors):
    rows, width = tokens.shape
    step = pl.BlockSpec((SEQ, width), lambda i: (i, 0))
    return call(
        norm_in_kernel,
        "norm_in",
        (rows // SEQ,),
        [step, fixed(vectors.shape, 0, 0)],
        [((SEQ, width), lambda i: (i, 0), (rows, width), bf16)],
        estimate=cost(16 * rows * width, tokens, tokens),
    )(tokens, vectors)[0]


def project_kernel(h_ref, w_ref, bias_ref, out_ref):
    for shard in range(out_ref.shape[0]):
        out_ref[shard] = (dot(h_ref[...], w_ref[shard]) + bias_ref[shard]).astype(bf16)


def project(h1, weights, bias):
    rows, width = h1.shape
    shards, _, cols = bias.shape
    size = block_rows(rows)
    return call(
        project_kernel,
        "project",
        (rows // size,),
        [
            pl.BlockSpec((size, width), lambda i: (i, 0)),
            fixed((shards, width, cols), 0, 0, 0),
            fixed(bias.shape, 0, 0, 0),
        ],
        [((shards, size, cols), lambda i: (0, i, 0), (shards, rows, cols), bf16)],
        estimate=cost(2 * rows * width * cols * shards, h1, weights),
    )(h1, weights, bias)[0]


def mix_kernel(attn_ref, w_ref, x_ref, vec_ref, mixed_ref, h_ref):
    total = dot_flip(attn_ref[0], w_ref[0])
    for shard in range(1, attn_ref.shape[0]):
        total += dot_flip(attn_ref[shard], w_ref[shard])
    mixed = x_ref[...].astype(f32) + total + row(vec_ref, SHIFT3)
    normed, _ = norm_parts(mixed)
    mixed_ref[...] = mixed
    h_ref[...] = (normed * row(vec_ref, GAIN2) + row(vec_ref, SHIFT2)).astype(bf16)


def mix(attn, weights, tokens, vectors):
    shards, rows, cols = attn.shape
    width = tokens.shape[1]
    size = block_rows(rows)
    step = lambda i: (i, 0)
    return call(
        mix_kernel,
        "mix",
        (rows // size,),
        [
            pl.BlockSpec((shards, size, cols), lambda i: (0, i, 0)),
            fixed(weights.shape, 0, 0, 0),
            pl.BlockSpec((size, width), step),
            fixed(vectors.shape, 0, 0),
        ],
        [
            ((size, width), step, (rows, width), f32),
            ((size, width), step, (rows, width), bf16),
        ],
        estimate=cost(2 * rows * width * cols * shards, attn, tokens),
    )(attn, weights, tokens, vectors)


GELU_IN = 0.7978845608
GELU_CUBE = 0.044715


def gelu_parts(pre):
    cube = (GELU_IN * GELU_CUBE) * (pre * pre)
    half = 0.5 * jnp.tanh(pre * (GELU_IN + cube)) + 0.5
    act = pre * half
    return act, half + (act - act * half) * (2.0 * GELU_IN + 6.0 * cube)


CHUNK = 512


def expand_kernel(h_ref, w_ref, bias_ref, act_ref, slope_ref):
    cols = act_ref.shape[2]
    chunk = min(CHUNK, cols)
    for start in range(0, cols, chunk):
        part = slice(start, start + chunk)
        act, slope = gelu_parts(dot(h_ref[...], w_ref[0, :, part]) + bias_ref[0, :, part])
        act_ref[0, :, part] = act.astype(bf16)
        slope_ref[0, :, part] = slope.astype(bf16)


def expand(h2, weights, bias):
    rows, width = h2.shape
    shards, _, cols = weights.shape
    size = block_rows(rows)
    out = ((1, size, cols), lambda t, i: (t, i, 0), (shards, rows, cols), bf16)
    return call(
        expand_kernel,
        "expand",
        (shards, rows // size),
        [
            pl.BlockSpec((size, width), lambda t, i: (i, 0)),
            pl.BlockSpec((1, width, cols), lambda t, i: (t, 0, 0)),
            pl.BlockSpec((1, 1, cols), lambda t, i: (t, 0, 0)),
        ],
        [out, out],
        estimate=cost(3 * rows * width * cols * shards, h2, weights),
    )(h2, weights, bias)


def expand_back_kernel(g_ref, w_ref, slope_ref, out_ref, bias_ref):
    @pl.when(pl.program_id(1) == 0)
    def _():
        bias_ref[...] = jnp.zeros_like(bias_ref)

    cols = out_ref.shape[2]
    chunk = min(CHUNK, cols)
    for start in range(0, cols, chunk):
        part = slice(start, start + chunk)
        grad = (dot(g_ref[...], w_ref[0, :, part]) * slope_ref[0, :, part].astype(f32)).astype(bf16)
        out_ref[0, :, part] = grad
        bias_ref[0, :, part] += jnp.sum(grad.astype(f32), axis=0, keepdims=True)


def expand_back(grad, weights, slope):
    rows, width = grad.shape
    shards, _, cols = weights.shape
    size = block_rows(rows)
    step = lambda t, i: (t, i, 0)
    return call(
        expand_back_kernel,
        "expand_back",
        (shards, rows // size),
        [
            pl.BlockSpec((size, width), lambda t, i: (i, 0)),
            pl.BlockSpec((1, width, cols), lambda t, i: (t, 0, 0)),
            pl.BlockSpec((1, size, cols), step),
        ],
        [
            ((1, size, cols), step, (shards, rows, cols), bf16),
            ((1, 1, cols), lambda t, i: (t, 0, 0), (shards, 1, cols), f32),
        ],
        estimate=cost(2 * rows * width * cols * shards, slope, slope),
    )(grad, weights, slope)


def dot_rows(left, right):
    return lax.dot_general(left, right, (((0,), (0,)), ((), ())), preferred_element_type=f32)


def weight_grad_kernel(left_ref, right_ref, out_ref, *, chunk, fill):
    which = pl.program_id(1)
    start = pl.multiple_of(which * chunk, chunk)
    out_ref[0, :, pl.ds(start, chunk)] = dot_rows(left_ref[...], right_ref[0]).astype(bf16)
    if fill:

        @pl.when(which == 0)
        def _():
            spare = jnp.zeros((out_ref.shape[1], fill), bf16)
            out_ref[0, :, out_ref.shape[2] - fill :] = spare


def weight_grad(left, right, spare):
    rows, width = left.shape
    shards, _, used = right.shape
    chunk = min(512, used)
    block = (1, width, used + spare)
    return call(
        functools.partial(weight_grad_kernel, chunk=chunk, fill=spare),
        "weight_grad",
        (shards, used // chunk),
        [
            fixed((rows, width), 0, 0),
            pl.BlockSpec((1, rows, chunk), lambda t, n: (t, 0, n)),
        ],
        [(block, lambda t, n: (t, 0, 0), (shards,) + block[1:], bf16)],
        estimate=cost(2 * rows * width * used * shards, left, right),
    )(left, right)[0]


def weight_grad_into_kernel(left_ref, right_ref, _, out_ref):
    out_ref[0] = dot_rows(left_ref[...], right_ref[0]).astype(bf16)


def weight_grad_into(left, right, out):
    rows, width = left.shape
    shards, _, cols = right.shape
    place = out.shape[2] // cols - 1
    return call(
        weight_grad_into_kernel,
        "weight_grad_into",
        (shards,),
        [
            fixed((rows, width), 0, 0),
            pl.BlockSpec((1, rows, cols), lambda t: (t, 0, 0)),
            pl.BlockSpec(memory_space=pl.ANY),
        ],
        [((1, width, cols), lambda t: (t, 0, place), out.shape, bf16)],
        aliases={2: 0},
        estimate=cost(2 * rows * width * cols * shards, left, right),
    )(left, right, out)[0]


def weight_grad_slots_kernel(slot_ref, left_ref, right_ref, out_ref, *, owners):
    grad = dot_rows(left_ref[...], right_ref[0]).astype(bf16)
    part = out_ref.shape[1]
    for owner in range(owners):
        slot = slot_ref[pl.program_id(1) * owners + owner]
        out_ref[slot] = grad[owner * part : (owner + 1) * part]


def weight_grad_slots(left, right, which, shares, slots):
    rows, width = left.shape
    shards, _, cols = right.shape
    share = cols // shares
    count = slots.shape[0]
    owners = count // shards
    part = width // owners
    chunk = share if share <= 1024 else 512
    first = which * share // chunk
    return call(
        functools.partial(weight_grad_slots_kernel, owners=owners),
        "weight_grad_slots",
        (share // chunk, shards),
        [
            fixed((rows, width), 0, 0),
            pl.BlockSpec((1, rows, chunk), lambda n, t, s: (t, 0, first + n)),
        ],
        [((count, part, chunk), lambda n, t, s: (0, 0, n), (count, part, share), bf16)],
        prefetch=1,
        estimate=cost(2 * rows * width * share * shards, left, right),
    )(slots, left, right)[0]


def weight_grad_halves_kernel(slot_ref, left_ref, right_ref, first_ref, second_ref, *, owners, steps):
    grad = dot_rows(left_ref[...], right_ref[0]).astype(bf16)

    @pl.when(pl.program_id(0) < steps)
    def _():
        first_ref[0] = grad

    @pl.when(pl.program_id(0) >= steps)
    def _():
        part = second_ref.shape[1]
        for owner in range(owners):
            slot = slot_ref[pl.program_id(1) * owners + owner]
            second_ref[slot] = grad[owner * part : (owner + 1) * part]


def weight_grad_halves(left, right, spare, slots):
    rows, width = left.shape
    shards, _, cols = right.shape
    half = cols // 2
    count = slots.shape[0]
    owners = count // shards
    part = width // owners
    chunk = min(512, half)
    steps = half // chunk
    early = lambda n, value, last: jnp.where(n < steps, value, last)
    return call(
        functools.partial(weight_grad_halves_kernel, owners=owners, steps=steps),
        "weight_grad_halves",
        (2 * steps, shards),
        [
            fixed((rows, width), 0, 0),
            pl.BlockSpec((1, rows, chunk), lambda n, t, s: (t, 0, n)),
        ],
        [
            (
                (1, width, chunk),
                lambda n, t, s: (early(n, t, shards - 1), 0, early(n, n, steps - 1)),
                (shards, width, half + spare),
                bf16,
            ),
            (
                (count, part, chunk),
                lambda n, t, s: (0, 0, jnp.maximum(n - steps, 0)),
                (count, part, half),
                bf16,
            ),
        ],
        prefetch=1,
        estimate=cost(2 * rows * width * cols * shards, left, right),
    )(slots, left, right)


def middle_back_kernel(
    g_ref, up_ref, mixed_ref, gm_ref, vec_ref, out_w_ref, gmixed_ref, go_ref, gattn_ref, sums_ref
):
    @pl.when(pl.program_id(0) == 0)
    def _():
        sums_ref[...] = jnp.zeros_like(sums_ref)

    grad_h = dot_flip(g_ref[0], up_ref[0])
    for shard in range(1, g_ref.shape[0]):
        grad_h += dot_flip(g_ref[shard], up_ref[shard])
    normed, inverse = norm_parts(mixed_ref[...])
    grad = gm_ref[...].astype(f32)
    grad_mixed = grad + norm_back(grad_h * row(vec_ref, GAIN2), normed, inverse)
    gmixed_ref[...] = grad_mixed
    rounded = grad_mixed.astype(bf16)
    go_ref[...] = rounded
    for index, value in ((1, grad_h * normed), (3, grad_h), (4, grad_mixed), (5, grad)):
        sums_ref[index : index + 1, :] += jnp.sum(value, axis=0, keepdims=True)
    for shard in range(gattn_ref.shape[0]):
        gattn_ref[shard] = dot(rounded, out_w_ref[shard]).astype(bf16)


def middle_back(grad_pre, up, mixed, grad_m, vectors, weights):
    shards, rows, cols = grad_pre.shape
    width = mixed.shape[1]
    heads = weights.shape[2]
    step = lambda i: (i, 0)
    wide = pl.BlockSpec((SEQ, width), step)
    return call(
        middle_back_kernel,
        "middle_back",
        (rows // SEQ,),
        [
            pl.BlockSpec((shards, SEQ, cols), lambda i: (0, i, 0)),
            fixed(up.shape, 0, 0, 0),
            wide,
            wide,
            fixed(vectors.shape, 0, 0),
            fixed(weights.shape, 0, 0, 0),
        ],
        [
            ((SEQ, width), step, (rows, width), f32),
            ((SEQ, width), step, (rows, width), bf16),
            ((shards, SEQ, heads), lambda i: (0, i, 0), (shards, rows, heads), bf16),
            ((8, width), lambda i: (0, 0), (8, width), f32),
        ],
        estimate=cost(2 * rows * width * (cols + heads) * shards, grad_pre, up, mixed),
    )(grad_pre, up, mixed, grad_m, vectors, weights)


def input_back_kernel(g_ref, w_ref, x_ref, gmixed_ref, vec_ref, before_ref, out_ref, sums_ref):
    @pl.when(pl.program_id(0) == 0)
    def _():
        sums_ref[...] = before_ref[...]

    grad_h = dot_flip(g_ref[0], w_ref[0])
    for shard in range(1, g_ref.shape[0]):
        grad_h += dot_flip(g_ref[shard], w_ref[shard])
    normed, inverse = norm_parts(x_ref[...].astype(f32))
    out_ref[...] = gmixed_ref[...] + norm_back(grad_h * row(vec_ref, GAIN1), normed, inverse)
    for index, value in ((0, grad_h * normed), (2, grad_h)):
        sums_ref[index : index + 1, :] += jnp.sum(value, axis=0, keepdims=True)


def input_back(grad_heads, weights, tokens, grad_mixed, vectors, sums):
    shards, rows, cols = grad_heads.shape
    width = tokens.shape[1]
    step = lambda i: (i, 0)
    wide = pl.BlockSpec((SEQ, width), step)
    return call(
        input_back_kernel,
        "input_back",
        (rows // SEQ,),
        [
            pl.BlockSpec((shards, SEQ, cols), lambda i: (0, i, 0)),
            fixed(weights.shape, 0, 0, 0),
            wide,
            wide,
            fixed(vectors.shape, 0, 0),
            fixed(sums.shape, 0, 0),
        ],
        [
            ((SEQ, width), step, (rows, width), f32),
            (sums.shape, lambda i: (0, 0), sums.shape, f32),
        ],
        estimate=cost(2 * rows * width * cols * shards, weights, tokens, grad_mixed),
    )(grad_heads, weights, tokens, grad_mixed, vectors, sums)


def shrink_kernel(kept_ref, act_ref, w_ref, mixed_ref, vec_ref, *refs, first):
    out_ref = refs[-1]
    total = dot_flip(act_ref[0], w_ref[0])
    for shard in range(1, act_ref.shape[0]):
        total += dot_flip(act_ref[shard], w_ref[shard])
    valid = BUFFER + kept_ref[first + pl.program_id(0)]
    alive = lax.broadcasted_iota(jnp.int32, (SEQ, 1), 0) < valid
    result = mixed_ref[...] + total + row(vec_ref, SHIFT4)
    out_ref[...] = jnp.where(alive, result, 0.0).astype(bf16)


def shrink(first, count, kept, act, weights, mixed, vectors, *out):
    shards, rows, cols = act.shape
    width = mixed.shape[1]
    step = lambda i, k: (first + i, 0)
    return call(
        functools.partial(shrink_kernel, first=first),
        "shrink",
        (count,),
        [
            pl.BlockSpec((shards, SEQ, cols), lambda i, k: (0, first + i, 0)),
            fixed(weights.shape, 0, 0, 0),
            pl.BlockSpec((SEQ, width), step),
            fixed(vectors.shape, 0, 0),
        ]
        + [pl.BlockSpec(memory_space=pl.ANY)] * len(out),
        [((SEQ, width), step, (rows, width), bf16)],
        prefetch=1,
        aliases={5: 0} if out else None,
        estimate=cost(2 * count * SEQ * width * cols * shards, weights),
    )(kept, act, weights, mixed, vectors, *out)[0]


def swap(values, axis, bit):
    places = range(lax.axis_size(axis))
    return lax.ppermute(values, axis, [(place, place ^ bit) for place in places])


def bits_of(axis):
    return [1 << power for power in range(lax.axis_size(axis).bit_length() - 1)]


def flip_gather(part, order):
    dp, shards = lax.axis_size("dp"), lax.axis_size("tensor")
    values = part[None]
    index = jnp.arange(shards * dp, dtype=jnp.int32)
    apart = {
        "tensor": (index // dp) ^ lax.axis_index("tensor").astype(jnp.int32),
        "dp": (index % dp) ^ lax.axis_index("dp").astype(jnp.int32),
    }
    place = jnp.zeros_like(index)
    for axis, bit in order:
        place += jnp.where((apart[axis] & bit) != 0, values.shape[0], 0)
        values = jnp.concatenate([values, swap(values, axis, bit)], 0)
    return jnp.take(values, place, axis=0)


def slot_table(order):
    dp, shards = lax.axis_size("dp"), lax.axis_size("tensor")
    index = jnp.arange(shards * dp, dtype=jnp.int32)
    apart = {
        "tensor": (index // dp) ^ lax.axis_index("tensor").astype(jnp.int32),
        "dp": (index % dp) ^ lax.axis_index("dp").astype(jnp.int32),
    }
    slot = jnp.zeros_like(index)
    for depth, (axis, bit) in enumerate(order):
        slot += jnp.where((apart[axis] & bit) != 0, 1 << (len(order) - 1 - depth), 0)
    return slot


class Chain:
    def __init__(self, values, order):
        self.values, self.order = values, list(order)
        self.send()

    def send(self):
        half = self.values.shape[0] // 2
        self.near = self.values[:half]
        self.far = swap(self.values[half:], *self.order.pop(0))

    def settle(self):
        self.values = self.near + self.far

    def finish(self):
        self.settle()
        while self.order:
            self.send()
            self.settle()
        return self.values


class Sum(Chain):
    def __init__(self, values, order):
        super().__init__(values, [order[at : at + 2] for at in range(0, len(order), 2)])

    def send(self):
        shards = lax.axis_size("tensor")
        places = range(lax.axis_size("dp") * shards)
        masks = [0]
        for axis, bit in self.order.pop(0):
            masks += [mask ^ (bit * shards if axis == "dp" else bit) for mask in masks]
        self.far = [
            lax.ppermute(self.values, ("dp", "tensor"), [(place, place ^ mask) for place in places])
            for mask in masks[1:]
        ]

    def settle(self):
        self.values = sum(self.far, self.values)


def meet(values, *chains):
    values, far = lax.optimization_barrier((values, [chain.far for chain in chains]))
    for chain, arrived in zip(chains, far):
        chain.far = arrived
        chain.settle()
        if chain.order:
            chain.send()
    return values


def gather(part):
    full = lax.all_gather(part, ("tensor", "dp"), axis=0, tiled=True)
    return full.reshape(lax.axis_size("tensor"), -1, part.shape[1])


def scatter(full):
    flat = full.reshape(-1, full.shape[2])
    return lax.psum_scatter(flat, ("tensor", "dp"), scatter_dimension=0, tiled=True)


def body(tokens, kept, cotangent, w_qkv, w_out, w_up, w_down, qv_bias, up_bias, ln_gain, shift):
    rows, width = tokens.shape
    dp, shards = lax.axis_size("dp"), lax.axis_size("tensor")
    images = rows // SEQ
    part = w_qkv.shape[1]
    cols = w_qkv.shape[2]
    own = ln_gain.shape[1]
    barrier = lax.optimization_barrier

    core, along_x = [("dp", 1)], [("tensor", bit) for bit in bits_of("tensor")[::-1]]
    low, high = [("dp", 2)], [("dp", bit) for bit in bits_of("dp")[::-1] if bit > 2]
    order_x, order_low = core + along_x + low + high, core + low + along_x + high

    full_qkv = gather(w_qkv.transpose(1, 0, 2).reshape(part, 3 * cols))
    full_up = gather(w_up)
    full_down = gather(w_down.T)

    small = jnp.concatenate(
        [ln_gain, shift, qv_bias.astype(f32), up_bias.astype(f32).reshape(-1, own)], 0
    )
    small = flip_gather(small, high + low + along_x + core)
    small = small.reshape((shards, dp) + small.shape[1:])
    vectors = small[:, :, :6].transpose(2, 1, 0, 3).reshape(6, width)
    vectors = jnp.concatenate([vectors, jnp.zeros((2, width), f32)], 0)
    bias_qv = small[:, :, 6:8].transpose(0, 2, 1, 3).reshape(shards, 2, cols)
    bias_up = small[:, :, 8:].reshape(shards, 1, -1)
    bias_heads = jnp.concatenate([bias_qv[:, :1], jnp.zeros_like(bias_qv[:, :1]), bias_qv[:, 1:]], 2)
    full_out = flip_gather(w_out.T, high + low + along_x + core).reshape(shards, width, cols)

    first_image = lax.axis_index("tensor") * images
    kept_own = lax.dynamic_slice_in_dim(kept, first_image, images, 0)
    positions = jnp.arange(SEQ, dtype=jnp.int32)
    alive = (positions[None, :] < BUFFER + kept_own[:, None]).reshape(rows, 1)
    grad_m = jnp.where(alive, cotangent, jnp.zeros_like(cotangent))

    tables = [slot_table(order_x), slot_table(order_low)]

    h1 = norm_in(tokens, vectors)
    qkv = project(h1, full_qkv, bias_heads)
    attn, expo, inverse_sum = attend(qkv, kept_own)
    mixed, h2 = mix(attn, full_out, tokens, vectors)
    act, slope = expand(h2, full_up, bias_up)

    hidden = act.shape[2]
    grad_down = weight_grad(grad_m, act, hidden // 8)
    grad_m, grad_down = barrier((grad_m, grad_down))
    sent_down = scatter(grad_down)[:, :hidden]
    grad_pre, grad_bias_up = expand_back(grad_m, full_down, slope)

    share = hidden // 2
    grad_first, grad_second = weight_grad_halves(h2, grad_pre, cols, tables[0])
    grad_pre, grad_first, grad_second = barrier((grad_pre, grad_first, grad_second))
    chain_up = Chain(grad_second, order_x)
    grad_mixed, grad_o, grad_attn, sums2 = middle_back(
        grad_pre, full_up, mixed, grad_m, vectors, full_out
    )
    grad_o = meet(grad_o, chain_up)
    grad_first = weight_grad_into(grad_o, attn, grad_first)
    grad_attn, grad_first = barrier((grad_attn, grad_first))
    grad_heads, grad_bias_qv = attend_back(qkv, grad_attn, attn, expo, inverse_sum)
    grad_heads = meet(grad_heads, chain_up)
    grad_heads, sent_down, grad_first = barrier((grad_heads, sent_down, grad_first))
    sent_first = scatter(grad_first)

    chains_qkv = []
    shares = 2 if (3 * cols // 2) % LANES == 0 else 1
    for which, order in enumerate((order_x, order_low)[:shares]):
        grad_qkv = weight_grad_slots(h1, grad_heads, which, shares, tables[which])
        grad_heads, grad_qkv = barrier((grad_heads, grad_qkv))
        if which == shares - 1:
            grad_qkv = meet(grad_qkv, chain_up, *chains_qkv)
        chains_qkv.append(Chain(grad_qkv, order))
    sums = jnp.concatenate(
        [
            sums2[:6],
            grad_bias_qv.transpose(1, 0, 2).reshape(2, width),
            grad_bias_up.reshape(-1, width),
        ],
        0,
    )
    grad_heads = meet(grad_heads, *chains_qkv[1:])
    grad_tokens, sums = input_back(grad_heads, full_qkv, tokens, grad_mixed, vectors, sums)
    sums, act = meet((sums, act), chain_up, *chains_qkv)
    chain_small = Sum(sums, order_x)
    first = images // 2
    layer_out = shrink(0, first, kept_own, act, full_down, mixed, vectors)
    layer_out = meet(layer_out, chain_up, chain_small, *chains_qkv)
    layer_out = shrink(first, images - first, kept_own, act, full_down, mixed, vectors, layer_out)
    layer_out = meet(layer_out, chain_small, *chains_qkv)
    sent_up = jnp.concatenate([sent_first[:, :share], chain_up.finish()[0]], 1)
    sent_qkv = jnp.concatenate([chain.finish()[0] for chain in chains_qkv], 1)
    small = chain_small.finish()
    at_dp, at_tensor = lax.axis_index("dp"), lax.axis_index("tensor")
    row_place, shard_place = at_dp * shards + at_tensor, at_tensor * dp + at_dp
    rows_own = lax.dynamic_slice(small, (0, row_place * own), (6, own))
    heads_own = lax.dynamic_slice(small, (6, shard_place * own), (2, own))
    count = up_bias.shape[0]
    start = shard_place * count
    up_own = lax.dynamic_slice(small, (8 + start // width, start % width), (1, count))

    return (
        layer_out,
        grad_tokens,
        sent_qkv.astype(f32).reshape(part, 3, cols).transpose(1, 0, 2),
        sent_first[:, share:].astype(f32).T,
        sent_up.astype(f32),
        sent_down.astype(f32).T,
        heads_own,
        up_own.reshape(-1),
        rows_own[:2],
        rows_own[2:],
    )


def solution(mesh):
    both = P(("dp", "tensor"), None)
    matrices = (
        P(None, "dp", "tensor"),
        P("tensor", "dp"),
        P("dp", "tensor"),
        P("tensor", "dp"),
        P(None, ("tensor", "dp")),
        P(("tensor", "dp")),
        P(None, ("dp", "tensor")),
        P(None, ("dp", "tensor")),
    )
    return jax.shard_map(
        body,
        mesh=mesh,
        in_specs=(both, P("dp"), both) + matrices,
        out_specs=(both, both) + matrices,
        check_vma=False,
    )
```

```python
import functools

import jax
import jax.numpy as jnp
from jax import lax
from jax.experimental import pallas as pl
from jax.experimental.pallas import tpu as pltpu
from jax.sharding import PartitionSpec as P


HEAD_DIM = 64
BUFFER = 64
SEQ = 320
KEYS = 384
LANES = 128
EPSILON = 1e-06
SCALE = HEAD_DIM ** (-0.5)
LOG2E = 1.4426950408889634
NEGATIVE = -1000000000.0 / SCALE
VMEM = 40 << 20


f32 = jnp.float32
bf16 = jnp.bfloat16


def dot(left, right):
    return lax.dot_general(left, right, (((1,), (0,)), ((), ())), preferred_element_type=f32)


def dot_flip(left, right):
    return lax.dot_general(left, right, (((1,), (1,)), ((), ())), preferred_element_type=f32)


def split_heads(values):
    low = lax.broadcasted_iota(jnp.int32, (1, LANES), 1) < HEAD_DIM
    zero = jnp.zeros_like(values)
    return jnp.where(low, values, zero), jnp.where(low, zero, values)


def pad_keys(values):
    return jnp.concatenate([values, jnp.zeros((KEYS - SEQ, values.shape[1]), values.dtype)], 0)


def attend_kernel(kept_ref, q_ref, k_ref, v_ref, o_ref, e_ref, r_ref, *, pairs):
    valid = BUFFER + kept_ref[pl.program_id(1)]
    alive = lax.broadcasted_iota(jnp.int32, (1, KEYS), 1) < valid
    ones = split_heads(jnp.ones((KEYS, LANES), bf16))
    for pair in range(pairs):
        cols = slice(LANES * pair, LANES * (pair + 1))
        keys = pad_keys(k_ref[0, :, cols])
        values = split_heads(pad_keys(v_ref[0, :, cols]))
        expos = []
        for head, query in enumerate(split_heads(q_ref[0, :, cols])):
            scores = jnp.where(alive, dot_flip(query, keys), NEGATIVE)
            highest = jnp.max(scores, axis=-1, keepdims=True)
            expo = jnp.exp2((scores - highest) * (SCALE * LOG2E)).astype(bf16)
            e_ref[0, 0, pair, head] = expo
            expos.append(expo)
        right = jnp.concatenate(
            [jnp.concatenate([value, one], 1) for value, one in zip(values, ones)], 0
        )
        both = dot(jnp.concatenate(expos, 1), right)
        inverse = 1.0 / both[:, LANES:]
        o_ref[0, :, cols] = (both[:, :LANES] * inverse).astype(bf16)
        r_ref[0, :, cols] = inverse


def attend(qkv, kept):
    shards, rows, width = qkv.shape
    cols = width // 3
    pairs = cols // LANES
    images = rows // SEQ
    part = lambda which: pl.BlockSpec((1, SEQ, cols), lambda t, i, k: (t, i, which))
    probs = pl.BlockSpec((1, 1, pairs, 2, SEQ, KEYS), lambda t, i, k: (t, i, 0, 0, 0, 0))
    return pl.pallas_call(
        functools.partial(attend_kernel, pairs=pairs),
        grid_spec=pltpu.PrefetchScalarGridSpec(
            num_scalar_prefetch=1,
            grid=(shards, images),
            in_specs=[part(0), part(1), part(2)],
            out_specs=[part(0), probs, part(0)],
        ),
        out_shape=[
            jax.ShapeDtypeStruct((shards, rows, cols), bf16),
            jax.ShapeDtypeStruct((shards, images, pairs, 2, SEQ, KEYS), bf16),
            jax.ShapeDtypeStruct((shards, rows, cols), f32),
        ],
        name="attend",
        cost_estimate=cost(rows * cols * shards * SEQ * 16, qkv, qkv),
        compiler_params=pltpu.CompilerParams(
            dimension_semantics=("arbitrary", "arbitrary"), vmem_limit_bytes=VMEM
        ),
    )(kept, qkv, qkv, qkv)


def attend_back_kernel(q_ref, k_ref, v_ref, g_ref, o_ref, e_ref, r_ref, out_ref, bias_ref, *, pairs):
    width = pairs * LANES

    @pl.when(pl.program_id(1) == 0)
    def _():
        bias_ref[...] = jnp.zeros_like(bias_ref)

    for pair in range(pairs):
        cols = slice(LANES * pair, LANES * (pair + 1))
        query = q_ref[0, :, cols]
        values = pad_keys(v_ref[0, :, cols])
        grad = (g_ref[0, :, cols].astype(f32) * r_ref[0, :, cols]).astype(bf16)
        product = split_heads(grad.astype(f32) * o_ref[0, :, cols].astype(f32))
        grads = []
        for head, grad_head in enumerate(split_heads(grad)):
            inner = jnp.sum(product[head], axis=-1, keepdims=True)
            expo = e_ref[0, 0, pair, head].astype(f32)
            grads.append((expo * (dot_flip(grad_head, values) - inner)).astype(bf16))
        keys = jnp.concatenate(split_heads(pad_keys(k_ref[0, :, cols])), 0)
        grad_query = (dot(jnp.concatenate(grads, 1), keys) * SCALE).astype(bf16)
        query_flip, grad_flip = query.T, grad.T
        halves = [slice(HEAD_DIM * head, HEAD_DIM * (head + 1)) for head in range(2)]
        grad_key = jnp.concatenate([dot(query_flip[half], grads[h]) for h, half in enumerate(halves)], 0)
        grad_value = jnp.concatenate(
            [dot(grad_flip[half], e_ref[0, 0, pair, h]) for h, half in enumerate(halves)], 0
        )
        grad_key = (grad_key.T[:SEQ] * SCALE).astype(bf16)
        grad_value = grad_value.T[:SEQ].astype(bf16)
        for which, value in enumerate((grad_query, grad_key, grad_value)):
            start = which * width + LANES * pair
            out_ref[0, :, start : start + LANES] = value
        bias_ref[0, 0:1, cols] += jnp.sum(grad_query.astype(f32), axis=0, keepdims=True)
        bias_ref[0, 1:2, cols] += jnp.sum(grad_value.astype(f32), axis=0, keepdims=True)


def attend_back(qkv, grad, attn, expo, inverse):
    shards, rows, width = qkv.shape
    cols = width // 3
    pairs = cols // LANES
    images = rows // SEQ
    part = lambda which: pl.BlockSpec((1, SEQ, cols), lambda t, i: (t, i, which))
    probs = pl.BlockSpec((1, 1, pairs, 2, SEQ, KEYS), lambda t, i: (t, i, 0, 0, 0, 0))
    return pl.pallas_call(
        functools.partial(attend_back_kernel, pairs=pairs),
        grid=(shards, images),
        in_specs=[part(0), part(1), part(2), part(0), part(0), probs, part(0)],
        out_specs=[
            pl.BlockSpec((1, SEQ, width), lambda t, i: (t, i, 0)),
            pl.BlockSpec((1, 2, cols), lambda t, i: (t, 0, 0)),
        ],
        out_shape=[
            jax.ShapeDtypeStruct((shards, rows, width), bf16),
            jax.ShapeDtypeStruct((shards, 2, cols), f32),
        ],
        name="attend_back",
        cost_estimate=cost(rows * cols * shards * SEQ * 24, qkv, qkv, expo),
        compiler_params=pltpu.CompilerParams(
            dimension_semantics=("arbitrary", "arbitrary"), vmem_limit_bytes=VMEM
        ),
    )(qkv, qkv, qkv, grad, attn, expo, inverse)


def norm_parts(values):
    centred = values - jnp.mean(values, axis=-1, keepdims=True)
    inverse = lax.rsqrt(jnp.mean(centred * centred, axis=-1, keepdims=True) + EPSILON)
    return centred * inverse, inverse


def norm_back(grad_normed, normed, inverse):
    first = jnp.mean(grad_normed, axis=-1, keepdims=True)
    second = jnp.mean(grad_normed * normed, axis=-1, keepdims=True)
    return inverse * (grad_normed - first - normed * second)


def block_rows(rows):
    return next(size for size in (512, 320, rows) if rows % size == 0)


def cost(flops, *arrays):
    return pl.CostEstimate(
        flops=flops, transcendentals=0, bytes_accessed=sum(a.size * a.dtype.itemsize for a in arrays)
    )


def call(kernel, grid, in_specs, outs, prefetch=0, aliases=None, estimate=None):
    return pl.pallas_call(
        kernel,
        grid_spec=pltpu.PrefetchScalarGridSpec(
            num_scalar_prefetch=prefetch,
            grid=grid,
            in_specs=in_specs,
            out_specs=[pl.BlockSpec(block, index) for block, index, _, _ in outs],
        ),
        out_shape=[jax.ShapeDtypeStruct(shape, kind) for _, _, shape, kind in outs],
        input_output_aliases=aliases or {},
        cost_estimate=estimate,
        compiler_params=pltpu.CompilerParams(
            dimension_semantics=("arbitrary",) * len(grid), vmem_limit_bytes=VMEM
        ),
    )


def fixed(block, *index):
    return pl.BlockSpec(block, lambda *_: index, pipeline_mode=pl.Buffered(1))


GAIN1, GAIN2, SHIFT1, SHIFT2, SHIFT3, SHIFT4 = range(6)


def row(ref, index):
    return ref[index : index + 1, :]


def norm_in_kernel(x_ref, vec_ref, h_ref):
    normed, _ = norm_parts(x_ref[...].astype(f32))
    h_ref[...] = (normed * row(vec_ref, GAIN1) + row(vec_ref, SHIFT1)).astype(bf16)


def norm_in(tokens, vectors):
    rows, width = tokens.shape
    step = pl.BlockSpec((SEQ, width), lambda i: (i, 0))
    return call(
        norm_in_kernel,
        (rows // SEQ,),
        [step, fixed(vectors.shape, 0, 0)],
        [((SEQ, width), lambda i: (i, 0), (rows, width), bf16)],
        estimate=cost(16 * rows * width, tokens, tokens),
    )(tokens, vectors)[0]


def project_kernel(h_ref, w_ref, bias_ref, out_ref):
    for shard in range(out_ref.shape[0]):
        out_ref[shard] = (dot(h_ref[...], w_ref[shard]) + bias_ref[shard]).astype(bf16)


def project(h1, weights, bias):
    rows, width = h1.shape
    shards, _, cols = bias.shape
    size = block_rows(rows)
    return call(
        project_kernel,
        (rows // size,),
        [
            pl.BlockSpec((size, width), lambda i: (i, 0)),
            fixed((shards, width, cols), 0, 0, 0),
            fixed(bias.shape, 0, 0, 0),
        ],
        [((shards, size, cols), lambda i: (0, i, 0), (shards, rows, cols), bf16)],
        estimate=cost(2 * rows * width * cols * shards, h1, weights),
    )(h1, weights, bias)[0]


def mix_kernel(attn_ref, w_ref, x_ref, vec_ref, mixed_ref, h_ref):
    total = dot_flip(attn_ref[0], w_ref[0])
    for shard in range(1, attn_ref.shape[0]):
        total += dot_flip(attn_ref[shard], w_ref[shard])
    mixed = x_ref[...].astype(f32) + total + row(vec_ref, SHIFT3)
    normed, _ = norm_parts(mixed)
    mixed_ref[...] = mixed
    h_ref[...] = (normed * row(vec_ref, GAIN2) + row(vec_ref, SHIFT2)).astype(bf16)


def mix(attn, weights, tokens, vectors):
    shards, rows, cols = attn.shape
    width = tokens.shape[1]
    size = block_rows(rows)
    step = lambda i: (i, 0)
    return call(
        mix_kernel,
        (rows // size,),
        [
            pl.BlockSpec((shards, size, cols), lambda i: (0, i, 0)),
            fixed(weights.shape, 0, 0, 0),
            pl.BlockSpec((size, width), step),
            fixed(vectors.shape, 0, 0),
        ],
        [
            ((size, width), step, (rows, width), f32),
            ((size, width), step, (rows, width), bf16),
        ],
        estimate=cost(2 * rows * width * cols * shards, attn, tokens),
    )(attn, weights, tokens, vectors)


GELU_IN = 0.7978845608
GELU_CUBE = 0.044715


def gelu_parts(pre):
    cube = (GELU_IN * GELU_CUBE) * (pre * pre)
    half = 0.5 * jnp.tanh(pre * (GELU_IN + cube)) + 0.5
    act = pre * half
    return act, half + (act - act * half) * (2.0 * GELU_IN + 6.0 * cube)


CHUNK = 512


def expand_kernel(h_ref, w_ref, bias_ref, act_ref, slope_ref):
    cols = act_ref.shape[2]
    chunk = min(CHUNK, cols)
    for start in range(0, cols, chunk):
        part = slice(start, start + chunk)
        act, slope = gelu_parts(dot(h_ref[...], w_ref[0, :, part]) + bias_ref[0, :, part])
        act_ref[0, :, part] = act.astype(bf16)
        slope_ref[0, :, part] = slope.astype(bf16)


def expand(h2, weights, bias):
    rows, width = h2.shape
    shards, _, cols = weights.shape
    size = block_rows(rows)
    out = ((1, size, cols), lambda t, i: (t, i, 0), (shards, rows, cols), bf16)
    return call(
        expand_kernel,
        (shards, rows // size),
        [
            pl.BlockSpec((size, width), lambda t, i: (i, 0)),
            pl.BlockSpec((1, width, cols), lambda t, i: (t, 0, 0)),
            pl.BlockSpec((1, 1, cols), lambda t, i: (t, 0, 0)),
        ],
        [out, out],
        estimate=cost(3 * rows * width * cols * shards, h2, weights),
    )(h2, weights, bias)


def expand_back_kernel(g_ref, w_ref, slope_ref, out_ref, bias_ref):
    @pl.when(pl.program_id(1) == 0)
    def _():
        bias_ref[...] = jnp.zeros_like(bias_ref)

    cols = out_ref.shape[2]
    chunk = min(CHUNK, cols)
    for start in range(0, cols, chunk):
        part = slice(start, start + chunk)
        grad = (dot(g_ref[...], w_ref[0, :, part]) * slope_ref[0, :, part].astype(f32)).astype(bf16)
        out_ref[0, :, part] = grad
        bias_ref[0, :, part] += jnp.sum(grad.astype(f32), axis=0, keepdims=True)


def expand_back(grad, weights, slope):
    rows, width = grad.shape
    shards, _, cols = weights.shape
    size = block_rows(rows)
    step = lambda t, i: (t, i, 0)
    return call(
        expand_back_kernel,
        (shards, rows // size),
        [
            pl.BlockSpec((size, width), lambda t, i: (i, 0)),
            pl.BlockSpec((1, width, cols), lambda t, i: (t, 0, 0)),
            pl.BlockSpec((1, size, cols), step),
        ],
        [
            ((1, size, cols), step, (shards, rows, cols), bf16),
            ((1, 1, cols), lambda t, i: (t, 0, 0), (shards, 1, cols), f32),
        ],
        estimate=cost(2 * rows * width * cols * shards, slope, slope),
    )(grad, weights, slope)


def dot_rows(left, right):
    return lax.dot_general(left, right, (((0,), (0,)), ((), ())), preferred_element_type=f32)


def weight_grad_kernel(left_ref, right_ref, out_ref, *, chunk, fill):
    which = pl.program_id(1)
    start = pl.multiple_of(which * chunk, chunk)
    out_ref[0, :, pl.ds(start, chunk)] = dot_rows(left_ref[...], right_ref[0]).astype(bf16)
    if fill:

        @pl.when(which == 0)
        def _():
            spare = jnp.zeros((out_ref.shape[1], fill), bf16)
            out_ref[0, :, out_ref.shape[2] - fill :] = spare


def weight_grad(left, right, spare):
    rows, width = left.shape
    shards, _, used = right.shape
    chunk = min(512, used)
    block = (1, width, used + spare)
    return call(
        functools.partial(weight_grad_kernel, chunk=chunk, fill=spare),
        (shards, used // chunk),
        [
            fixed((rows, width), 0, 0),
            pl.BlockSpec((1, rows, chunk), lambda t, n: (t, 0, n)),
        ],
        [(block, lambda t, n: (t, 0, 0), (shards,) + block[1:], bf16)],
        estimate=cost(2 * rows * width * used * shards, left, right),
    )(left, right)[0]


def weight_grad_into_kernel(left_ref, right_ref, _, out_ref):
    out_ref[0] = dot_rows(left_ref[...], right_ref[0]).astype(bf16)


def weight_grad_into(left, right, out):
    rows, width = left.shape
    shards, _, cols = right.shape
    place = out.shape[2] // cols - 1
    return call(
        weight_grad_into_kernel,
        (shards,),
        [
            fixed((rows, width), 0, 0),
            pl.BlockSpec((1, rows, cols), lambda t: (t, 0, 0)),
            pl.BlockSpec(memory_space=pl.ANY),
        ],
        [((1, width, cols), lambda t: (t, 0, place), out.shape, bf16)],
        aliases={2: 0},
        estimate=cost(2 * rows * width * cols * shards, left, right),
    )(left, right, out)[0]


def weight_grad_slots_kernel(slot_ref, left_ref, right_ref, out_ref, *, owners):
    grad = dot_rows(left_ref[...], right_ref[0]).astype(bf16)
    part = out_ref.shape[1]
    for owner in range(owners):
        slot = slot_ref[pl.program_id(1) * owners + owner]
        out_ref[slot] = grad[owner * part : (owner + 1) * part]


def weight_grad_slots(left, right, which, shares, slots):
    rows, width = left.shape
    shards, _, cols = right.shape
    share = cols // shares
    count = slots.shape[0]
    owners = count // shards
    part = width // owners
    chunk = share if share <= 1024 else 512
    first = which * share // chunk
    return call(
        functools.partial(weight_grad_slots_kernel, owners=owners),
        (share // chunk, shards),
        [
            fixed((rows, width), 0, 0),
            pl.BlockSpec((1, rows, chunk), lambda n, t, s: (t, 0, first + n)),
        ],
        [((count, part, chunk), lambda n, t, s: (0, 0, n), (count, part, share), bf16)],
        prefetch=1,
        estimate=cost(2 * rows * width * share * shards, left, right),
    )(slots, left, right)[0]


def weight_grad_halves_kernel(slot_ref, left_ref, right_ref, first_ref, second_ref, *, owners, steps):
    grad = dot_rows(left_ref[...], right_ref[0]).astype(bf16)

    @pl.when(pl.program_id(0) < steps)
    def _():
        first_ref[0] = grad

    @pl.when(pl.program_id(0) >= steps)
    def _():
        part = second_ref.shape[1]
        for owner in range(owners):
            slot = slot_ref[pl.program_id(1) * owners + owner]
            second_ref[slot] = grad[owner * part : (owner + 1) * part]


def weight_grad_halves(left, right, spare, slots):
    rows, width = left.shape
    shards, _, cols = right.shape
    half = cols // 2
    count = slots.shape[0]
    owners = count // shards
    part = width // owners
    chunk = min(512, half)
    steps = half // chunk
    early = lambda n, value, last: jnp.where(n < steps, value, last)
    return call(
        functools.partial(weight_grad_halves_kernel, owners=owners, steps=steps),
        (2 * steps, shards),
        [
            fixed((rows, width), 0, 0),
            pl.BlockSpec((1, rows, chunk), lambda n, t, s: (t, 0, n)),
        ],
        [
            (
                (1, width, chunk),
                lambda n, t, s: (early(n, t, shards - 1), 0, early(n, n, steps - 1)),
                (shards, width, half + spare),
                bf16,
            ),
            (
                (count, part, chunk),
                lambda n, t, s: (0, 0, jnp.maximum(n - steps, 0)),
                (count, part, half),
                bf16,
            ),
        ],
        prefetch=1,
        estimate=cost(2 * rows * width * cols * shards, left, right),
    )(slots, left, right)


def middle_back_kernel(
    g_ref, up_ref, mixed_ref, gm_ref, vec_ref, out_w_ref, gmixed_ref, go_ref, gattn_ref, sums_ref
):
    @pl.when(pl.program_id(0) == 0)
    def _():
        sums_ref[...] = jnp.zeros_like(sums_ref)

    grad_h = dot_flip(g_ref[0], up_ref[0])
    for shard in range(1, g_ref.shape[0]):
        grad_h += dot_flip(g_ref[shard], up_ref[shard])
    normed, inverse = norm_parts(mixed_ref[...])
    grad = gm_ref[...].astype(f32)
    grad_mixed = grad + norm_back(grad_h * row(vec_ref, GAIN2), normed, inverse)
    gmixed_ref[...] = grad_mixed
    rounded = grad_mixed.astype(bf16)
    go_ref[...] = rounded
    for index, value in ((1, grad_h * normed), (3, grad_h), (4, grad_mixed), (5, grad)):
        sums_ref[index : index + 1, :] += jnp.sum(value, axis=0, keepdims=True)
    for shard in range(gattn_ref.shape[0]):
        gattn_ref[shard] = dot(rounded, out_w_ref[shard]).astype(bf16)


def middle_back(grad_pre, up, mixed, grad_m, vectors, weights):
    shards, rows, cols = grad_pre.shape
    width = mixed.shape[1]
    heads = weights.shape[2]
    step = lambda i: (i, 0)
    wide = pl.BlockSpec((SEQ, width), step)
    return call(
        middle_back_kernel,
        (rows // SEQ,),
        [
            pl.BlockSpec((shards, SEQ, cols), lambda i: (0, i, 0)),
            fixed(up.shape, 0, 0, 0),
            wide,
            wide,
            fixed(vectors.shape, 0, 0),
            fixed(weights.shape, 0, 0, 0),
        ],
        [
            ((SEQ, width), step, (rows, width), f32),
            ((SEQ, width), step, (rows, width), bf16),
            ((shards, SEQ, heads), lambda i: (0, i, 0), (shards, rows, heads), bf16),
            ((8, width), lambda i: (0, 0), (8, width), f32),
        ],
        estimate=cost(2 * rows * width * (cols + heads) * shards, grad_pre, up, mixed),
    )(grad_pre, up, mixed, grad_m, vectors, weights)


def input_back_kernel(g_ref, w_ref, x_ref, gmixed_ref, vec_ref, before_ref, out_ref, sums_ref):
    @pl.when(pl.program_id(0) == 0)
    def _():
        sums_ref[...] = before_ref[...]

    grad_h = dot_flip(g_ref[0], w_ref[0])
    for shard in range(1, g_ref.shape[0]):
        grad_h += dot_flip(g_ref[shard], w_ref[shard])
    normed, inverse = norm_parts(x_ref[...].astype(f32))
    out_ref[...] = gmixed_ref[...] + norm_back(grad_h * row(vec_ref, GAIN1), normed, inverse)
    for index, value in ((0, grad_h * normed), (2, grad_h)):
        sums_ref[index : index + 1, :] += jnp.sum(value, axis=0, keepdims=True)


def input_back(grad_heads, weights, tokens, grad_mixed, vectors, sums):
    shards, rows, cols = grad_heads.shape
    width = tokens.shape[1]
    step = lambda i: (i, 0)
    wide = pl.BlockSpec((SEQ, width), step)
    return call(
        input_back_kernel,
        (rows // SEQ,),
        [
            pl.BlockSpec((shards, SEQ, cols), lambda i: (0, i, 0)),
            fixed(weights.shape, 0, 0, 0),
            wide,
            wide,
            fixed(vectors.shape, 0, 0),
            fixed(sums.shape, 0, 0),
        ],
        [
            ((SEQ, width), step, (rows, width), f32),
            (sums.shape, lambda i: (0, 0), sums.shape, f32),
        ],
        estimate=cost(2 * rows * width * cols * shards, weights, tokens, grad_mixed),
    )(grad_heads, weights, tokens, grad_mixed, vectors, sums)


def shrink_kernel(kept_ref, act_ref, w_ref, mixed_ref, vec_ref, *refs, first):
    out_ref = refs[-1]
    total = dot_flip(act_ref[0], w_ref[0])
    for shard in range(1, act_ref.shape[0]):
        total += dot_flip(act_ref[shard], w_ref[shard])
    valid = BUFFER + kept_ref[first + pl.program_id(0)]
    alive = lax.broadcasted_iota(jnp.int32, (SEQ, 1), 0) < valid
    result = mixed_ref[...] + total + row(vec_ref, SHIFT4)
    out_ref[...] = jnp.where(alive, result, 0.0).astype(bf16)


def shrink(first, count, kept, act, weights, mixed, vectors, *out):
    shards, rows, cols = act.shape
    width = mixed.shape[1]
    step = lambda i, k: (first + i, 0)
    return call(
        functools.partial(shrink_kernel, first=first),
        (count,),
        [
            pl.BlockSpec((shards, SEQ, cols), lambda i, k: (0, first + i, 0)),
            fixed(weights.shape, 0, 0, 0),
            pl.BlockSpec((SEQ, width), step),
            fixed(vectors.shape, 0, 0),
        ]
        + [pl.BlockSpec(memory_space=pl.ANY)] * len(out),
        [((SEQ, width), step, (rows, width), bf16)],
        prefetch=1,
        aliases={5: 0} if out else None,
        estimate=cost(2 * count * SEQ * width * cols * shards, weights),
    )(kept, act, weights, mixed, vectors, *out)[0]


def swap(values, axis, bit):
    places = range(lax.axis_size(axis))
    return lax.ppermute(values, axis, [(place, place ^ bit) for place in places])


def bits_of(axis):
    return [1 << power for power in range(lax.axis_size(axis).bit_length() - 1)]


def flip_gather(part, order):
    dp, shards = lax.axis_size("dp"), lax.axis_size("tensor")
    values = part[None]
    index = jnp.arange(shards * dp, dtype=jnp.int32)
    apart = {
        "tensor": (index // dp) ^ lax.axis_index("tensor").astype(jnp.int32),
        "dp": (index % dp) ^ lax.axis_index("dp").astype(jnp.int32),
    }
    place = jnp.zeros_like(index)
    for axis, bit in order:
        place += jnp.where((apart[axis] & bit) != 0, values.shape[0], 0)
        values = jnp.concatenate([values, swap(values, axis, bit)], 0)
    return jnp.take(values, place, axis=0)


def slot_table(order):
    dp, shards = lax.axis_size("dp"), lax.axis_size("tensor")
    index = jnp.arange(shards * dp, dtype=jnp.int32)
    apart = {
        "tensor": (index // dp) ^ lax.axis_index("tensor").astype(jnp.int32),
        "dp": (index % dp) ^ lax.axis_index("dp").astype(jnp.int32),
    }
    slot = jnp.zeros_like(index)
    for depth, (axis, bit) in enumerate(order):
        slot += jnp.where((apart[axis] & bit) != 0, 1 << (len(order) - 1 - depth), 0)
    return slot


class Chain:
    def __init__(self, values, order):
        self.values, self.order = values, list(order)
        self.send()

    def send(self):
        half = self.values.shape[0] // 2
        self.near = self.values[:half]
        self.far = swap(self.values[half:], *self.order.pop(0))

    def settle(self):
        self.values = self.near + self.far

    def finish(self):
        self.settle()
        while self.order:
            self.send()
            self.settle()
        return self.values


class Sum(Chain):
    def __init__(self, values, order):
        super().__init__(values, [order[at : at + 2] for at in range(0, len(order), 2)])

    def send(self):
        shards = lax.axis_size("tensor")
        places = range(lax.axis_size("dp") * shards)
        masks = [0]
        for axis, bit in self.order.pop(0):
            masks += [mask ^ (bit * shards if axis == "dp" else bit) for mask in masks]
        self.far = [
            lax.ppermute(self.values, ("dp", "tensor"), [(place, place ^ mask) for place in places])
            for mask in masks[1:]
        ]

    def settle(self):
        self.values = sum(self.far, self.values)


def meet(values, *chains):
    values, far = lax.optimization_barrier((values, [chain.far for chain in chains]))
    for chain, arrived in zip(chains, far):
        chain.far = arrived
        chain.settle()
        if chain.order:
            chain.send()
    return values


def gather(part):
    full = lax.all_gather(part, ("tensor", "dp"), axis=0, tiled=True)
    return full.reshape(lax.axis_size("tensor"), -1, part.shape[1])


def scatter(full):
    flat = full.reshape(-1, full.shape[2])
    return lax.psum_scatter(flat, ("tensor", "dp"), scatter_dimension=0, tiled=True)


def body(tokens, kept, cotangent, w_qkv, w_out, w_up, w_down, qv_bias, up_bias, ln_gain, shift):
    rows, width = tokens.shape
    dp, shards = lax.axis_size("dp"), lax.axis_size("tensor")
    images = rows // SEQ
    part = w_qkv.shape[1]
    cols = w_qkv.shape[2]
    own = ln_gain.shape[1]
    barrier = lax.optimization_barrier

    core, along_x = [("dp", 1)], [("tensor", bit) for bit in bits_of("tensor")[::-1]]
    low, high = [("dp", 2)], [("dp", bit) for bit in bits_of("dp")[::-1] if bit > 2]
    order_x, order_low = core + along_x + low + high, core + low + high + along_x

    full_qkv = gather(w_qkv.transpose(1, 0, 2).reshape(part, 3 * cols))
    full_up = gather(w_up)
    full_down = gather(w_down.T)

    small = jnp.concatenate(
        [ln_gain, shift, qv_bias.astype(f32), up_bias.astype(f32).reshape(-1, own)], 0
    )
    small = flip_gather(small, high + low + along_x + core)
    small = small.reshape((shards, dp) + small.shape[1:])
    vectors = small[:, :, :6].transpose(2, 1, 0, 3).reshape(6, width)
    vectors = jnp.concatenate([vectors, jnp.zeros((2, width), f32)], 0)
    bias_qv = small[:, :, 6:8].transpose(0, 2, 1, 3).reshape(shards, 2, cols)
    bias_up = small[:, :, 8:].reshape(shards, 1, -1)
    bias_heads = jnp.concatenate([bias_qv[:, :1], jnp.zeros_like(bias_qv[:, :1]), bias_qv[:, 1:]], 2)
    full_out = flip_gather(w_out.T, high + low + along_x + core).reshape(shards, width, cols)

    first_image = lax.axis_index("tensor") * images
    kept_own = lax.dynamic_slice_in_dim(kept, first_image, images, 0)
    positions = jnp.arange(SEQ, dtype=jnp.int32)
    alive = (positions[None, :] < BUFFER + kept_own[:, None]).reshape(rows, 1)
    grad_m = jnp.where(alive, cotangent, jnp.zeros_like(cotangent))

    tables = [slot_table(order_x), slot_table(order_low)]

    h1 = norm_in(tokens, vectors)
    qkv = project(h1, full_qkv, bias_heads)
    attn, expo, inverse_sum = attend(qkv, kept_own)
    mixed, h2 = mix(attn, full_out, tokens, vectors)
    act, slope = expand(h2, full_up, bias_up)

    hidden = act.shape[2]
    grad_down = weight_grad(grad_m, act, hidden // 8)
    grad_m, grad_down = barrier((grad_m, grad_down))
    sent_down = scatter(grad_down)[:, :hidden]
    grad_pre, grad_bias_up = expand_back(grad_m, full_down, slope)

    share = hidden // 2
    grad_first, grad_second = weight_grad_halves(h2, grad_pre, cols, tables[0])
    grad_pre, grad_first, grad_second = barrier((grad_pre, grad_first, grad_second))
    chain_up = Chain(grad_second, order_x)
    grad_mixed, grad_o, grad_attn, sums2 = middle_back(
        grad_pre, full_up, mixed, grad_m, vectors, full_out
    )
    grad_o = meet(grad_o, chain_up)
    grad_first = weight_grad_into(grad_o, attn, grad_first)
    grad_attn, grad_first = barrier((grad_attn, grad_first))
    sent_first = scatter(grad_first)
    grad_heads, grad_bias_qv = attend_back(qkv, grad_attn, attn, expo, inverse_sum)
    grad_heads = meet(grad_heads, chain_up)
    grad_heads, sent_down = barrier((grad_heads, sent_down))

    chains_qkv = []
    shares = 2 if (3 * cols // 2) % LANES == 0 else 1
    for which, order in enumerate((order_x, order_low)[:shares]):
        grad_qkv = weight_grad_slots(h1, grad_heads, which, shares, tables[which])
        grad_heads, grad_qkv = barrier((grad_heads, grad_qkv))
        if which == shares - 1:
            grad_qkv = meet(grad_qkv, chain_up, *chains_qkv)
        chains_qkv.append(Chain(grad_qkv, order))
    sums = jnp.concatenate(
        [
            sums2[:6],
            grad_bias_qv.transpose(1, 0, 2).reshape(2, width),
            grad_bias_up.reshape(-1, width),
        ],
        0,
    )
    grad_heads = meet(grad_heads, *chains_qkv[1:])
    grad_tokens, sums = input_back(grad_heads, full_qkv, tokens, grad_mixed, vectors, sums)
    sums, act = meet((sums, act), chain_up, *chains_qkv)
    chain_small = Sum(sums, order_x)
    first = images // 2
    layer_out = shrink(0, first, kept_own, act, full_down, mixed, vectors)
    layer_out = meet(layer_out, chain_up, chain_small, *chains_qkv)
    layer_out = shrink(first, images - first, kept_own, act, full_down, mixed, vectors, layer_out)
    layer_out = meet(layer_out, chain_small, *chains_qkv)
    sent_up = jnp.concatenate([sent_first[:, :share], chain_up.finish()[0]], 1)
    sent_qkv = jnp.concatenate([chain.finish()[0] for chain in chains_qkv], 1)
    small = chain_small.finish()
    at_dp, at_tensor = lax.axis_index("dp"), lax.axis_index("tensor")
    row_place, shard_place = at_dp * shards + at_tensor, at_tensor * dp + at_dp
    rows_own = lax.dynamic_slice(small, (0, row_place * own), (6, own))
    heads_own = lax.dynamic_slice(small, (6, shard_place * own), (2, own))
    count = up_bias.shape[0]
    start = shard_place * count
    up_own = lax.dynamic_slice(small, (8 + start // width, start % width), (1, count))

    return (
        layer_out,
        grad_tokens,
        sent_qkv.astype(f32).reshape(part, 3, cols).transpose(1, 0, 2),
        sent_first[:, share:].astype(f32).T,
        sent_up.astype(f32),
        sent_down.astype(f32).T,
        heads_own,
        up_own.reshape(-1),
        rows_own[:2],
        rows_own[2:],
    )


def solution(mesh):
    both = P(("dp", "tensor"), None)
    matrices = (
        P(None, "dp", "tensor"),
        P("tensor", "dp"),
        P("dp", "tensor"),
        P("tensor", "dp"),
        P(None, ("tensor", "dp")),
        P(("tensor", "dp")),
        P(None, ("dp", "tensor")),
        P(None, ("dp", "tensor")),
    )
    return jax.shard_map(
        body,
        mesh=mesh,
        in_specs=(both, P("dp"), both) + matrices,
        out_specs=(both, both) + matrices,
        check_vma=False,
    )
```

```python
import functools

import jax
import jax.numpy as jnp
from jax import lax
from jax.experimental import pallas as pl
from jax.experimental.pallas import tpu as pltpu
from jax.sharding import PartitionSpec as P


HEAD_DIM = 64
BUFFER = 64
SEQ = 320
KEYS = 384
LANES = 128
EPSILON = 1e-06
SCALE = HEAD_DIM ** (-0.5)
LOG2E = 1.4426950408889634
NEGATIVE = -1000000000.0 / SCALE
VMEM = 40 << 20
WHOLE_VMEM = 56 << 20
STREAMING = ("project", "expand", "expand_back", "input_back")


f32 = jnp.float32
bf16 = jnp.bfloat16


def dot(left, right):
    return lax.dot_general(left, right, (((1,), (0,)), ((), ())), preferred_element_type=f32)


def dot_flip(left, right):
    return lax.dot_general(left, right, (((1,), (1,)), ((), ())), preferred_element_type=f32)


def split_heads(values):
    low = lax.broadcasted_iota(jnp.int32, (1, LANES), 1) < HEAD_DIM
    zero = jnp.zeros_like(values)
    return jnp.where(low, values, zero), jnp.where(low, zero, values)


def pad_keys(values):
    return jnp.concatenate([values, jnp.zeros((KEYS - SEQ, values.shape[1]), values.dtype)], 0)


def attend_kernel(kept_ref, q_ref, k_ref, v_ref, o_ref, e_ref, r_ref, *, pairs):
    valid = BUFFER + kept_ref[pl.program_id(1)]
    alive = lax.broadcasted_iota(jnp.int32, (1, KEYS), 1) < valid
    ones = split_heads(jnp.ones((KEYS, LANES), bf16))
    for pair in range(pairs):
        cols = slice(LANES * pair, LANES * (pair + 1))
        keys = pad_keys(k_ref[0, :, cols])
        values = split_heads(pad_keys(v_ref[0, :, cols]))
        expos = []
        for head, query in enumerate(split_heads(q_ref[0, :, cols])):
            scores = jnp.where(alive, dot_flip(query, keys), NEGATIVE)
            highest = jnp.max(scores, axis=-1, keepdims=True)
            expo = jnp.exp2((scores - highest) * (SCALE * LOG2E)).astype(bf16)
            e_ref[0, 0, pair, head] = expo
            expos.append(expo)
        right = jnp.concatenate(
            [jnp.concatenate([value, one], 1) for value, one in zip(values, ones)], 0
        )
        both = dot(jnp.concatenate(expos, 1), right)
        inverse = 1.0 / both[:, LANES:]
        o_ref[0, :, cols] = (both[:, :LANES] * inverse).astype(bf16)
        r_ref[0, :, cols] = inverse


def attend(qkv, kept):
    shards, rows, width = qkv.shape
    cols = width // 3
    pairs = cols // LANES
    images = rows // SEQ
    part = lambda which: pl.BlockSpec((1, SEQ, cols), lambda t, i, k: (t, i, which))
    probs = pl.BlockSpec((1, 1, pairs, 2, SEQ, KEYS), lambda t, i, k: (t, i, 0, 0, 0, 0))
    return pl.pallas_call(
        functools.partial(attend_kernel, pairs=pairs),
        grid_spec=pltpu.PrefetchScalarGridSpec(
            num_scalar_prefetch=1,
            grid=(shards, images),
            in_specs=[part(0), part(1), part(2)],
            out_specs=[part(0), probs, part(0)],
        ),
        out_shape=[
            jax.ShapeDtypeStruct((shards, rows, cols), bf16),
            jax.ShapeDtypeStruct((shards, images, pairs, 2, SEQ, KEYS), bf16),
            jax.ShapeDtypeStruct((shards, rows, cols), f32),
        ],
        name="attend",
        cost_estimate=cost(rows * cols * shards * SEQ * 16, qkv, qkv),
        compiler_params=pltpu.CompilerParams(
            dimension_semantics=("arbitrary", "arbitrary"), vmem_limit_bytes=VMEM
        ),
    )(kept, qkv, qkv, qkv)


def attend_back_kernel(q_ref, k_ref, v_ref, g_ref, o_ref, e_ref, r_ref, out_ref, bias_ref, *, pairs):
    width = pairs * LANES

    @pl.when(pl.program_id(1) == 0)
    def _():
        bias_ref[...] = jnp.zeros_like(bias_ref)

    for pair in range(pairs):
        cols = slice(LANES * pair, LANES * (pair + 1))
        query = q_ref[0, :, cols]
        values = pad_keys(v_ref[0, :, cols])
        grad = (g_ref[0, :, cols].astype(f32) * r_ref[0, :, cols]).astype(bf16)
        product = split_heads(grad.astype(f32) * o_ref[0, :, cols].astype(f32))
        grads = []
        for head, grad_head in enumerate(split_heads(grad)):
            inner = jnp.sum(product[head], axis=-1, keepdims=True)
            expo = e_ref[0, 0, pair, head].astype(f32)
            grads.append((expo * (dot_flip(grad_head, values) - inner)).astype(bf16))
        keys = jnp.concatenate(split_heads(pad_keys(k_ref[0, :, cols])), 0)
        grad_query = (dot(jnp.concatenate(grads, 1), keys) * SCALE).astype(bf16)
        query_flip, grad_flip = query.T, grad.T
        halves = [slice(HEAD_DIM * head, HEAD_DIM * (head + 1)) for head in range(2)]
        grad_key = jnp.concatenate([dot(query_flip[half], grads[h]) for h, half in enumerate(halves)], 0)
        grad_value = jnp.concatenate(
            [dot(grad_flip[half], e_ref[0, 0, pair, h]) for h, half in enumerate(halves)], 0
        )
        grad_key = (grad_key.T[:SEQ] * SCALE).astype(bf16)
        grad_value = grad_value.T[:SEQ].astype(bf16)
        for which, value in enumerate((grad_query, grad_key, grad_value)):
            start = which * width + LANES * pair
            out_ref[0, :, start : start + LANES] = value
        bias_ref[0, 0:1, cols] += jnp.sum(grad_query.astype(f32), axis=0, keepdims=True)
        bias_ref[0, 1:2, cols] += jnp.sum(grad_value.astype(f32), axis=0, keepdims=True)


def attend_back(qkv, grad, attn, expo, inverse):
    shards, rows, width = qkv.shape
    cols = width // 3
    pairs = cols // LANES
    images = rows // SEQ
    part = lambda which: pl.BlockSpec((1, SEQ, cols), lambda t, i: (t, i, which))
    probs = pl.BlockSpec((1, 1, pairs, 2, SEQ, KEYS), lambda t, i: (t, i, 0, 0, 0, 0))
    return pl.pallas_call(
        functools.partial(attend_back_kernel, pairs=pairs),
        grid=(shards, images),
        in_specs=[part(0), part(1), part(2), part(0), part(0), probs, part(0)],
        out_specs=[
            pl.BlockSpec((1, SEQ, width), lambda t, i: (t, i, 0)),
            pl.BlockSpec((1, 2, cols), lambda t, i: (t, 0, 0)),
        ],
        out_shape=[
            jax.ShapeDtypeStruct((shards, rows, width), bf16),
            jax.ShapeDtypeStruct((shards, 2, cols), f32),
        ],
        name="attend_back",
        cost_estimate=cost(rows * cols * shards * SEQ * 24, qkv, qkv, expo),
        compiler_params=pltpu.CompilerParams(
            dimension_semantics=("arbitrary", "arbitrary"), vmem_limit_bytes=WHOLE_VMEM
        ),
    )(qkv, qkv, qkv, grad, attn, expo, inverse)


def norm_parts(values):
    centred = values - jnp.mean(values, axis=-1, keepdims=True)
    inverse = lax.rsqrt(jnp.mean(centred * centred, axis=-1, keepdims=True) + EPSILON)
    return centred * inverse, inverse


def norm_back(grad_normed, normed, inverse):
    first = jnp.mean(grad_normed, axis=-1, keepdims=True)
    second = jnp.mean(grad_normed * normed, axis=-1, keepdims=True)
    return inverse * (grad_normed - first - normed * second)


def block_rows(rows):
    return next(size for size in (512, 320, rows) if rows % size == 0)


def cost(flops, *arrays):
    return pl.CostEstimate(
        flops=flops, transcendentals=0, bytes_accessed=sum(a.size * a.dtype.itemsize for a in arrays)
    )


def call(kernel, name, grid, in_specs, outs, prefetch=0, aliases=None, estimate=None):
    return pl.pallas_call(
        kernel,
        grid_spec=pltpu.PrefetchScalarGridSpec(
            num_scalar_prefetch=prefetch,
            grid=grid,
            in_specs=in_specs,
            out_specs=[pl.BlockSpec(block, index) for block, index, _, _ in outs],
        ),
        out_shape=[jax.ShapeDtypeStruct(shape, kind) for _, _, shape, kind in outs],
        input_output_aliases=aliases or {},
        cost_estimate=estimate,
        compiler_params=pltpu.CompilerParams(
            dimension_semantics=("arbitrary",) * len(grid),
            vmem_limit_bytes=WHOLE_VMEM if name in STREAMING else VMEM,
        ),
    )


def fixed(block, *index):
    return pl.BlockSpec(block, lambda *_: index, pipeline_mode=pl.Buffered(1))


GAIN1, GAIN2, SHIFT1, SHIFT2, SHIFT3, SHIFT4 = range(6)


def row(ref, index):
    return ref[index : index + 1, :]


def norm_in_kernel(x_ref, vec_ref, h_ref):
    normed, _ = norm_parts(x_ref[...].astype(f32))
    h_ref[...] = (normed * row(vec_ref, GAIN1) + row(vec_ref, SHIFT1)).astype(bf16)


def norm_in(tokens, vectors):
    rows, width = tokens.shape
    step = pl.BlockSpec((SEQ, width), lambda i: (i, 0))
    return call(
        norm_in_kernel,
        "norm_in",
        (rows // SEQ,),
        [step, fixed(vectors.shape, 0, 0)],
        [((SEQ, width), lambda i: (i, 0), (rows, width), bf16)],
        estimate=cost(16 * rows * width, tokens, tokens),
    )(tokens, vectors)[0]


def project_kernel(h_ref, w_ref, bias_ref, out_ref):
    for shard in range(out_ref.shape[0]):
        out_ref[shard] = (dot(h_ref[...], w_ref[shard]) + bias_ref[shard]).astype(bf16)


def project(h1, weights, bias):
    rows, width = h1.shape
    shards, _, cols = bias.shape
    size = block_rows(rows)
    return call(
        project_kernel,
        "project",
        (rows // size,),
        [
            pl.BlockSpec((size, width), lambda i: (i, 0)),
            fixed((shards, width, cols), 0, 0, 0),
            fixed(bias.shape, 0, 0, 0),
        ],
        [((shards, size, cols), lambda i: (0, i, 0), (shards, rows, cols), bf16)],
        estimate=cost(2 * rows * width * cols * shards, h1, weights),
    )(h1, weights, bias)[0]


def mix_kernel(attn_ref, w_ref, x_ref, vec_ref, mixed_ref, h_ref):
    total = dot_flip(attn_ref[0], w_ref[0])
    for shard in range(1, attn_ref.shape[0]):
        total += dot_flip(attn_ref[shard], w_ref[shard])
    mixed = x_ref[...].astype(f32) + total + row(vec_ref, SHIFT3)
    normed, _ = norm_parts(mixed)
    mixed_ref[...] = mixed
    h_ref[...] = (normed * row(vec_ref, GAIN2) + row(vec_ref, SHIFT2)).astype(bf16)


def mix(attn, weights, tokens, vectors):
    shards, rows, cols = attn.shape
    width = tokens.shape[1]
    size = block_rows(rows)
    step = lambda i: (i, 0)
    return call(
        mix_kernel,
        "mix",
        (rows // size,),
        [
            pl.BlockSpec((shards, size, cols), lambda i: (0, i, 0)),
            fixed(weights.shape, 0, 0, 0),
            pl.BlockSpec((size, width), step),
            fixed(vectors.shape, 0, 0),
        ],
        [
            ((size, width), step, (rows, width), f32),
            ((size, width), step, (rows, width), bf16),
        ],
        estimate=cost(2 * rows * width * cols * shards, attn, tokens),
    )(attn, weights, tokens, vectors)


GELU_IN = 0.7978845608
GELU_CUBE = 0.044715


def gelu_parts(pre):
    cube = (GELU_IN * GELU_CUBE) * (pre * pre)
    half = 0.5 * jnp.tanh(pre * (GELU_IN + cube)) + 0.5
    act = pre * half
    return act, half + (act - act * half) * (2.0 * GELU_IN + 6.0 * cube)


CHUNK = 512


def expand_kernel(h_ref, w_ref, bias_ref, act_ref, slope_ref):
    cols = act_ref.shape[2]
    chunk = min(CHUNK, cols)
    for start in range(0, cols, chunk):
        part = slice(start, start + chunk)
        act, slope = gelu_parts(dot(h_ref[...], w_ref[0, :, part]) + bias_ref[0, :, part])
        act_ref[0, :, part] = act.astype(bf16)
        slope_ref[0, :, part] = slope.astype(bf16)


def expand(h2, weights, bias):
    rows, width = h2.shape
    shards, _, cols = weights.shape
    size = block_rows(rows)
    out = ((1, size, cols), lambda t, i: (t, i, 0), (shards, rows, cols), bf16)
    return call(
        expand_kernel,
        "expand",
        (shards, rows // size),
        [
            pl.BlockSpec((size, width), lambda t, i: (i, 0)),
            pl.BlockSpec((1, width, cols), lambda t, i: (t, 0, 0)),
            pl.BlockSpec((1, 1, cols), lambda t, i: (t, 0, 0)),
        ],
        [out, out],
        estimate=cost(3 * rows * width * cols * shards, h2, weights),
    )(h2, weights, bias)


def expand_back_kernel(g_ref, w_ref, slope_ref, out_ref, bias_ref):
    @pl.when(pl.program_id(1) == 0)
    def _():
        bias_ref[...] = jnp.zeros_like(bias_ref)

    cols = out_ref.shape[2]
    chunk = min(CHUNK, cols)
    for start in range(0, cols, chunk):
        part = slice(start, start + chunk)
        grad = (dot(g_ref[...], w_ref[0, :, part]) * slope_ref[0, :, part].astype(f32)).astype(bf16)
        out_ref[0, :, part] = grad
        bias_ref[0, :, part] += jnp.sum(grad.astype(f32), axis=0, keepdims=True)


def expand_back(grad, weights, slope):
    rows, width = grad.shape
    shards, _, cols = weights.shape
    size = block_rows(rows)
    step = lambda t, i: (t, i, 0)
    return call(
        expand_back_kernel,
        "expand_back",
        (shards, rows // size),
        [
            pl.BlockSpec((size, width), lambda t, i: (i, 0)),
            pl.BlockSpec((1, width, cols), lambda t, i: (t, 0, 0)),
            pl.BlockSpec((1, size, cols), step),
        ],
        [
            ((1, size, cols), step, (shards, rows, cols), bf16),
            ((1, 1, cols), lambda t, i: (t, 0, 0), (shards, 1, cols), f32),
        ],
        estimate=cost(2 * rows * width * cols * shards, slope, slope),
    )(grad, weights, slope)


def dot_rows(left, right):
    return lax.dot_general(left, right, (((0,), (0,)), ((), ())), preferred_element_type=f32)


def weight_grad_kernel(left_ref, right_ref, out_ref, *, chunk, fill):
    which = pl.program_id(1)
    start = pl.multiple_of(which * chunk, chunk)
    out_ref[0, :, pl.ds(start, chunk)] = dot_rows(left_ref[...], right_ref[0]).astype(bf16)
    if fill:

        @pl.when(which == 0)
        def _():
            spare = jnp.zeros((out_ref.shape[1], fill), bf16)
            out_ref[0, :, out_ref.shape[2] - fill :] = spare


def weight_grad(left, right, spare):
    rows, width = left.shape
    shards, _, used = right.shape
    chunk = min(512, used)
    block = (1, width, used + spare)
    return call(
        functools.partial(weight_grad_kernel, chunk=chunk, fill=spare),
        "weight_grad",
        (shards, used // chunk),
        [
            fixed((rows, width), 0, 0),
            pl.BlockSpec((1, rows, chunk), lambda t, n: (t, 0, n)),
        ],
        [(block, lambda t, n: (t, 0, 0), (shards,) + block[1:], bf16)],
        estimate=cost(2 * rows * width * used * shards, left, right),
    )(left, right)[0]


def weight_grad_into_kernel(left_ref, right_ref, _, out_ref):
    out_ref[0] = dot_rows(left_ref[...], right_ref[0]).astype(bf16)


def weight_grad_into(left, right, out):
    rows, width = left.shape
    shards, _, cols = right.shape
    place = out.shape[2] // cols - 1
    return call(
        weight_grad_into_kernel,
        "weight_grad_into",
        (shards,),
        [
            fixed((rows, width), 0, 0),
            pl.BlockSpec((1, rows, cols), lambda t: (t, 0, 0)),
            pl.BlockSpec(memory_space=pl.ANY),
        ],
        [((1, width, cols), lambda t: (t, 0, place), out.shape, bf16)],
        aliases={2: 0},
        estimate=cost(2 * rows * width * cols * shards, left, right),
    )(left, right, out)[0]


def weight_grad_slots_kernel(slot_ref, left_ref, right_ref, out_ref, *, owners):
    grad = dot_rows(left_ref[...], right_ref[0]).astype(bf16)
    part = out_ref.shape[1]
    for owner in range(owners):
        slot = slot_ref[pl.program_id(1) * owners + owner]
        out_ref[slot] = grad[owner * part : (owner + 1) * part]


def weight_grad_slots(left, right, which, shares, slots):
    rows, width = left.shape
    shards, _, cols = right.shape
    share = cols // shares
    count = slots.shape[0]
    owners = count // shards
    part = width // owners
    chunk = share if share <= 1024 else 512
    first = which * share // chunk
    return call(
        functools.partial(weight_grad_slots_kernel, owners=owners),
        "weight_grad_slots",
        (share // chunk, shards),
        [
            fixed((rows, width), 0, 0),
            pl.BlockSpec((1, rows, chunk), lambda n, t, s: (t, 0, first + n)),
        ],
        [((count, part, chunk), lambda n, t, s: (0, 0, n), (count, part, share), bf16)],
        prefetch=1,
        estimate=cost(2 * rows * width * share * shards, left, right),
    )(slots, left, right)[0]


def weight_grad_halves_kernel(slot_ref, left_ref, right_ref, first_ref, second_ref, *, owners, steps):
    grad = dot_rows(left_ref[...], right_ref[0]).astype(bf16)

    @pl.when(pl.program_id(0) < steps)
    def _():
        first_ref[0] = grad

    @pl.when(pl.program_id(0) >= steps)
    def _():
        part = second_ref.shape[1]
        for owner in range(owners):
            slot = slot_ref[pl.program_id(1) * owners + owner]
            second_ref[slot] = grad[owner * part : (owner + 1) * part]


def weight_grad_halves(left, right, spare, slots):
    rows, width = left.shape
    shards, _, cols = right.shape
    half = cols // 2
    count = slots.shape[0]
    owners = count // shards
    part = width // owners
    chunk = min(512, half)
    steps = half // chunk
    early = lambda n, value, last: jnp.where(n < steps, value, last)
    return call(
        functools.partial(weight_grad_halves_kernel, owners=owners, steps=steps),
        "weight_grad_halves",
        (2 * steps, shards),
        [
            fixed((rows, width), 0, 0),
            pl.BlockSpec((1, rows, chunk), lambda n, t, s: (t, 0, n)),
        ],
        [
            (
                (1, width, chunk),
                lambda n, t, s: (early(n, t, shards - 1), 0, early(n, n, steps - 1)),
                (shards, width, half + spare),
                bf16,
            ),
            (
                (count, part, chunk),
                lambda n, t, s: (0, 0, jnp.maximum(n - steps, 0)),
                (count, part, half),
                bf16,
            ),
        ],
        prefetch=1,
        estimate=cost(2 * rows * width * cols * shards, left, right),
    )(slots, left, right)


def middle_back_kernel(
    g_ref, up_ref, mixed_ref, gm_ref, vec_ref, out_w_ref, gmixed_ref, go_ref, gattn_ref, sums_ref
):
    @pl.when(pl.program_id(0) == 0)
    def _():
        sums_ref[...] = jnp.zeros_like(sums_ref)

    grad_h = dot_flip(g_ref[0], up_ref[0])
    for shard in range(1, g_ref.shape[0]):
        grad_h += dot_flip(g_ref[shard], up_ref[shard])
    normed, inverse = norm_parts(mixed_ref[...])
    grad = gm_ref[...].astype(f32)
    grad_mixed = grad + norm_back(grad_h * row(vec_ref, GAIN2), normed, inverse)
    gmixed_ref[...] = grad_mixed
    rounded = grad_mixed.astype(bf16)
    go_ref[...] = rounded
    for index, value in ((1, grad_h * normed), (3, grad_h), (4, grad_mixed), (5, grad)):
        sums_ref[index : index + 1, :] += jnp.sum(value, axis=0, keepdims=True)
    for shard in range(gattn_ref.shape[0]):
        gattn_ref[shard] = dot(rounded, out_w_ref[shard]).astype(bf16)


def middle_back(grad_pre, up, mixed, grad_m, vectors, weights):
    shards, rows, cols = grad_pre.shape
    width = mixed.shape[1]
    heads = weights.shape[2]
    step = lambda i: (i, 0)
    wide = pl.BlockSpec((SEQ, width), step)
    return call(
        middle_back_kernel,
        "middle_back",
        (rows // SEQ,),
        [
            pl.BlockSpec((shards, SEQ, cols), lambda i: (0, i, 0)),
            fixed(up.shape, 0, 0, 0),
            wide,
            wide,
            fixed(vectors.shape, 0, 0),
            fixed(weights.shape, 0, 0, 0),
        ],
        [
            ((SEQ, width), step, (rows, width), f32),
            ((SEQ, width), step, (rows, width), bf16),
            ((shards, SEQ, heads), lambda i: (0, i, 0), (shards, rows, heads), bf16),
            ((8, width), lambda i: (0, 0), (8, width), f32),
        ],
        estimate=cost(2 * rows * width * (cols + heads) * shards, grad_pre, up, mixed),
    )(grad_pre, up, mixed, grad_m, vectors, weights)


def input_back_kernel(g_ref, w_ref, x_ref, gmixed_ref, vec_ref, before_ref, out_ref, sums_ref):
    @pl.when(pl.program_id(0) == 0)
    def _():
        sums_ref[...] = before_ref[...]

    grad_h = dot_flip(g_ref[0], w_ref[0])
    for shard in range(1, g_ref.shape[0]):
        grad_h += dot_flip(g_ref[shard], w_ref[shard])
    normed, inverse = norm_parts(x_ref[...].astype(f32))
    out_ref[...] = gmixed_ref[...] + norm_back(grad_h * row(vec_ref, GAIN1), normed, inverse)
    for index, value in ((0, grad_h * normed), (2, grad_h)):
        sums_ref[index : index + 1, :] += jnp.sum(value, axis=0, keepdims=True)


def input_back(grad_heads, weights, tokens, grad_mixed, vectors, sums):
    shards, rows, cols = grad_heads.shape
    width = tokens.shape[1]
    step = lambda i: (i, 0)
    wide = pl.BlockSpec((SEQ, width), step)
    return call(
        input_back_kernel,
        "input_back",
        (rows // SEQ,),
        [
            pl.BlockSpec((shards, SEQ, cols), lambda i: (0, i, 0)),
            fixed(weights.shape, 0, 0, 0),
            wide,
            wide,
            fixed(vectors.shape, 0, 0),
            fixed(sums.shape, 0, 0),
        ],
        [
            ((SEQ, width), step, (rows, width), f32),
            (sums.shape, lambda i: (0, 0), sums.shape, f32),
        ],
        estimate=cost(2 * rows * width * cols * shards, weights, tokens, grad_mixed),
    )(grad_heads, weights, tokens, grad_mixed, vectors, sums)


def shrink_kernel(kept_ref, act_ref, w_ref, mixed_ref, vec_ref, *refs, first):
    out_ref = refs[-1]
    total = dot_flip(act_ref[0], w_ref[0])
    for shard in range(1, act_ref.shape[0]):
        total += dot_flip(act_ref[shard], w_ref[shard])
    valid = BUFFER + kept_ref[first + pl.program_id(0)]
    alive = lax.broadcasted_iota(jnp.int32, (SEQ, 1), 0) < valid
    result = mixed_ref[...] + total + row(vec_ref, SHIFT4)
    out_ref[...] = jnp.where(alive, result, 0.0).astype(bf16)


def shrink(first, count, kept, act, weights, mixed, vectors, *out):
    shards, rows, cols = act.shape
    width = mixed.shape[1]
    step = lambda i, k: (first + i, 0)
    return call(
        functools.partial(shrink_kernel, first=first),
        "shrink",
        (count,),
        [
            pl.BlockSpec((shards, SEQ, cols), lambda i, k: (0, first + i, 0)),
            fixed(weights.shape, 0, 0, 0),
            pl.BlockSpec((SEQ, width), step),
            fixed(vectors.shape, 0, 0),
        ]
        + [pl.BlockSpec(memory_space=pl.ANY)] * len(out),
        [((SEQ, width), step, (rows, width), bf16)],
        prefetch=1,
        aliases={5: 0} if out else None,
        estimate=cost(2 * count * SEQ * width * cols * shards, weights),
    )(kept, act, weights, mixed, vectors, *out)[0]


def swap(values, axis, bit):
    places = range(lax.axis_size(axis))
    return lax.ppermute(values, axis, [(place, place ^ bit) for place in places])


def bits_of(axis):
    return [1 << power for power in range(lax.axis_size(axis).bit_length() - 1)]


def flip_gather(part, order):
    dp, shards = lax.axis_size("dp"), lax.axis_size("tensor")
    values = part[None]
    index = jnp.arange(shards * dp, dtype=jnp.int32)
    apart = {
        "tensor": (index // dp) ^ lax.axis_index("tensor").astype(jnp.int32),
        "dp": (index % dp) ^ lax.axis_index("dp").astype(jnp.int32),
    }
    place = jnp.zeros_like(index)
    for axis, bit in order:
        place += jnp.where((apart[axis] & bit) != 0, values.shape[0], 0)
        values = jnp.concatenate([values, swap(values, axis, bit)], 0)
    return jnp.take(values, place, axis=0)


def slot_table(order):
    dp, shards = lax.axis_size("dp"), lax.axis_size("tensor")
    index = jnp.arange(shards * dp, dtype=jnp.int32)
    apart = {
        "tensor": (index // dp) ^ lax.axis_index("tensor").astype(jnp.int32),
        "dp": (index % dp) ^ lax.axis_index("dp").astype(jnp.int32),
    }
    slot = jnp.zeros_like(index)
    for depth, (axis, bit) in enumerate(order):
        slot += jnp.where((apart[axis] & bit) != 0, 1 << (len(order) - 1 - depth), 0)
    return slot


class Chain:
    def __init__(self, values, order):
        self.values, self.order = values, list(order)
        self.send()

    def send(self):
        half = self.values.shape[0] // 2
        self.near = self.values[:half]
        self.far = swap(self.values[half:], *self.order.pop(0))

    def settle(self):
        self.values = self.near + self.far

    def finish(self):
        self.settle()
        while self.order:
            self.send()
            self.settle()
        return self.values


class Sum(Chain):
    def __init__(self, values, order):
        super().__init__(values, [order[at : at + 2] for at in range(0, len(order), 2)])

    def send(self):
        shards = lax.axis_size("tensor")
        places = range(lax.axis_size("dp") * shards)
        masks = [0]
        for axis, bit in self.order.pop(0):
            masks += [mask ^ (bit * shards if axis == "dp" else bit) for mask in masks]
        self.far = [
            lax.ppermute(self.values, ("dp", "tensor"), [(place, place ^ mask) for place in places])
            for mask in masks[1:]
        ]

    def settle(self):
        self.values = sum(self.far, self.values)


def meet(values, *chains):
    values, far = lax.optimization_barrier((values, [chain.far for chain in chains]))
    for chain, arrived in zip(chains, far):
        chain.far = arrived
        chain.settle()
        if chain.order:
            chain.send()
    return values


def gather(part):
    full = lax.all_gather(part, ("tensor", "dp"), axis=0, tiled=True)
    return full.reshape(lax.axis_size("tensor"), -1, part.shape[1])


def scatter(full):
    flat = full.reshape(-1, full.shape[2])
    return lax.psum_scatter(flat, ("tensor", "dp"), scatter_dimension=0, tiled=True)


def body(tokens, kept, cotangent, w_qkv, w_out, w_up, w_down, qv_bias, up_bias, ln_gain, shift):
    rows, width = tokens.shape
    dp, shards = lax.axis_size("dp"), lax.axis_size("tensor")
    images = rows // SEQ
    part = w_qkv.shape[1]
    cols = w_qkv.shape[2]
    own = ln_gain.shape[1]
    barrier = lax.optimization_barrier

    core, along_x = [("dp", 1)], [("tensor", bit) for bit in bits_of("tensor")[::-1]]
    low, high = [("dp", 2)], [("dp", bit) for bit in bits_of("dp")[::-1] if bit > 2]
    order_x, order_low = core + along_x + low + high, core + low + high + along_x

    full_qkv = gather(w_qkv.transpose(1, 0, 2).reshape(part, 3 * cols))
    full_up = gather(w_up)
    full_down = gather(w_down.T)

    small = jnp.concatenate(
        [ln_gain, shift, qv_bias.astype(f32), up_bias.astype(f32).reshape(-1, own)], 0
    )
    small = flip_gather(small, high + low + along_x + core)
    small = small.reshape((shards, dp) + small.shape[1:])
    vectors = small[:, :, :6].transpose(2, 1, 0, 3).reshape(6, width)
    vectors = jnp.concatenate([vectors, jnp.zeros((2, width), f32)], 0)
    bias_qv = small[:, :, 6:8].transpose(0, 2, 1, 3).reshape(shards, 2, cols)
    bias_up = small[:, :, 8:].reshape(shards, 1, -1)
    bias_heads = jnp.concatenate([bias_qv[:, :1], jnp.zeros_like(bias_qv[:, :1]), bias_qv[:, 1:]], 2)
    full_out = flip_gather(w_out.T, high + low + along_x + core).reshape(shards, width, cols)

    first_image = lax.axis_index("tensor") * images
    kept_own = lax.dynamic_slice_in_dim(kept, first_image, images, 0)
    positions = jnp.arange(SEQ, dtype=jnp.int32)
    alive = (positions[None, :] < BUFFER + kept_own[:, None]).reshape(rows, 1)
    grad_m = jnp.where(alive, cotangent, jnp.zeros_like(cotangent))

    tables = [slot_table(order_x), slot_table(order_low)]

    h1 = norm_in(tokens, vectors)
    qkv = project(h1, full_qkv, bias_heads)
    attn, expo, inverse_sum = attend(qkv, kept_own)
    mixed, h2 = mix(attn, full_out, tokens, vectors)
    act, slope = expand(h2, full_up, bias_up)

    hidden = act.shape[2]
    grad_down = weight_grad(grad_m, act, hidden // 8)
    grad_m, grad_down = barrier((grad_m, grad_down))
    sent_down = scatter(grad_down)[:, :hidden]
    grad_pre, grad_bias_up = expand_back(grad_m, full_down, slope)

    share = hidden // 2
    grad_first, grad_second = weight_grad_halves(h2, grad_pre, cols, tables[0])
    grad_pre, grad_first, grad_second = barrier((grad_pre, grad_first, grad_second))
    chain_up = Chain(grad_second, order_x)
    grad_mixed, grad_o, grad_attn, sums2 = middle_back(
        grad_pre, full_up, mixed, grad_m, vectors, full_out
    )
    grad_o = meet(grad_o, chain_up)
    grad_first = weight_grad_into(grad_o, attn, grad_first)
    grad_attn, grad_first = barrier((grad_attn, grad_first))
    sent_first = scatter(grad_first)
    grad_heads, grad_bias_qv = attend_back(qkv, grad_attn, attn, expo, inverse_sum)
    grad_heads = meet(grad_heads, chain_up)
    grad_heads, sent_down = barrier((grad_heads, sent_down))

    chains_qkv = []
    shares = 2 if (3 * cols // 2) % LANES == 0 else 1
    for which, order in enumerate((order_x, order_low)[:shares]):
        grad_qkv = weight_grad_slots(h1, grad_heads, which, shares, tables[which])
        grad_heads, grad_qkv = barrier((grad_heads, grad_qkv))
        if which == shares - 1:
            grad_qkv = meet(grad_qkv, chain_up, *chains_qkv)
        chains_qkv.append(Chain(grad_qkv, order))
    sums = jnp.concatenate(
        [
            sums2[:6],
            grad_bias_qv.transpose(1, 0, 2).reshape(2, width),
            grad_bias_up.reshape(-1, width),
        ],
        0,
    )
    grad_heads = meet(grad_heads, *chains_qkv[1:])
    grad_tokens, sums = input_back(grad_heads, full_qkv, tokens, grad_mixed, vectors, sums)
    sums, act = meet((sums, act), chain_up, *chains_qkv)
    chain_small = Sum(sums, order_x)
    first = images // 2
    layer_out = shrink(0, first, kept_own, act, full_down, mixed, vectors)
    layer_out = meet(layer_out, chain_up, chain_small, *chains_qkv)
    layer_out = shrink(first, images - first, kept_own, act, full_down, mixed, vectors, layer_out)
    layer_out = meet(layer_out, chain_small, *chains_qkv)
    sent_up = jnp.concatenate([sent_first[:, :share], chain_up.finish()[0]], 1)
    sent_qkv = jnp.concatenate([chain.finish()[0] for chain in chains_qkv], 1)
    small = chain_small.finish()
    at_dp, at_tensor = lax.axis_index("dp"), lax.axis_index("tensor")
    row_place, shard_place = at_dp * shards + at_tensor, at_tensor * dp + at_dp
    rows_own = lax.dynamic_slice(small, (0, row_place * own), (6, own))
    heads_own = lax.dynamic_slice(small, (6, shard_place * own), (2, own))
    count = up_bias.shape[0]
    start = shard_place * count
    up_own = lax.dynamic_slice(small, (8 + start // width, start % width), (1, count))

    return (
        layer_out,
        grad_tokens,
        sent_qkv.astype(f32).reshape(part, 3, cols).transpose(1, 0, 2),
        sent_first[:, share:].astype(f32).T,
        sent_up.astype(f32),
        sent_down.astype(f32).T,
        heads_own,
        up_own.reshape(-1),
        rows_own[:2],
        rows_own[2:],
    )


def solution(mesh):
    both = P(("dp", "tensor"), None)
    matrices = (
        P(None, "dp", "tensor"),
        P("tensor", "dp"),
        P("dp", "tensor"),
        P("tensor", "dp"),
        P(None, ("tensor", "dp")),
        P(("tensor", "dp")),
        P(None, ("dp", "tensor")),
        P(None, ("dp", "tensor")),
    )
    return jax.shard_map(
        body,
        mesh=mesh,
        in_specs=(both, P("dp"), both) + matrices,
        out_specs=(both, both) + matrices,
        check_vma=False,
    )
```
